256 devices in a mesh: ep: 32 (over y_lo, z, core), tp: 8 (over x, y_hi).
Axes of the slice: x: 4, y: 4 (y_hi: 2, y_lo: 2; y = y_hi * 2 + y_lo), z: 8, core: 2. Of those that a mesh axis runs over, the one named last changes fastest.
Arguments:
- tokens_in: bfloat16 [32768, 1536], P('ep'), may hold values from -12 to 12
- lengths: int32 [32], P('ep'), may hold values from 1 to 1024, 16384 in all
- attn_gain: float32 [1536], replicated, may hold values from 0.1 to 1.9
- q_proj: float32 [1536, 1536], P('ep', 'tp'), may hold values from -2 to 2
- k_proj: float32 [1536, 512], P('ep', 'tp'), may hold values from -2 to 2
- value_projection: float32 [1536, 512], P('ep', 'tp'), may hold values from -0.15625 to 0.15625
- o_proj: float32 [1536, 1536], P('tp', 'ep'), may hold values from -2.5 to 2.5
- key_value_pages: bfloat16 [256, 16, 1024], P('ep', None, 'tp'), may hold values from -6 to 6
- page_table: int32 [32, 32, 2], P(None, 'ep'), may hold values from 0 to 7
- moe_gain: float32 [1536], replicated, may hold values from 0.1 to 1.9
- router: bfloat16 [1536, 32], replicated, may hold values from -5 to 5
- expert_ids: int32 [32768, 8], P(('ep', 'tp')), may hold values from 0 to 31, all different within a row; in each aligned block of 128 rows (0 to 127, 128 to 255, ...) at most 48 rows name the same one
- gate_up_proj: float32 [32, 1536, 1024], P('ep', 'tp'), may hold values from -0.15625 to 0.15625
- down_proj: float32 [32, 512, 1536], P('ep', 'tp'), may hold values from -0.25 to 0.25
Outputs:
- layer_out: bfloat16 [32768, 1536], P(('ep', 'tp'))
The draws below stay inside these ranges and needn't reach their ends.
Inputs may be any that keep to these rules, and one draw needn't show every extreme that they name: `expert_ids`: among the 128 token slots of each aligned block (one device's slots), no expert is named more than 48 times, a bound that some block reaches. `lengths`: some prompt is 1024 tokens long.
All inputs are finite; a program needn't handle non-finite values. No bound on the sum of `lengths` on one device may be relied on, other than what follows from the above.
Results may differ from the reference program's by a relative error of at most 0.018.
Values may be sent and summed in bfloat16 or wider, within the bound.
No kernel may reach another device: no remote copies, remote signals or barrier semaphores. Data moves between devices by JAX's collectives and lax.ppermute only.
A program may use at most 128 MiB of HBM per device.

```python
import math
import jax
import jax.numpy as jnp
import numpy as np
from jax import lax

MODEL_DIM = 1536
QUERY_HEADS = 24
KEY_VALUE_HEADS = 8
HEAD_WIDTH = 64
FF = 512
TOPK = 8
PROMPT_SLOTS = 1024
PAGE_TOKENS = 16
SLOTS = 2
POOL_PAGES = 8
EXPERTS = 32
PROMPTS = 32
TOKENS = 32768
ROWS = 128
CAP = 48
N_EP = 32
N_TP = 8


def draw_tokens_in(key, part):
    draw_sample = jax.random.truncated_normal(jax.random.fold_in(key, 1), -6.0, 6.0, (TOKENS, MODEL_DIM), jnp.float32)
    return draw_sample.astype(jnp.bfloat16)


def draw_q_proj(key, part):
    draw_sample = jax.random.truncated_normal(jax.random.fold_in(key, 11), -6.0, 6.0, (MODEL_DIM, QUERY_HEADS * HEAD_WIDTH), jnp.float32) * MODEL_DIM ** (-0.5)
    return draw_sample


def draw_k_proj(key, part):
    draw_sample = jax.random.truncated_normal(jax.random.fold_in(key, 21), -6.0, 6.0, (MODEL_DIM, KEY_VALUE_HEADS * HEAD_WIDTH), jnp.float32) * MODEL_DIM ** (-0.5)
    return draw_sample


def draw_router(key, part):
    draw_sample = jax.random.truncated_normal(jax.random.fold_in(key, 31), -6.0, 6.0, (MODEL_DIM, EXPERTS), jnp.float32) * MODEL_DIM ** (-0.5)
    return draw_sample.astype(jnp.bfloat16)


def place_ends(entries, rng, least, largest):
    spot = [jax.random.randint(jax.random.fold_in(rng, axis), (), 0, length) for axis, length in enumerate(entries.shape)]
    widest = entries.shape.index(max(entries.shape))
    neighbour = spot[:widest] + [(spot[widest] + 1) % entries.shape[widest]] + spot[widest + 1:]
    return entries.at[tuple(spot)].set(least).at[tuple(neighbour)].set(largest)


def steps_of(rng, dims, shards, low, top_value):
    loudness, own = 1.0, jax.random.fold_in(rng, 6)
    for axis_at, blocks in shards:
        heights = jnp.exp(jax.random.uniform(jax.random.fold_in(own, axis_at), (blocks,), jnp.float32, low / len(shards), top_value / len(shards)))
        loudness = loudness * jnp.repeat(heights, dims[axis_at] // blocks).reshape([-1 if axis == axis_at else 1 for axis in range(len(dims))])
    return loudness


def length_profile(count, total, most, lean):
    portions = [(1 << 20) // math.isqrt(standing ** lean) + 1 for standing in range(2, count + 1)]
    rest, given = total - most - (count - 1), [1] * (count - 1)
    while rest > 0:
        movable = [i for i in range(count - 1) if given[i] < most]
        mass, budget = sum([portions[i] for i in movable]), rest
        for i in movable:
            addition = min(most - given[i], max(1, budget * portions[i] // mass), rest)
            given[i] = given[i] + addition
            rest = rest - addition
    return np.array([most] + given)


def ragged(own_key, count, total, bound, slope):
    if count == 2:
        one = jax.random.randint(own_key, (), max(1, total - bound), min(bound, total - 1) + 1)
        return jnp.stack([one, total - one])
    sizes = jnp.asarray(length_profile(count, total, bound, slope), jnp.int32)
    couples = (count - 1) // 2
    source_of, receiver = sizes[1:1 + 2 * couples:2], sizes[2:2 + 2 * couples:2]
    slack = jnp.minimum(source_of - 1, bound - receiver)
    passed = jax.random.randint(jax.random.fold_in(own_key, 1), (couples,), 0, 1 << 20) % (slack + 1)
    sizes = sizes.at[1:1 + 2 * couples:2].set(source_of - passed).at[2:2 + 2 * couples:2].set(receiver + passed)
    return sizes[jax.random.permutation(jax.random.fold_in(own_key, 2), count)]


def shared_out(key, own, number, rows, amount, top, bound, lean):
    sequence = jax.random.permutation(key, amount)
    crowded, usual = shares(amount, rows * top, bound, lean, True), shares(amount, rows * top, bound, lean, False)
    places = jnp.arange(amount)

    def named(tallies, rotation):
        used = int((tallies > 0).sum())
        fixed = max(1, used // 4)
        passed = fixed + (places - fixed + rotation * (used - fixed)) % max(1, amount - fixed)
        return jnp.zeros((amount,), jnp.int32).at[sequence[jnp.where(places < fixed, places, passed)]].set(jnp.asarray(tallies, jnp.int32))

    tallies = jnp.where(number % 4 == 0, named(crowded, number // 4), named(usual, number - number // 4 - 1))
    mixed = jax.random.permutation(jax.random.fold_in(own, 3), amount)
    source_of, taker = mixed[0:amount // 2 * 2:2], mixed[1:amount // 2 * 2:2]
    slack = jnp.minimum(tallies[source_of] - 1, bound - tallies[taker]) // 2
    slack = jnp.where((source_of == sequence[0]) | (taker == sequence[0]) | (tallies[taker] == 0), 0, jnp.maximum(slack, 0))
    passed = jax.random.randint(jax.random.fold_in(own, 4), (amount // 2,), 0, 1 << 20) % (slack + 1)
    tallies = tallies.at[source_of].add(-passed).at[taker].add(passed)
    members = jnp.searchsorted(jnp.cumsum(tallies), jnp.arange(rows * top), side="right").astype(jnp.int32)
    grid = members.reshape(top, rows).T
    grid = grid[jax.random.permutation(jax.random.fold_in(own, 1), rows)]
    rotation = jax.random.randint(jax.random.fold_in(own, 2), (rows, 1), 0, top)
    return jnp.take_along_axis(grid, (jnp.arange(top)[None, :] + rotation) % top, axis=1)


def shares(amount, total, reach, skew, full):
    portions = [(1 << 20) // math.isqrt(grade ** skew) + 1 for grade in range(1, amount + 1)]
    largest = reach if full else min(reach, max(-(-total // amount), total * portions[0] // sum(portions)))
    least = 1 if total - largest >= amount - 1 else 0
    holding, rest = [largest] + [least] * (amount - 1), total - largest - least * (amount - 1)
    while rest > 0:
        candidates = [i for i in range(1, amount) if holding[i] < largest] or [i for i in range(1, amount) if holding[i] < reach]
        mass, budget = sum([portions[i] for i in candidates]), rest
        for i in candidates:
            more = min(reach - holding[i], max(1, budget * portions[i] // mass), rest)
            holding[i] = holding[i] + more
            rest = rest - more
    return np.array(holding)


def noise(key, shape, deviation, most, pieces=(), kind=jnp.bfloat16):
    loudness = steps_of(key, shape, pieces, -0.22, 0.18) if pieces else 1.0
    values = jax.random.normal(key, shape, jnp.float32) * deviation * loudness
    return jnp.minimum(jnp.maximum(values, -most), most).astype(kind)


def setup_inputs(seed: int = 0) -> dict:
    key_list = jax.random.split(jax.random.key(seed), 15)
    tokens_in = draw_tokens_in(jax.random.fold_in(key_list[14], 71), 0)
    lengths = ragged(key_list[1], PROMPTS, PROMPTS * PROMPT_SLOTS // 2, PROMPT_SLOTS, 2).astype(jnp.int32)
    attn_gain = jnp.clip(1.0 + 0.18 * jax.random.normal(key_list[2], (MODEL_DIM,), jnp.float32), 0.1, 1.9)
    q_proj = draw_q_proj(jax.random.fold_in(key_list[14], 71), 0)
    k_proj = draw_k_proj(jax.random.fold_in(key_list[14], 71), 0)
    value_projection = noise(key_list[5], (MODEL_DIM, KEY_VALUE_HEADS * HEAD_WIDTH), MODEL_DIM ** -0.5, 0.15625, ((0, 32), (1, 8)), jnp.float32)
    o_proj = noise(key_list[6], (QUERY_HEADS * HEAD_WIDTH, MODEL_DIM), 0.25, 2.5, ((0, 8), (1, 32)), jnp.float32)
    key_value_pages = noise(key_list[7], (N_EP * POOL_PAGES, PAGE_TOKENS, KEY_VALUE_HEADS * 2 * HEAD_WIDTH), 1.0, 6.0, ((0, 32), (2, 8)))
    page_table = place_ends(jax.random.randint(key_list[8], (PROMPTS, N_EP, SLOTS), 0, POOL_PAGES), jax.random.fold_in(key_list[8], 1), 0, POOL_PAGES - 1).astype(jnp.int32)
    moe_gain = jnp.clip(1.0 + 0.18 * jax.random.normal(key_list[9], (MODEL_DIM,), jnp.float32), 0.1, 1.9)
    router = draw_router(jax.random.fold_in(key_list[14], 71), 0)
    expert_ids_keys = jax.random.split(jax.random.fold_in(key_list[11], 1), TOKENS // ROWS)
    expert_ids_turns = jax.random.permutation(jax.random.fold_in(key_list[11], 3), TOKENS // ROWS)
    expert_ids = jax.vmap(lambda own, number: shared_out(jax.random.fold_in(key_list[11], 2), own, number, ROWS, EXPERTS, TOPK, CAP, 2))(expert_ids_keys, expert_ids_turns).reshape((TOKENS, TOPK))
    gate_up_proj = noise(key_list[12], (EXPERTS, MODEL_DIM, 2 * FF), MODEL_DIM ** -0.5, 0.15625, ((0, 32), (1, 8)), jnp.float32)
    down_proj = noise(key_list[13], (EXPERTS, FF, MODEL_DIM), FF ** -0.5, 0.25, ((0, 32), (1, 8)), jnp.float32)
    return {"tokens_in": tokens_in, "lengths": lengths, "attn_gain": attn_gain, "q_proj": q_proj, "k_proj": k_proj, "value_projection": value_projection, "o_proj": o_proj, "key_value_pages": key_value_pages, "page_table": page_table, "moe_gain": moe_gain, "router": router, "expert_ids": expert_ids, "gate_up_proj": gate_up_proj, "down_proj": down_proj}


epsilon = 1e-05

def rms_scale(values, norm_gain):
    mean_square = lax.optimization_barrier(jnp.mean(values * values, axis=-1, keepdims=True))
    return values * lax.rsqrt(mean_square + epsilon) * norm_gain

def apply_rotary(vectors, token_positions):
    half_width = vectors.shape[-1] // 2
    frequency = jnp.exp(jnp.arange(half_width, dtype=jnp.float32) * (-2.0 * math.log(10000.0) / vectors.shape[-1]))
    angles = token_positions.astype(jnp.float32)[:, None] * frequency[None, :]
    cosine = jnp.cos(angles)[:, None, :]
    sine_table = jnp.sin(angles)[:, None, :]
    first_half = vectors[..., :half_width]
    second_half = vectors[..., half_width:]
    return jnp.concatenate([first_half * cosine - second_half * sine_table, second_half * cosine + first_half * sine_table], axis=-1)

def reference(tokens_in, lengths, attn_gain, q_proj, k_proj, value_projection, o_proj, key_value_pages, page_table, moe_gain, router, expert_ids, gate_up_proj, down_proj):
    query_weight = q_proj.astype(jnp.bfloat16)
    key_matrix = k_proj.astype(jnp.bfloat16)
    value_matrix = value_projection.astype(jnp.bfloat16)
    output_weight = o_proj.astype(jnp.bfloat16)
    prefix_length = N_EP * SLOTS * PAGE_TOKENS
    heads_per_group = QUERY_HEADS // KEY_VALUE_HEADS
    group_width = QUERY_HEADS * HEAD_WIDTH // N_TP
    pooled_page_count = key_value_pages.reshape(N_EP, POOL_PAGES, PAGE_TOKENS, KEY_VALUE_HEADS, 2, HEAD_WIDTH)
    token_positions = prefix_length + jnp.arange(PROMPT_SLOTS)
    key_pos = jnp.arange(prefix_length + PROMPT_SLOTS)
    query_pos = jnp.arange(PROMPT_SLOTS)
    source_pages = jnp.arange(N_EP)
    grouped_out = output_weight.reshape(N_TP, group_width, MODEL_DIM).astype(jnp.float32)

    def one_prompt(inputs):
        rows, length_here, lookup_table = inputs
        normalized_input = rms_scale(rows.astype(jnp.float32), attn_gain).astype(jnp.bfloat16)
        query_rows = apply_rotary(jnp.dot(normalized_input, query_weight, preferred_element_type=jnp.float32).reshape(PROMPT_SLOTS, QUERY_HEADS, HEAD_WIDTH), token_positions).astype(jnp.bfloat16)
        fresh_keys = apply_rotary(jnp.dot(normalized_input, key_matrix, preferred_element_type=jnp.float32).reshape(PROMPT_SLOTS, KEY_VALUE_HEADS, HEAD_WIDTH), token_positions).astype(jnp.bfloat16)
        fresh_values = jnp.dot(normalized_input, value_matrix, preferred_element_type=jnp.float32).reshape(PROMPT_SLOTS, KEY_VALUE_HEADS, HEAD_WIDTH).astype(jnp.bfloat16)
        page_list = pooled_page_count[source_pages[:, None], lookup_table].reshape(prefix_length, KEY_VALUE_HEADS, 2, HEAD_WIDTH)
        all_keys = jnp.concatenate([page_list[:, :, 0], fresh_keys], 0).astype(jnp.float32).transpose(1, 0, 2)
        all_values = jnp.concatenate([page_list[:, :, 1], fresh_values], 0).astype(jnp.float32).transpose(1, 0, 2)
        own = key_pos[None, :] - prefix_length
        allowed = (own < 0) | (own <= query_pos[:, None]) & (own < length_here)
        grouped_queries = query_rows.reshape(PROMPT_SLOTS, KEY_VALUE_HEADS, heads_per_group, HEAD_WIDTH).astype(jnp.float32).transpose(1, 2, 0, 3)

        def one_head(head_inputs):
            query_group, keys_here, values_here = head_inputs
            scores = jnp.einsum('gqd,kd->gqk', query_group, keys_here) * HEAD_WIDTH ** (-0.5)
            scores = jnp.where(allowed[None], scores, -1e+30)
            top_score = lax.optimization_barrier(jnp.max(scores, axis=-1, keepdims=True))
            weights = jnp.exp(scores - top_score)
            probs = (weights / lax.optimization_barrier(jnp.sum(weights, axis=-1, keepdims=True))).astype(jnp.bfloat16)
            return jnp.einsum('gqk,kd->gqd', probs.astype(jnp.float32), values_here).astype(jnp.bfloat16)
        heads_out = lax.map(one_head, (grouped_queries, all_keys, all_values))
        attended = heads_out.transpose(2, 0, 1, 3).reshape(PROMPT_SLOTS, QUERY_HEADS * HEAD_WIDTH)
        parts = jnp.einsum('lgw,gwd->gld', attended.reshape(PROMPT_SLOTS, N_TP, group_width).astype(jnp.float32), grouped_out)
        parts = lax.optimization_barrier(parts.astype(jnp.bfloat16)).astype(jnp.float32)
        return rows.astype(jnp.float32) + lax.optimization_barrier(jnp.sum(parts, axis=0))
    hidden = lax.map(one_prompt, (tokens_in.reshape(PROMPTS, PROMPT_SLOTS, MODEL_DIM), lengths, page_table)).reshape(TOKENS, MODEL_DIM)
    moe_in = rms_scale(hidden, moe_gain).astype(jnp.bfloat16)
    logits = jnp.dot(moe_in, router, preferred_element_type=jnp.float32)
    picked = jnp.take_along_axis(logits, expert_ids, axis=1)
    top_logit = lax.optimization_barrier(jnp.max(picked, axis=-1, keepdims=True))
    raised = jnp.exp(picked - top_logit)
    gates = raised / lax.optimization_barrier(jnp.sum(raised, axis=-1, keepdims=True))
    flat_ids = expert_ids.reshape(-1)
    flat_gates = gates.reshape(-1)
    order = jnp.argsort(flat_ids, stable=True).astype(jnp.int32)
    counts = lax.optimization_barrier(jnp.sum((flat_ids[:, None] == jnp.arange(EXPERTS)[None, :]).astype(jnp.int32), axis=0))
    starts = (jnp.cumsum(counts) - counts).astype(jnp.int32)
    most_rows = TOKENS // ROWS * CAP
    padded_order = jnp.concatenate([order, jnp.zeros((most_rows,), jnp.int32)])
    gate_up_all = gate_up_proj.astype(jnp.bfloat16)
    down_all = down_proj.astype(jnp.bfloat16)

    def one_expert(mixed, expert_inputs):
        gate_up_weight, down_weight, start, count = expert_inputs
        picks = lax.dynamic_slice_in_dim(padded_order, start.astype(jnp.int32), most_rows)
        live = jnp.arange(most_rows) < count
        token_index = picks // TOPK
        rows = moe_in[token_index]
        gate_up = jnp.dot(rows, gate_up_weight, preferred_element_type=jnp.float32)
        activated = (jax.nn.silu(gate_up[:, :FF]) * gate_up[:, FF:]).astype(jnp.bfloat16)
        expert_out = jnp.dot(activated, down_weight, preferred_element_type=jnp.float32).astype(jnp.bfloat16)
        weight_rows = jnp.where(live, flat_gates[picks], 0.0)
        return (mixed.at[token_index].add(expert_out.astype(jnp.float32) * weight_rows[:, None]), None)
    mixed, unused = lax.scan(one_expert, jnp.zeros((TOKENS, MODEL_DIM), jnp.float32), (gate_up_all, down_all, starts, counts))
    slot_index = jnp.arange(TOKENS)
    valid = slot_index % PROMPT_SLOTS < lengths[slot_index // PROMPT_SLOTS]
    return jnp.where(valid[:, None], hidden + mixed, 0.0).astype(jnp.bfloat16)
```

```python
import math

import jax
import jax.numpy as jnp
from jax import lax
from jax.sharding import PartitionSpec as P

HEAD_WIDTH = 64
FF = 512


epsilon = 1e-05

Z_GROUPS = [[y * 16 + z * 2 + c for z in range(8)] for y in range(2) for c in range(2)]
CHIP_PAIR_GROUPS = [[y * 16 + z * 2 + c for y in range(2) for c in range(2)] for z in range(8)]
PLANE_GROUPS = [
    [(y * 16 + z * 2 + c) * 8 + t for y in range(2) for c in range(2) for t in range(8)]
    for z in range(8)
]


def rms_scale(values, norm_gain):
    mean_square = jnp.mean(values * values, axis=-1, keepdims=True)
    return values * lax.rsqrt(mean_square + epsilon) * norm_gain


def apply_rotary(vectors, token_positions):
    half_width = vectors.shape[-1] // 2
    frequency = jnp.exp(
        jnp.arange(half_width, dtype=jnp.float32) * (-2.0 * math.log(10000.0) / vectors.shape[-1])
    )
    angles = token_positions.astype(jnp.float32)[:, None] * frequency[None, :]
    cosine = jnp.cos(angles)[:, None, :]
    sine_table = jnp.sin(angles)[:, None, :]
    first_half = vectors[..., :half_width]
    second_half = vectors[..., half_width:]
    return jnp.concatenate(
        [
            first_half * cosine - second_half * sine_table,
            second_half * cosine + first_half * sine_table,
        ],
        axis=-1,
    )


def on_device(
    tokens_in,
    lengths,
    attn_gain,
    q_proj,
    k_proj,
    value_projection,
    o_proj,
    key_value_pages,
    page_table,
    moe_gain,
    router,
    expert_ids,
    gate_up_proj,
    down_proj,
):
    seq_len, model_width = tokens_in.shape
    ep_count = lax.axis_size("ep")
    tp_index = lax.axis_index("tp")
    kv_local = key_value_pages.shape[2] // (2 * HEAD_WIDTH)
    query_local = q_proj.shape[1] // HEAD_WIDTH
    packed_shard = jnp.concatenate(
        [q_proj, k_proj, value_projection, o_proj.T], axis=1
    ).astype(jnp.bfloat16)
    along_z = lax.all_to_all(
        jnp.broadcast_to(packed_shard[None], (8, *packed_shard.shape)),
        "ep", 0, 0, axis_index_groups=Z_GROUPS, tiled=True,
    )
    across = lax.all_to_all(
        jnp.broadcast_to(along_z[None], (4, *along_z.shape)),
        "ep", 0, 0, axis_index_groups=CHIP_PAIR_GROUPS, tiled=True,
    )
    packed = (
        across.reshape(2, 2, 8, *packed_shard.shape)
        .transpose(0, 2, 1, 3, 4)
        .reshape(model_width, packed_shard.shape[1])
    )
    query_weight = packed[:, :192]
    key_matrix = packed[:, 192:256]
    value_matrix = packed[:, 256:320]
    output_weight = packed[:, 320:].T
    gate_up_planes = lax.all_gather(
        gate_up_proj[0].astype(jnp.bfloat16), "ep", axis_index_groups=Z_GROUPS
    )
    down_planes = lax.all_gather(
        down_proj[0].astype(jnp.bfloat16), "ep", axis_index_groups=Z_GROUPS
    )
    gate_up_full = lax.all_to_all(gate_up_planes, "tp", 0, 0, tiled=True).reshape(model_width, -1)
    down_full = lax.all_to_all(down_planes, "tp", 0, 0, tiled=True).reshape(-1, model_width)
    chosen_pages = key_value_pages[page_table[:, 0, :]]
    arrived = lax.all_to_all(chosen_pages, "ep", split_axis=0, concat_axis=0, tiled=True)
    prefix_length = arrived.shape[0] * arrived.shape[1] * arrived.shape[2]
    prefix = arrived.reshape(prefix_length, kv_local, 2, HEAD_WIDTH)
    normalized_input = rms_scale(tokens_in.astype(jnp.float32), attn_gain).astype(jnp.bfloat16)
    token_positions = prefix_length + jnp.arange(seq_len)
    query_rows = apply_rotary(
        jnp.dot(normalized_input, query_weight, preferred_element_type=jnp.float32).reshape(
            seq_len, query_local, HEAD_WIDTH
        ),
        token_positions,
    ).astype(jnp.bfloat16)
    fresh_keys = apply_rotary(
        jnp.dot(normalized_input, key_matrix, preferred_element_type=jnp.float32).reshape(
            seq_len, kv_local, HEAD_WIDTH
        ),
        token_positions,
    ).astype(jnp.bfloat16)
    fresh_values = (
        jnp.dot(normalized_input, value_matrix, preferred_element_type=jnp.float32)
        .reshape(seq_len, kv_local, HEAD_WIDTH)
        .astype(jnp.bfloat16)
    )
    length_here = lengths[0]
    own = jnp.arange(prefix_length + seq_len)[None, :] - prefix_length
    block_rows = min(512, seq_len)
    all_keys = jnp.concatenate([prefix[:, 0, 0], fresh_keys[:, 0]], 0)
    all_values = jnp.concatenate([prefix[:, 0, 1], fresh_values[:, 0]], 0)
    grouped_queries = query_rows.transpose(1, 0, 2)
    blocks = []
    for block_start in range(0, seq_len, block_rows):
        query_block = grouped_queries[:, block_start : block_start + block_rows]
        scores = jnp.einsum(
            "gqd,kd->gqk", query_block, all_keys, preferred_element_type=jnp.float32
        ) * HEAD_WIDTH ** (-0.5)
        query_pos = block_start + jnp.arange(block_rows)
        allowed = (own < 0) | (own <= query_pos[:, None]) & (own < length_here)
        scores = jnp.where(allowed[None], scores, -1e30)
        top_score = jnp.max(scores, axis=-1, keepdims=True)
        weights = jnp.exp(scores - top_score)
        probs = (weights / jnp.sum(weights, axis=-1, keepdims=True)).astype(jnp.bfloat16)
        blocks.append(
            jnp.einsum("gqk,kd->gqd", probs, all_values, preferred_element_type=jnp.float32).astype(
                jnp.bfloat16
            )
        )
    head_outputs = jnp.concatenate(blocks, axis=1)
    attended = head_outputs.transpose(1, 0, 2).reshape(seq_len, query_local * HEAD_WIDTH)
    partial_out = jnp.dot(attended, output_weight, preferred_element_type=jnp.float32)
    row_count = seq_len // 8
    parts = lax.all_to_all(
        partial_out.astype(jnp.bfloat16).reshape(8, row_count, model_width), "tp", 0, 0, tiled=True
    )
    attn_sum = jnp.sum(parts.astype(jnp.float32), axis=0)
    own_rows = lax.dynamic_slice_in_dim(tokens_in, tp_index * row_count, row_count, 0)
    hidden = own_rows.astype(jnp.float32) + attn_sum
    moe_in = rms_scale(hidden, moe_gain).astype(jnp.bfloat16)
    expert_count = router.shape[1]
    capacity = 48
    logits = jnp.dot(moe_in, router, preferred_element_type=jnp.float32)
    host = jnp.arange(expert_count)
    expert_at = (host // 16) * 16 + (host % 8) * 2 + (host // 8) % 2
    logits = logits.reshape(row_count, 2, 8, 2).transpose(0, 1, 3, 2).reshape(row_count, expert_count)
    chosen = jnp.any(expert_ids[:, :, None] == expert_at[None, None, :], axis=1)
    top_logit = jnp.max(jnp.where(chosen, logits, -jnp.inf), axis=-1, keepdims=True)
    raised = jnp.where(chosen, jnp.exp(logits - top_logit), 0.0)
    gates = raised / jnp.sum(raised, axis=-1, keepdims=True)
    token = jnp.arange(row_count)
    before = (token[None, :] < token[:, None]).astype(jnp.bfloat16)
    rank = jnp.dot(before, chosen.astype(jnp.bfloat16), preferred_element_type=jnp.float32)
    rank = jnp.where(chosen, rank, -1.0)
    slots = jnp.arange(capacity, dtype=jnp.float32)
    place = (rank.T[:, None, :] == slots[None, :, None]).astype(jnp.bfloat16)
    send_rows = jnp.dot(
        place.reshape(expert_count * capacity, row_count), moe_in, preferred_element_type=jnp.float32
    ).astype(jnp.bfloat16)
    received = lax.all_to_all(
        send_rows.reshape(expert_count, capacity, model_width), ("ep", "tp"), 0, 0,
        axis_index_groups=PLANE_GROUPS, tiled=True,
    ).reshape(expert_count * capacity, model_width)
    gate_up = jnp.dot(received, gate_up_full, preferred_element_type=jnp.float32)
    activated = (jax.nn.silu(gate_up[..., :FF]) * gate_up[..., FF:]).astype(jnp.bfloat16)
    expert_out = jnp.dot(activated, down_full, preferred_element_type=jnp.float32).astype(jnp.bfloat16)
    returned = lax.all_to_all(
        expert_out.reshape(expert_count, capacity, model_width), ("ep", "tp"), 0, 0,
        axis_index_groups=PLANE_GROUPS, tiled=True,
    ).reshape(expert_count * capacity, model_width)
    weigh = jnp.where(rank[:, :, None] == slots, gates[:, :, None], 0.0).reshape(row_count, -1)
    weigh_high = weigh.astype(jnp.bfloat16)
    weigh_low = (weigh - weigh_high.astype(jnp.float32)).astype(jnp.bfloat16)
    mixed = jnp.dot(
        jnp.concatenate([weigh_high, weigh_low], axis=1),
        jnp.concatenate([returned, returned], axis=0),
        preferred_element_type=jnp.float32,
    )
    valid = tp_index * row_count + jnp.arange(row_count) < length_here
    return jnp.where(valid[:, None], hidden + mixed, 0.0).astype(jnp.bfloat16)


def solution(mesh):
    in_specs = (
        P("ep", None),
        P("ep"),
        P(),
        P("ep", "tp"),
        P("ep", "tp"),
        P("ep", "tp"),
        P("tp", "ep"),
        P("ep", None, "tp"),
        P(None, "ep", None),
        P(),
        P(),
        P(("ep", "tp"), None),
        P("ep", "tp", None),
        P("ep", "tp", None),
    )
    out_specs = P(("ep", "tp"), None)
    return jax.shard_map(
        on_device, mesh=mesh, in_specs=in_specs, out_specs=out_specs, check_vma=False
    )
```

```python
import math

import jax
import jax.numpy as jnp
from jax import lax
from jax.experimental import pallas as pl
from jax.experimental.pallas import tpu as pltpu
from jax.sharding import PartitionSpec as P

HEAD_WIDTH = 64
FF = 512
CAPACITY = 48
EXPERTS = 32


epsilon = 1e-05

Z_GROUPS = [[y * 16 + z * 2 + c for z in range(8)] for y in range(2) for c in range(2)]
CHIP_PAIR_GROUPS = [[y * 16 + z * 2 + c for y in range(2) for c in range(2)] for z in range(8)]
PLANE_GROUPS = [
    [(y * 16 + z * 2 + c) * 8 + t for y in range(2) for c in range(2) for t in range(8)]
    for z in range(8)
]


def rms_scale(values, norm_gain):
    mean_square = jnp.mean(values * values, axis=-1, keepdims=True)
    return values * lax.rsqrt(mean_square + epsilon) * norm_gain


def apply_rotary(vectors, token_positions):
    half_width = vectors.shape[-1] // 2
    frequency = jnp.exp(
        jnp.arange(half_width, dtype=jnp.float32) * (-2.0 * math.log(10000.0) / vectors.shape[-1])
    )
    angles = token_positions.astype(jnp.float32)[:, None] * frequency[None, :]
    cosine = jnp.cos(angles)[:, None, :]
    sine_table = jnp.sin(angles)[:, None, :]
    first_half = vectors[..., :half_width]
    second_half = vectors[..., half_width:]
    return jnp.concatenate(
        [
            first_half * cosine - second_half * sine_table,
            second_half * cosine + first_half * sine_table,
        ],
        axis=-1,
    )


def project_body(
    parts_ref, weight_hbm, rows_ref, gain_ref, router_ref, ids_ref,
    hidden_ref, send_ref, high_ref, low_ref,
    weight, attended, place, sem,
):
    copies = []
    for z in range(8):
        for y in range(2):
            copy = pltpu.make_async_copy(
                weight_hbm.at[z, y], weight.at[pl.ds((y * 8 + z) * 96, 96)], sem.at[z * 2 + y]
            )
            copy.start()
            copies.append(copy)
    for t in range(8):
        attended[:, t * 192 : (t + 1) * 192] = parts_ref[t]
    tokens = rows_ref.shape[0]
    host = lax.broadcasted_iota(jnp.int32, (EXPERTS, tokens), 0)
    expert_at = (host // 16) * 16 + (host % 8) * 2 + (host // 8) % 2
    chosen = jnp.zeros((EXPERTS, tokens), jnp.float32)
    for k in range(ids_ref.shape[0]):
        chosen = jnp.where(ids_ref[k : k + 1, :] == expert_at, 1.0, chosen)
    earlier = lax.broadcasted_iota(jnp.int32, (tokens, tokens), 0) < lax.broadcasted_iota(
        jnp.int32, (tokens, tokens), 1
    )
    rank = jnp.dot(
        chosen.astype(jnp.bfloat16),
        jnp.where(earlier, 1.0, 0.0).astype(jnp.bfloat16),
        preferred_element_type=jnp.float32,
    )
    rank = jnp.where(chosen > 0.0, rank, -1.0)
    slot = lax.broadcasted_iota(jnp.int32, (CAPACITY, tokens), 0).astype(jnp.float32)
    for g in range(EXPERTS):
        place[g * CAPACITY : (g + 1) * CAPACITY, :] = jnp.where(
            rank[g : g + 1, :] == slot, 1.0, 0.0
        ).astype(jnp.bfloat16)
    for copy in copies:
        copy.wait()
    for c in range(0, 1536, 256):
        hidden_ref[:, c : c + 256] = rows_ref[:, c : c + 256].astype(jnp.float32) + lax.dot_general(
            attended[...],
            weight[c : c + 256, :],
            (((1,), (1,)), ((), ())),
            preferred_element_type=jnp.float32,
        )
    hidden = hidden_ref[...]
    moe_in = rms_scale(hidden, gain_ref[...]).astype(jnp.bfloat16)
    for c in range(0, EXPERTS * CAPACITY, 256):
        send_ref[c : c + 256, :] = jnp.dot(
            place[c : c + 256, :], moe_in, preferred_element_type=jnp.float32
        ).astype(jnp.bfloat16)
    logits = lax.dot_general(
        router_ref[...], moe_in, (((1,), (1,)), ((), ())), preferred_element_type=jnp.float32
    )
    top_logit = jnp.max(jnp.where(chosen > 0.0, logits, -3e38), axis=0, keepdims=True)
    raised = jnp.where(chosen > 0.0, jnp.exp(jnp.minimum(logits - top_logit, 0.0)), 0.0)
    gates = raised / jnp.sum(raised, axis=0, keepdims=True)
    for g in range(EXPERTS):
        weigh = place[g * CAPACITY : (g + 1) * CAPACITY, :].astype(jnp.float32) * gates[g : g + 1, :]
        high = weigh.astype(jnp.bfloat16)
        high_ref[g * CAPACITY : (g + 1) * CAPACITY, :] = high
        low_ref[g * CAPACITY : (g + 1) * CAPACITY, :] = (
            weigh - high.astype(jnp.float32)
        ).astype(jnp.bfloat16)


def project_and_dispatch(parts, output_weight, own_rows, moe_gain, router_hosted, ids_by_choice):
    row_count, model_width = own_rows.shape
    slots = EXPERTS * CAPACITY
    vmem = pl.BlockSpec(memory_space=pltpu.VMEM)
    return pl.pallas_call(
        project_body,
        out_shape=(
            jax.ShapeDtypeStruct((row_count, model_width), jnp.float32),
            jax.ShapeDtypeStruct((slots, model_width), jnp.bfloat16),
            jax.ShapeDtypeStruct((slots, row_count), jnp.bfloat16),
            jax.ShapeDtypeStruct((slots, row_count), jnp.bfloat16),
        ),
        in_specs=[vmem, pl.BlockSpec(memory_space=pltpu.HBM), vmem, vmem, vmem, vmem],
        out_specs=(vmem, vmem, vmem, vmem),
        scratch_shapes=[
            pltpu.VMEM((model_width, model_width), jnp.bfloat16),
            pltpu.VMEM((row_count, model_width), jnp.bfloat16),
            pltpu.VMEM((slots, row_count), jnp.bfloat16),
            pltpu.SemaphoreType.DMA((16,)),
        ],
        compiler_params=pltpu.CompilerParams(vmem_limit_bytes=40 << 20),
        cost_estimate=pl.CostEstimate(
            flops=4 * row_count * model_width * model_width,
            bytes_accessed=4 * model_width * model_width,
            transcendentals=0,
        ),
        name="project_and_dispatch",
    )(
        parts,
        output_weight.reshape(8, 2, 96, model_width),
        own_rows,
        moe_gain.reshape(1, model_width),
        router_hosted,
        ids_by_choice,
    )


def on_device(
    tokens_in,
    lengths,
    attn_gain,
    q_proj,
    k_proj,
    value_projection,
    o_proj,
    key_value_pages,
    page_table,
    moe_gain,
    router,
    expert_ids,
    gate_up_proj,
    down_proj,
):
    seq_len, model_width = tokens_in.shape
    ep_count = lax.axis_size("ep")
    tp_index = lax.axis_index("tp")
    kv_local = key_value_pages.shape[2] // (2 * HEAD_WIDTH)
    query_local = q_proj.shape[1] // HEAD_WIDTH
    packed_shard = jnp.concatenate(
        [q_proj, k_proj, value_projection], axis=1
    ).astype(jnp.bfloat16)
    gate_up_planes = lax.all_gather(
        gate_up_proj[0].astype(jnp.bfloat16), "ep", axis_index_groups=Z_GROUPS
    )
    along_z = lax.all_to_all(
        jnp.broadcast_to(packed_shard[None], (8, *packed_shard.shape)),
        "ep", 0, 0, axis_index_groups=Z_GROUPS, tiled=True,
    )
    across = lax.all_to_all(
        jnp.broadcast_to(along_z[None], (4, *along_z.shape)),
        "ep", 0, 0, axis_index_groups=CHIP_PAIR_GROUPS, tiled=True,
    )
    packed = (
        across.reshape(2, 2, 8, *packed_shard.shape)
        .transpose(0, 2, 1, 3, 4)
        .reshape(model_width, packed_shard.shape[1])
    )
    query_weight = packed[:, :192]
    key_matrix = packed[:, 192:256]
    value_matrix = packed[:, 256:320]
    chosen_pages = key_value_pages[page_table[:, 0, :]]
    chosen_pages, across = lax.optimization_barrier((chosen_pages, across))
    arrived = lax.all_to_all(chosen_pages, "ep", split_axis=0, concat_axis=0, tiled=True)
    output_shard = o_proj.T.astype(jnp.bfloat16)
    output_shard, arrived = lax.optimization_barrier((output_shard, arrived))
    output_plane = lax.all_to_all(
        jnp.broadcast_to(output_shard[None], (32, *output_shard.shape)),
        ("ep", "tp"), 0, 0, axis_index_groups=PLANE_GROUPS, tiled=True,
    )
    output_plane = (
        output_plane.reshape(4, 8, 48, 192).transpose(0, 2, 1, 3).reshape(192, model_width)
    )
    output_plane, gate_up_planes = lax.optimization_barrier((output_plane, gate_up_planes))
    output_weight = lax.all_gather(output_plane, "ep", axis_index_groups=Z_GROUPS)
    gate_up_full = lax.all_to_all(gate_up_planes, "tp", 0, 0, tiled=True).reshape(model_width, -1)
    prefix_length = arrived.shape[0] * arrived.shape[1] * arrived.shape[2]
    prefix = arrived.reshape(prefix_length, kv_local, 2, HEAD_WIDTH)
    normalized_input = rms_scale(tokens_in.astype(jnp.float32), attn_gain).astype(jnp.bfloat16)
    token_positions = prefix_length + jnp.arange(seq_len)
    query_rows = apply_rotary(
        jnp.dot(normalized_input, query_weight, preferred_element_type=jnp.float32).reshape(
            seq_len, query_local, HEAD_WIDTH
        ),
        token_positions,
    ).astype(jnp.bfloat16)
    fresh_keys = apply_rotary(
        jnp.dot(normalized_input, key_matrix, preferred_element_type=jnp.float32).reshape(
            seq_len, kv_local, HEAD_WIDTH
        ),
        token_positions,
    ).astype(jnp.bfloat16)
    fresh_values = (
        jnp.dot(normalized_input, value_matrix, preferred_element_type=jnp.float32)
        .reshape(seq_len, kv_local, HEAD_WIDTH)
        .astype(jnp.bfloat16)
    )
    length_here = lengths[0]
    own = jnp.arange(prefix_length + seq_len)[None, :] - prefix_length
    block_rows = min(512, seq_len)
    all_keys = jnp.concatenate([prefix[:, 0, 0], fresh_keys[:, 0]], 0)
    all_values = jnp.concatenate([prefix[:, 0, 1], fresh_values[:, 0]], 0)
    grouped_queries = query_rows.transpose(1, 0, 2)
    blocks = []
    for block_start in range(0, seq_len, block_rows):
        query_block = grouped_queries[:, block_start : block_start + block_rows]
        scores = jnp.einsum(
            "gqd,kd->gqk", query_block, all_keys, preferred_element_type=jnp.float32
        ) * HEAD_WIDTH ** (-0.5)
        query_pos = block_start + jnp.arange(block_rows)
        allowed = (own < 0) | (own <= query_pos[:, None]) & (own < length_here)
        scores = jnp.where(allowed[None], scores, -1e30)
        top_score = jnp.max(scores, axis=-1, keepdims=True)
        weights = jnp.exp(scores - top_score)
        probs = (weights / jnp.sum(weights, axis=-1, keepdims=True)).astype(jnp.bfloat16)
        blocks.append(
            jnp.einsum("gqk,kd->gqd", probs, all_values, preferred_element_type=jnp.float32).astype(
                jnp.bfloat16
            )
        )
    head_outputs = jnp.concatenate(blocks, axis=1)
    attended = head_outputs.transpose(1, 0, 2).reshape(seq_len, query_local * HEAD_WIDTH)
    attended, gate_up_full = lax.optimization_barrier((attended, gate_up_full))
    row_count = seq_len // 8
    attn_parts = lax.all_to_all(
        attended.reshape(8, row_count, query_local * HEAD_WIDTH), "tp", 0, 0, tiled=True
    )
    own_rows = lax.dynamic_slice_in_dim(tokens_in, tp_index * row_count, row_count, 0)
    router_hosted = router.T.reshape(2, 8, 2, model_width).transpose(0, 2, 1, 3)
    hidden, send_rows, weigh_high, weigh_low = project_and_dispatch(
        attn_parts,
        output_weight,
        own_rows,
        moe_gain,
        router_hosted.reshape(EXPERTS, model_width),
        expert_ids.T,
    )
    received = lax.all_to_all(
        send_rows.reshape(EXPERTS, CAPACITY, model_width), ("ep", "tp"), 0, 0,
        axis_index_groups=PLANE_GROUPS, tiled=True,
    ).reshape(EXPERTS * CAPACITY, model_width)
    down_shard, output_weight = lax.optimization_barrier(
        (down_proj[0].astype(jnp.bfloat16), output_weight)
    )
    down_planes = lax.all_gather(down_shard, "ep", axis_index_groups=Z_GROUPS)
    down_planes, received = lax.optimization_barrier((down_planes, received))
    down_full = lax.all_to_all(down_planes, "tp", 0, 0, tiled=True).reshape(-1, model_width)
    gate_up = jnp.dot(received, gate_up_full, preferred_element_type=jnp.float32)
    activated = (jax.nn.silu(gate_up[..., :FF]) * gate_up[..., FF:]).astype(jnp.bfloat16)
    expert_out = jnp.dot(activated, down_full, preferred_element_type=jnp.float32).astype(jnp.bfloat16)
    returned = lax.all_to_all(
        expert_out.reshape(EXPERTS, CAPACITY, model_width), ("ep", "tp"), 0, 0,
        axis_index_groups=PLANE_GROUPS, tiled=True,
    ).reshape(EXPERTS * CAPACITY, model_width)
    mixed = lax.dot_general(
        jnp.concatenate([weigh_high, weigh_low], axis=0),
        jnp.concatenate([returned, returned], axis=0),
        (((0,), (0,)), ((), ())),
        preferred_element_type=jnp.float32,
    )
    valid = tp_index * row_count + jnp.arange(row_count) < length_here
    return jnp.where(valid[:, None], hidden + mixed, 0.0).astype(jnp.bfloat16)


def solution(mesh):
    in_specs = (
        P("ep", None),
        P("ep"),
        P(),
        P("ep", "tp"),
        P("ep", "tp"),
        P("ep", "tp"),
        P("tp", "ep"),
        P("ep", None, "tp"),
        P(None, "ep", None),
        P(),
        P(),
        P(("ep", "tp"), None),
        P("ep", "tp", None),
        P("ep", "tp", None),
    )
    out_specs = P(("ep", "tp"), None)
    return jax.shard_map(
        on_device, mesh=mesh, in_specs=in_specs, out_specs=out_specs, check_vma=False
    )
```

```python
import math

import jax
import jax.numpy as jnp
from jax import lax
from jax.experimental import pallas as pl
from jax.experimental.pallas import tpu as pltpu
from jax.sharding import PartitionSpec as P

HEAD_WIDTH = 64
FF = 512
CAPACITY = 48
HALF = CAPACITY // 2
EXPERTS = 32


epsilon = 1e-05

Z_GROUPS = [[y * 16 + z * 2 + c for z in range(8)] for y in range(2) for c in range(2)]
CHIP_PAIR_GROUPS = [[y * 16 + z * 2 + c for y in range(2) for c in range(2)] for z in range(8)]
PLANE_GROUPS = [
    [(y * 16 + z * 2 + c) * 8 + t for y in range(2) for c in range(2) for t in range(8)]
    for z in range(8)
]


def rms_scale(values, norm_gain):
    mean_square = jnp.mean(values * values, axis=-1, keepdims=True)
    return values * lax.rsqrt(mean_square + epsilon) * norm_gain


def rotary_tables(positions, first_position):
    lane = jnp.arange(2 * HEAD_WIDTH)
    frequency = jnp.exp(
        (lane % (HEAD_WIDTH // 2)).astype(jnp.float32) * (-2.0 * math.log(10000.0) / HEAD_WIDTH)
    )
    angles = (first_position + jnp.arange(positions)).astype(jnp.float32)[:, None] * frequency
    sign = jnp.where(lane % HEAD_WIDTH < HEAD_WIDTH // 2, -1.0, 1.0)
    return jnp.cos(angles), jnp.sin(angles) * sign


def attention_body(
    length_ref, tokens_ref, gain_ref, weight_ref, pages_ref, cosine_ref, sine_ref,
    out_ref, queries, keys, values,
):
    seq_len = tokens_ref.shape[0]
    prefix = pages_ref.shape[0]
    heads = queries.shape[0]
    chunk = 256
    lane = lax.broadcasted_iota(jnp.int32, (chunk, 256), 1)
    ones = jnp.ones((chunk, HEAD_WIDTH), jnp.bfloat16)
    for c in range(0, prefix, chunk):
        rows = pages_ref[c : c + chunk, :]
        keys[:, c : c + chunk] = rows.astype(jnp.float32).T[:HEAD_WIDTH].astype(jnp.bfloat16)
        values[c : c + chunk, :] = jnp.concatenate([rows[:, HEAD_WIDTH:], ones], axis=1)
    for c in range(0, seq_len, chunk):
        normalized = rms_scale(
            tokens_ref[c : c + chunk, :].astype(jnp.float32), gain_ref[...]
        ).astype(jnp.bfloat16)
        projected = jnp.dot(normalized, weight_ref[...], preferred_element_type=jnp.float32)
        plain = projected[:, :256]
        partner = jnp.where(
            lane % HEAD_WIDTH < HEAD_WIDTH // 2,
            pltpu.roll(plain, 256 - HEAD_WIDTH // 2, 1),
            pltpu.roll(plain, HEAD_WIDTH // 2, 1),
        )
        cosine = cosine_ref[c : c + chunk, :]
        sine = sine_ref[c : c + chunk, :]
        rotated = plain * jnp.concatenate([cosine, cosine], axis=1) + partner * jnp.concatenate(
            [sine, sine], axis=1
        )
        rounded = rotated.astype(jnp.bfloat16)
        for h in range(heads):
            queries[h, c : c + chunk, :] = (
                rounded[:, h * HEAD_WIDTH : (h + 1) * HEAD_WIDTH] * HEAD_WIDTH ** (-0.5)
            ).astype(jnp.bfloat16)
        keys[:, prefix + c : prefix + c + chunk] = (
            rotated.T[heads * HEAD_WIDTH :].astype(jnp.bfloat16)
        )
        values[prefix + c : prefix + c + chunk, :] = jnp.concatenate(
            [projected[:, 256 : 256 + HEAD_WIDTH].astype(jnp.bfloat16), ones], axis=1
        )
    block = out_ref.shape[1]
    length = length_ref[0]
    column = lax.broadcasted_iota(jnp.int32, (block, seq_len), 1)
    row = lax.broadcasted_iota(jnp.int32, (block, seq_len), 0)

    def one_block(i, carry):
        start = pl.multiple_of(i * block, block)
        allowed = (column <= row + start) & (column < length)
        outs = []
        for h in range(heads):
            query = queries[h, pl.ds(start, block), :]
            cached = jnp.dot(query, keys[:, :prefix], preferred_element_type=jnp.float32)
            own = jnp.dot(query, keys[:, prefix:], preferred_element_type=jnp.float32)
            own = jnp.where(allowed, own, -1e30)
            top = jnp.maximum(
                jnp.max(cached, axis=1, keepdims=True), jnp.max(own, axis=1, keepdims=True)
            )
            total = jnp.dot(
                jnp.exp(cached - top).astype(jnp.bfloat16),
                values[:prefix, :],
                preferred_element_type=jnp.float32,
            ) + jnp.dot(
                jnp.exp(own - top).astype(jnp.bfloat16),
                values[prefix:, :],
                preferred_element_type=jnp.float32,
            )
            outs.append(total[:, :HEAD_WIDTH] / total[:, HEAD_WIDTH : HEAD_WIDTH + 1])
        out_ref[i] = jnp.concatenate(outs, axis=1).astype(jnp.bfloat16)
        return carry

    lax.fori_loop(0, out_ref.shape[0], one_block, 0)


def attention(lengths, tokens, gain, weight, pages, cosine, sine, blocks):
    seq_len, model_width = tokens.shape
    heads = 3
    total = seq_len + pages.shape[0]
    vmem = pl.BlockSpec(memory_space=pltpu.VMEM)
    return pl.pallas_call(
        attention_body,
        out_shape=jax.ShapeDtypeStruct((blocks, seq_len // blocks, heads * HEAD_WIDTH), jnp.bfloat16),
        in_specs=[pl.BlockSpec(memory_space=pltpu.SMEM)] + [vmem] * 6,
        out_specs=vmem,
        scratch_shapes=[
            pltpu.VMEM((heads, seq_len, HEAD_WIDTH), jnp.bfloat16),
            pltpu.VMEM((HEAD_WIDTH, total), jnp.bfloat16),
            pltpu.VMEM((total, 2 * HEAD_WIDTH), jnp.bfloat16),
        ],
        compiler_params=pltpu.CompilerParams(vmem_limit_bytes=40 << 20),
        cost_estimate=pl.CostEstimate(
            flops=30_000_000_000, bytes_accessed=8 << 20, transcendentals=heads * seq_len * total
        ),
        name="attention",
    )(lengths, tokens, gain.reshape(1, model_width), weight, pages, cosine, sine)


def project_body(
    parts_ref, weight_hbm, rows_ref, gain_ref, router_ref, ids_ref,
    hidden_ref, first_ref, second_ref, high_ref, low_ref,
    weight, attended, place, sem,
):
    copies = []
    for z in range(8):
        for y in range(2):
            copy = pltpu.make_async_copy(
                weight_hbm.at[z, y], weight.at[pl.ds((y * 8 + z) * 96, 96)], sem.at[z * 2 + y]
            )
            copy.start()
            copies.append(copy)
    for t in range(8):
        attended[:, t * 192 : (t + 1) * 192] = parts_ref[t]
    tokens = rows_ref.shape[0]
    host = lax.broadcasted_iota(jnp.int32, (EXPERTS, tokens), 0)
    expert_at = (host // 16) * 16 + (host % 8) * 2 + (host // 8) % 2
    chosen = jnp.zeros((EXPERTS, tokens), jnp.float32)
    for k in range(ids_ref.shape[0]):
        chosen = jnp.where(ids_ref[k : k + 1, :] == expert_at, 1.0, chosen)
    earlier = lax.broadcasted_iota(jnp.int32, (tokens, tokens), 0) < lax.broadcasted_iota(
        jnp.int32, (tokens, tokens), 1
    )
    rank = jnp.dot(
        chosen.astype(jnp.bfloat16),
        jnp.where(earlier, 1.0, 0.0).astype(jnp.bfloat16),
        preferred_element_type=jnp.float32,
    )
    rank = jnp.where(chosen > 0.0, rank, -1.0)
    slot = lax.broadcasted_iota(jnp.int32, (HALF, tokens), 0).astype(jnp.float32)
    for half in range(2):
        for g in range(EXPERTS):
            at = (half * EXPERTS + g) * HALF
            place[at : at + HALF, :] = jnp.where(
                rank[g : g + 1, :] == slot + float(half * HALF), 1.0, 0.0
            ).astype(jnp.bfloat16)
    for copy in copies:
        copy.wait()
    for c in range(0, 1536, 256):
        hidden_ref[:, c : c + 256] = rows_ref[:, c : c + 256].astype(jnp.float32) + lax.dot_general(
            attended[...],
            weight[c : c + 256, :],
            (((1,), (1,)), ((), ())),
            preferred_element_type=jnp.float32,
        )
    hidden = hidden_ref[...]
    moe_in = rms_scale(hidden, gain_ref[...]).astype(jnp.bfloat16)
    for half, send_ref in enumerate((first_ref, second_ref)):
        for c in range(0, EXPERTS * HALF, 256):
            at = half * EXPERTS * HALF + c
            send_ref[c : c + 256, :] = jnp.dot(
                place[at : at + 256, :], moe_in, preferred_element_type=jnp.float32
            ).astype(jnp.bfloat16)
    logits = lax.dot_general(
        router_ref[...], moe_in, (((1,), (1,)), ((), ())), preferred_element_type=jnp.float32
    )
    top_logit = jnp.max(jnp.where(chosen > 0.0, logits, -3e38), axis=0, keepdims=True)
    raised = jnp.where(chosen > 0.0, jnp.exp(jnp.minimum(logits - top_logit, 0.0)), 0.0)
    gates = raised / jnp.sum(raised, axis=0, keepdims=True)
    for half in range(2):
        for g in range(EXPERTS):
            at = (half * EXPERTS + g) * HALF
            weigh = place[at : at + HALF, :].astype(jnp.float32) * gates[g : g + 1, :]
            high = weigh.astype(jnp.bfloat16)
            high_ref[at : at + HALF, :] = high
            low_ref[at : at + HALF, :] = (weigh - high.astype(jnp.float32)).astype(jnp.bfloat16)


def project_and_dispatch(parts, output_weight, own_rows, moe_gain, router_hosted, ids_by_choice):
    row_count, model_width = own_rows.shape
    slots = EXPERTS * CAPACITY
    vmem = pl.BlockSpec(memory_space=pltpu.VMEM)
    return pl.pallas_call(
        project_body,
        out_shape=(
            jax.ShapeDtypeStruct((row_count, model_width), jnp.float32),
            jax.ShapeDtypeStruct((slots // 2, model_width), jnp.bfloat16),
            jax.ShapeDtypeStruct((slots // 2, model_width), jnp.bfloat16),
            jax.ShapeDtypeStruct((slots, row_count), jnp.bfloat16),
            jax.ShapeDtypeStruct((slots, row_count), jnp.bfloat16),
        ),
        in_specs=[vmem, pl.BlockSpec(memory_space=pltpu.HBM), vmem, vmem, vmem, vmem],
        out_specs=(vmem, vmem, vmem, vmem, vmem),
        scratch_shapes=[
            pltpu.VMEM((model_width, model_width), jnp.bfloat16),
            pltpu.VMEM((row_count, model_width), jnp.bfloat16),
            pltpu.VMEM((slots, row_count), jnp.bfloat16),
            pltpu.SemaphoreType.DMA((16,)),
        ],
        compiler_params=pltpu.CompilerParams(vmem_limit_bytes=40 << 20),
        cost_estimate=pl.CostEstimate(
            flops=4 * row_count * model_width * model_width,
            bytes_accessed=4 * model_width * model_width,
            transcendentals=0,
        ),
        name="project_and_dispatch",
    )(
        parts,
        output_weight.reshape(8, 2, 96, model_width),
        own_rows,
        moe_gain.reshape(1, model_width),
        router_hosted,
        ids_by_choice,
    )


def on_device(
    tokens_in,
    lengths,
    attn_gain,
    q_proj,
    k_proj,
    value_projection,
    o_proj,
    key_value_pages,
    page_table,
    moe_gain,
    router,
    expert_ids,
    gate_up_proj,
    down_proj,
):
    seq_len, model_width = tokens_in.shape
    barrier = lax.optimization_barrier
    tp_index = lax.axis_index("tp")
    row_count = seq_len // 8

    def in_plane(rows):
        return lax.all_to_all(
            rows, ("ep", "tp"), 0, 0, axis_index_groups=PLANE_GROUPS, tiled=True
        )

    gate_up_planes = lax.all_gather(
        gate_up_proj[0].astype(jnp.bfloat16), "ep", axis_index_groups=Z_GROUPS
    )
    output_shard = o_proj.T.astype(jnp.bfloat16)
    output_plane = in_plane(jnp.broadcast_to(output_shard[None], (EXPERTS, *output_shard.shape)))
    output_plane = (
        output_plane.reshape(4, 8, 48, 192).transpose(0, 2, 1, 3).reshape(192, model_width)
    )
    output_weight = lax.all_gather(output_plane, "ep", axis_index_groups=Z_GROUPS)

    weight_shard = jnp.concatenate(
        [q_proj, k_proj, value_projection, jnp.zeros_like(k_proj)], axis=1
    ).astype(jnp.bfloat16)
    slabs = weight_shard.reshape(48, 3, 128).transpose(1, 0, 2).reshape(144, 128)
    pages = key_value_pages[page_table[:, 0, :]].reshape(2, 8, 2, 32, 128)
    payload = jnp.concatenate(
        [
            jnp.broadcast_to(slabs[None], (8, 144, 128)),
            pages.transpose(1, 0, 2, 3, 4).reshape(8, 128, 128),
        ],
        axis=1,
    )
    payload, output_plane = barrier((payload, output_plane))
    along_z = lax.all_to_all(payload, "ep", 0, 0, axis_index_groups=Z_GROUPS, tiled=True)
    payload = jnp.concatenate(
        [
            jnp.broadcast_to(along_z[None, :, :144], (4, 8, 144, 128)),
            along_z[:, 144:].reshape(8, 4, 32, 128).transpose(1, 0, 2, 3),
        ],
        axis=2,
    )
    across = lax.all_to_all(payload, "ep", 0, 0, axis_index_groups=CHIP_PAIR_GROUPS, tiled=True)
    weight = (
        across[:, :, :144]
        .reshape(2, 2, 8, 3, 48, 128)
        .transpose(0, 2, 1, 4, 3, 5)
        .reshape(model_width, 384)
    )
    prefix = across[:, :, 144:].reshape(2, 2, 8, 32, 128).transpose(0, 2, 1, 3, 4).reshape(-1, 128)
    cosine, sine = rotary_tables(seq_len, prefix.shape[0])
    weight, prefix, gate_up_planes = barrier((weight, prefix, gate_up_planes))
    gate_up_full = lax.all_to_all(gate_up_planes, "tp", 0, 0, tiled=True).reshape(model_width, -1)
    attended = attention(lengths, tokens_in, attn_gain, weight, prefix, cosine, sine, 8)
    attended, gate_up_full = barrier((attended, gate_up_full))
    attn_parts = lax.all_to_all(attended, "tp", 0, 0, tiled=True)
    own_rows = lax.dynamic_slice_in_dim(tokens_in, tp_index * row_count, row_count, 0)
    router_hosted = router.T.reshape(2, 8, 2, model_width).transpose(0, 2, 1, 3)
    hidden, send_first, send_second, weigh_high, weigh_low = project_and_dispatch(
        attn_parts,
        output_weight,
        own_rows,
        moe_gain,
        router_hosted.reshape(EXPERTS, model_width),
        expert_ids.T,
    )
    down_shard, output_plane = barrier((down_proj[0].astype(jnp.bfloat16), output_plane))
    down_planes = lax.all_gather(down_shard, "ep", axis_index_groups=Z_GROUPS)

    def experts(rows):
        rows = rows.reshape(EXPERTS * HALF, model_width)
        gate_up = jnp.dot(rows, gate_up_full, preferred_element_type=jnp.float32)
        activated = (jax.nn.silu(gate_up[..., :FF]) * gate_up[..., FF:]).astype(jnp.bfloat16)
        return (
            jnp.dot(activated, down_full, preferred_element_type=jnp.float32)
            .astype(jnp.bfloat16)
            .reshape(EXPERTS, HALF, model_width)
        )

    def mix(returned, half):
        at = slice(half * EXPERTS * HALF, (half + 1) * EXPERTS * HALF)
        rows = returned.reshape(EXPERTS * HALF, model_width)
        return lax.dot_general(
            jnp.concatenate([weigh_high[at], weigh_low[at]], axis=0),
            jnp.concatenate([rows, rows], axis=0),
            (((0,), (0,)), ((), ())),
            preferred_element_type=jnp.float32,
        )

    received_first = in_plane(send_first.reshape(EXPERTS, HALF, model_width))
    down_planes, received_first = barrier((down_planes, received_first))
    down_full = lax.all_to_all(down_planes, "tp", 0, 0, tiled=True).reshape(-1, model_width)
    send_second, down_full = barrier((send_second, down_full))
    received_second = in_plane(send_second.reshape(EXPERTS, HALF, model_width))
    out_first, received_second = barrier((experts(received_first), received_second))
    returned_first = in_plane(out_first)
    out_second, returned_first = barrier((experts(received_second), returned_first))
    returned_second = in_plane(out_second)
    mixed = hidden + mix(returned_first, 0) + mix(returned_second, 1)
    valid = tp_index * row_count + jnp.arange(row_count) < lengths[0]
    return jnp.where(valid[:, None], mixed, 0.0).astype(jnp.bfloat16)


def solution(mesh):
    in_specs = (
        P("ep", None),
        P("ep"),
        P(),
        P("ep", "tp"),
        P("ep", "tp"),
        P("ep", "tp"),
        P("tp", "ep"),
        P("ep", None, "tp"),
        P(None, "ep", None),
        P(),
        P(),
        P(("ep", "tp"), None),
        P("ep", "tp", None),
        P("ep", "tp", None),
    )
    out_specs = P(("ep", "tp"), None)
    return jax.shard_map(
        on_device, mesh=mesh, in_specs=in_specs, out_specs=out_specs, check_vma=False
    )
```

```python
import math

import jax
import jax.numpy as jnp
from jax import lax
from jax.experimental import pallas as pl
from jax.experimental.pallas import tpu as pltpu
from jax.sharding import PartitionSpec as P

HEAD_WIDTH = 64
FF = 512
CAPACITY = 48
EXPERTS = 32


epsilon = 1e-05

Z_GROUPS = [[y * 16 + z * 2 + c for z in range(8)] for y in range(2) for c in range(2)]
CHIP_PAIR_GROUPS = [[y * 16 + z * 2 + c for y in range(2) for c in range(2)] for z in range(8)]
PLANE_GROUPS = [
    [(y * 16 + z * 2 + c) * 8 + t for y in range(2) for c in range(2) for t in range(8)]
    for z in range(8)
]


def rms_scale(values, norm_gain):
    mean_square = jnp.mean(values * values, axis=-1, keepdims=True)
    return values * lax.rsqrt(mean_square + epsilon) * norm_gain


def rotary_tables(positions, first_position):
    lane = jnp.arange(2 * HEAD_WIDTH)
    frequency = jnp.exp(
        (lane % (HEAD_WIDTH // 2)).astype(jnp.float32) * (-2.0 * math.log(10000.0) / HEAD_WIDTH)
    )
    angles = (first_position + jnp.arange(positions)).astype(jnp.float32)[:, None] * frequency
    sign = jnp.where(lane % HEAD_WIDTH < HEAD_WIDTH // 2, -1.0, 1.0)
    return jnp.cos(angles), jnp.sin(angles) * sign


def attention_body(
    length_ref, tokens_ref, gain_ref, weight_ref, pages_ref, cosine_ref, sine_ref,
    out_ref, queries, keys, values,
):
    seq_len = tokens_ref.shape[0]
    prefix = pages_ref.shape[0]
    heads = queries.shape[0]
    chunk = 256
    lane = lax.broadcasted_iota(jnp.int32, (chunk, 256), 1)
    ones = jnp.ones((chunk, HEAD_WIDTH), jnp.bfloat16)
    for c in range(0, prefix, chunk):
        rows = pages_ref[c : c + chunk, :]
        keys[:, c : c + chunk] = rows.astype(jnp.float32).T[:HEAD_WIDTH].astype(jnp.bfloat16)
        values[c : c + chunk, :] = jnp.concatenate([rows[:, HEAD_WIDTH:], ones], axis=1)
    for c in range(0, seq_len, chunk):
        normalized = rms_scale(
            tokens_ref[c : c + chunk, :].astype(jnp.float32), gain_ref[...]
        ).astype(jnp.bfloat16)
        projected = jnp.dot(normalized, weight_ref[...], preferred_element_type=jnp.float32)
        plain = projected[:, :256]
        partner = jnp.where(
            lane % HEAD_WIDTH < HEAD_WIDTH // 2,
            pltpu.roll(plain, 256 - HEAD_WIDTH // 2, 1),
            pltpu.roll(plain, HEAD_WIDTH // 2, 1),
        )
        cosine = cosine_ref[c : c + chunk, :]
        sine = sine_ref[c : c + chunk, :]
        rotated = plain * jnp.concatenate([cosine, cosine], axis=1) + partner * jnp.concatenate(
            [sine, sine], axis=1
        )
        rounded = rotated.astype(jnp.bfloat16)
        for h in range(heads):
            queries[h, c : c + chunk, :] = (
                rounded[:, h * HEAD_WIDTH : (h + 1) * HEAD_WIDTH] * HEAD_WIDTH ** (-0.5)
            ).astype(jnp.bfloat16)
        keys[:, prefix + c : prefix + c + chunk] = (
            rotated.T[heads * HEAD_WIDTH :].astype(jnp.bfloat16)
        )
        values[prefix + c : prefix + c + chunk, :] = jnp.concatenate(
            [projected[:, 256 : 256 + HEAD_WIDTH].astype(jnp.bfloat16), ones], axis=1
        )
    block = out_ref.shape[1]
    length = length_ref[0]
    column = lax.broadcasted_iota(jnp.int32, (block, seq_len), 1)
    row = lax.broadcasted_iota(jnp.int32, (block, seq_len), 0)

    def one_block(i, carry):
        start = pl.multiple_of(i * block, block)
        allowed = (column <= row + start) & (column < length)
        outs = []
        for h in range(heads):
            query = queries[h, pl.ds(start, block), :]
            cached = jnp.dot(query, keys[:, :prefix], preferred_element_type=jnp.float32)
            own = jnp.dot(query, keys[:, prefix:], preferred_element_type=jnp.float32)
            own = jnp.where(allowed, own, -1e30)
            top = jnp.maximum(
                jnp.max(cached, axis=1, keepdims=True), jnp.max(own, axis=1, keepdims=True)
            )
            total = jnp.dot(
                jnp.exp(cached - top).astype(jnp.bfloat16),
                values[:prefix, :],
                preferred_element_type=jnp.float32,
            ) + jnp.dot(
                jnp.exp(own - top).astype(jnp.bfloat16),
                values[prefix:, :],
                preferred_element_type=jnp.float32,
            )
            outs.append(total[:, :HEAD_WIDTH] / total[:, HEAD_WIDTH : HEAD_WIDTH + 1])
        out_ref[i] = jnp.concatenate(outs, axis=1).astype(jnp.bfloat16)
        return carry

    lax.fori_loop(0, out_ref.shape[0], one_block, 0)


def attention(lengths, tokens, gain, weight, pages, cosine, sine, blocks):
    seq_len, model_width = tokens.shape
    heads = 3
    total = seq_len + pages.shape[0]
    vmem = pl.BlockSpec(memory_space=pltpu.VMEM)
    return pl.pallas_call(
        attention_body,
        out_shape=jax.ShapeDtypeStruct((blocks, seq_len // blocks, heads * HEAD_WIDTH), jnp.bfloat16),
        in_specs=[pl.BlockSpec(memory_space=pltpu.SMEM)] + [vmem] * 6,
        out_specs=vmem,
        scratch_shapes=[
            pltpu.VMEM((heads, seq_len, HEAD_WIDTH), jnp.bfloat16),
            pltpu.VMEM((HEAD_WIDTH, total), jnp.bfloat16),
            pltpu.VMEM((total, 2 * HEAD_WIDTH), jnp.bfloat16),
        ],
        compiler_params=pltpu.CompilerParams(vmem_limit_bytes=40 << 20),
        cost_estimate=pl.CostEstimate(
            flops=30_000_000_000, bytes_accessed=8 << 20, transcendentals=heads * seq_len * total
        ),
        name="attention",
    )(lengths, tokens, gain.reshape(1, model_width), weight, pages, cosine, sine)


def project_body(
    parts_ref, weight_hbm, rows_ref, gain_ref, router_ref, ids_ref,
    hidden_ref, send_ref, rank_ref, gates_ref,
    weight, attended, place, sem,
):
    copies = []
    for z in range(8):
        for y in range(2):
            copy = pltpu.make_async_copy(
                weight_hbm.at[z, y], weight.at[pl.ds((y * 8 + z) * 96, 96)], sem.at[z * 2 + y]
            )
            copy.start()
            copies.append(copy)
    for t in range(8):
        attended[:, t * 192 : (t + 1) * 192] = parts_ref[t]
    tokens = rows_ref.shape[0]
    host = lax.broadcasted_iota(jnp.int32, (EXPERTS, tokens), 0)
    expert_at = (host // 16) * 16 + (host % 8) * 2 + (host // 8) % 2
    chosen = jnp.zeros((EXPERTS, tokens), jnp.float32)
    for k in range(ids_ref.shape[0]):
        chosen = jnp.where(ids_ref[k : k + 1, :] == expert_at, 1.0, chosen)
    earlier = lax.broadcasted_iota(jnp.int32, (tokens, tokens), 0) < lax.broadcasted_iota(
        jnp.int32, (tokens, tokens), 1
    )
    rank = jnp.dot(
        chosen.astype(jnp.bfloat16),
        jnp.where(earlier, 1.0, 0.0).astype(jnp.bfloat16),
        preferred_element_type=jnp.float32,
    )
    rank = jnp.where(chosen > 0.0, rank, -1.0)
    rank_ref[...] = rank
    slot = lax.broadcasted_iota(jnp.int32, (CAPACITY, tokens), 0).astype(jnp.float32)
    for g in range(EXPERTS):
        place[g * CAPACITY : (g + 1) * CAPACITY, :] = jnp.where(
            rank[g : g + 1, :] == slot, 1.0, 0.0
        ).astype(jnp.bfloat16)
    for copy in copies:
        copy.wait()
    for c in range(0, 1536, 256):
        hidden_ref[:, c : c + 256] = rows_ref[:, c : c + 256].astype(jnp.float32) + lax.dot_general(
            attended[...],
            weight[c : c + 256, :],
            (((1,), (1,)), ((), ())),
            preferred_element_type=jnp.float32,
        )
    hidden = hidden_ref[...]
    moe_in = rms_scale(hidden, gain_ref[...]).astype(jnp.bfloat16)
    for c in range(0, EXPERTS * CAPACITY, 256):
        send_ref[c : c + 256, :] = jnp.dot(
            place[c : c + 256, :], moe_in, preferred_element_type=jnp.float32
        ).astype(jnp.bfloat16)
    logits = lax.dot_general(
        router_ref[...], moe_in, (((1,), (1,)), ((), ())), preferred_element_type=jnp.float32
    )
    top_logit = jnp.max(jnp.where(chosen > 0.0, logits, -3e38), axis=0, keepdims=True)
    raised = jnp.where(chosen > 0.0, jnp.exp(jnp.minimum(logits - top_logit, 0.0)), 0.0)
    gates_ref[...] = raised / jnp.sum(raised, axis=0, keepdims=True)


def project_and_dispatch(parts, output_weight, own_rows, moe_gain, router_hosted, ids_by_choice):
    row_count, model_width = own_rows.shape
    slots = EXPERTS * CAPACITY
    vmem = pl.BlockSpec(memory_space=pltpu.VMEM)
    return pl.pallas_call(
        project_body,
        out_shape=(
            jax.ShapeDtypeStruct((row_count, model_width), jnp.float32),
            jax.ShapeDtypeStruct((slots, model_width), jnp.bfloat16),
            jax.ShapeDtypeStruct((EXPERTS, row_count), jnp.float32),
            jax.ShapeDtypeStruct((EXPERTS, row_count), jnp.float32),
        ),
        in_specs=[vmem, pl.BlockSpec(memory_space=pltpu.HBM), vmem, vmem, vmem, vmem],
        out_specs=(vmem, vmem, vmem, vmem),
        scratch_shapes=[
            pltpu.VMEM((model_width, model_width), jnp.bfloat16),
            pltpu.VMEM((row_count, model_width), jnp.bfloat16),
            pltpu.VMEM((slots, row_count), jnp.bfloat16),
            pltpu.SemaphoreType.DMA((16,)),
        ],
        compiler_params=pltpu.CompilerParams(vmem_limit_bytes=40 << 20),
        cost_estimate=pl.CostEstimate(
            flops=4 * row_count * model_width * model_width,
            bytes_accessed=4 * model_width * model_width,
            transcendentals=0,
        ),
        name="project_and_dispatch",
    )(
        parts,
        output_weight.reshape(8, 2, 96, model_width),
        own_rows,
        moe_gain.reshape(1, model_width),
        router_hosted,
        ids_by_choice,
    )


def weigh_body(rank_ref, gates_ref, high_ref, low_ref, weigh):
    tokens = rank_ref.shape[1]
    slot = lax.broadcasted_iota(jnp.int32, (CAPACITY, tokens), 0).astype(jnp.float32)
    for g in range(EXPERTS):
        weigh[g * CAPACITY : (g + 1) * CAPACITY, :] = jnp.where(
            rank_ref[g : g + 1, :] == slot, gates_ref[g : g + 1, :], 0.0
        )
    for c in range(0, EXPERTS * CAPACITY, 128):
        by_token = weigh[c : c + 128, :].T
        high = by_token.astype(jnp.bfloat16)
        high_ref[:, c : c + 128] = high
        low_ref[:, c : c + 128] = (by_token - high.astype(jnp.float32)).astype(jnp.bfloat16)


def weighing(rank, gates):
    row_count = rank.shape[1]
    slots = EXPERTS * CAPACITY
    vmem = pl.BlockSpec(memory_space=pltpu.VMEM)
    shape = jax.ShapeDtypeStruct((row_count, slots), jnp.bfloat16)
    return pl.pallas_call(
        weigh_body,
        out_shape=(shape, shape),
        in_specs=[vmem, vmem],
        out_specs=(vmem, vmem),
        scratch_shapes=[pltpu.VMEM((slots, row_count), jnp.float32)],
        cost_estimate=pl.CostEstimate(flops=1 << 20, bytes_accessed=1 << 20, transcendentals=0),
        name="weighing",
    )(rank, gates)


def expert_body(rows_ref, gate_up_ref, down_ref, out_ref):
    gate_up = jnp.dot(rows_ref[...], gate_up_ref[...], preferred_element_type=jnp.float32)
    activated = (jax.nn.silu(gate_up[:, :FF]) * gate_up[:, FF:]).astype(jnp.bfloat16)
    out_ref[...] = jnp.dot(activated, down_ref[...], preferred_element_type=jnp.float32).astype(
        jnp.bfloat16
    )


def experts(rows, gate_up, down):
    count, model_width = rows.shape
    tile = 256
    return pl.pallas_call(
        expert_body,
        out_shape=jax.ShapeDtypeStruct((count, model_width), jnp.bfloat16),
        grid=(count // tile,),
        in_specs=[
            pl.BlockSpec((tile, model_width), lambda i: (i, 0)),
            pl.BlockSpec(gate_up.shape, lambda i: (0, 0)),
            pl.BlockSpec(down.shape, lambda i: (0, 0)),
        ],
        out_specs=pl.BlockSpec((tile, model_width), lambda i: (i, 0)),
        compiler_params=pltpu.CompilerParams(vmem_limit_bytes=40 << 20),
        cost_estimate=pl.CostEstimate(
            flops=2 * count * model_width * 3 * FF,
            bytes_accessed=4 * count * model_width + 6 * model_width * FF,
            transcendentals=count * FF,
        ),
        name="experts",
    )(rows, gate_up, down)


def combine_body(live_ref, high_ref, low_ref, returned_ref, hidden_ref, out_ref):
    mixed = jnp.dot(high_ref[...], returned_ref[...], preferred_element_type=jnp.float32) + jnp.dot(
        low_ref[...], returned_ref[...], preferred_element_type=jnp.float32
    )
    row = lax.broadcasted_iota(jnp.int32, mixed.shape, 0)
    out_ref[...] = jnp.where(row < live_ref[0], hidden_ref[...] + mixed, 0.0).astype(jnp.bfloat16)


def combine(live, high, low, returned, hidden):
    row_count, model_width = hidden.shape
    slots = returned.shape[0]
    tile = 256
    whole = pl.BlockSpec((row_count, slots), lambda i: (0, 0))
    column = pl.BlockSpec((row_count, tile), lambda i: (0, i))
    return pl.pallas_call(
        combine_body,
        out_shape=jax.ShapeDtypeStruct((row_count, model_width), jnp.bfloat16),
        grid=(model_width // tile,),
        in_specs=[
            pl.BlockSpec(memory_space=pltpu.SMEM),
            whole,
            whole,
            pl.BlockSpec((slots, tile), lambda i: (0, i)),
            column,
        ],
        out_specs=column,
        cost_estimate=pl.CostEstimate(
            flops=4 * row_count * slots * model_width,
            bytes_accessed=2 * slots * model_width + 6 * row_count * model_width,
            transcendentals=0,
        ),
        name="combine",
    )(live, high, low, returned, hidden)


def on_device(
    tokens_in,
    lengths,
    attn_gain,
    q_proj,
    k_proj,
    value_projection,
    o_proj,
    key_value_pages,
    page_table,
    moe_gain,
    router,
    expert_ids,
    gate_up_proj,
    down_proj,
):
    seq_len, model_width = tokens_in.shape
    barrier = lax.optimization_barrier
    tp_index = lax.axis_index("tp")
    row_count = seq_len // 8

    def in_plane(rows):
        return lax.all_to_all(
            rows, ("ep", "tp"), 0, 0, axis_index_groups=PLANE_GROUPS, tiled=True
        )

    output_shard = o_proj.T.astype(jnp.bfloat16)
    output_plane = in_plane(jnp.broadcast_to(output_shard[None], (EXPERTS, *output_shard.shape)))
    output_plane = (
        output_plane.reshape(4, 8, 48, 192).transpose(0, 2, 1, 3).reshape(192, model_width)
    )

    weight_shard = jnp.concatenate(
        [q_proj, k_proj, value_projection, jnp.zeros_like(k_proj)], axis=1
    ).astype(jnp.bfloat16)
    slabs = weight_shard.reshape(48, 3, 128).transpose(1, 0, 2).reshape(144, 128)
    pages = key_value_pages[page_table[:, 0, :]].reshape(2, 8, 2, 32, 128)
    payload = jnp.concatenate(
        [
            jnp.broadcast_to(slabs[None], (8, 144, 128)),
            pages.transpose(1, 0, 2, 3, 4).reshape(8, 128, 128),
        ],
        axis=1,
    )
    payload, output_plane = barrier((payload, output_plane))
    along_z = lax.all_to_all(payload, "ep", 0, 0, axis_index_groups=Z_GROUPS, tiled=True)
    output_plane, along_z = barrier((output_plane, along_z))
    output_weight = lax.all_gather(output_plane, "ep", axis_index_groups=Z_GROUPS)
    payload = jnp.concatenate(
        [
            jnp.broadcast_to(along_z[None, :, :144], (4, 8, 144, 128)),
            along_z[:, 144:].reshape(8, 4, 32, 128).transpose(1, 0, 2, 3),
        ],
        axis=2,
    )
    across = lax.all_to_all(payload, "ep", 0, 0, axis_index_groups=CHIP_PAIR_GROUPS, tiled=True)
    weight = (
        across[:, :, :144]
        .reshape(2, 2, 8, 3, 48, 128)
        .transpose(0, 2, 1, 4, 3, 5)
        .reshape(model_width, 384)
    )
    prefix = across[:, :, 144:].reshape(2, 2, 8, 32, 128).transpose(0, 2, 1, 3, 4).reshape(-1, 128)
    cosine, sine = rotary_tables(seq_len, prefix.shape[0])
    eighths = jnp.concatenate(
        [
            gate_up_proj.astype(jnp.bfloat16).reshape(8, 24, 2, 512).transpose(0, 2, 1, 3).reshape(8, 48, 512),
            down_proj.astype(jnp.bfloat16).reshape(8, 8, 3, 512).transpose(0, 2, 1, 3).reshape(8, 24, 512),
        ],
        axis=1,
    )
    eighths, weight, prefix = barrier((eighths, weight, prefix))
    by_expert = lax.all_to_all(eighths, "ep", 0, 0, axis_index_groups=Z_GROUPS, tiled=True)
    attended = attention(lengths, tokens_in, attn_gain, weight, prefix, cosine, sine, 8)
    attended, by_expert = barrier((attended, by_expert))
    attn_parts = lax.all_to_all(attended, "tp", 0, 0, tiled=True)
    attn_parts, by_expert = barrier((attn_parts, by_expert))
    hosted = lax.all_to_all(by_expert, "tp", 0, 0, tiled=True)
    own_rows = lax.dynamic_slice_in_dim(tokens_in, tp_index * row_count, row_count, 0)
    router_hosted = router.T.reshape(2, 8, 2, model_width).transpose(0, 2, 1, 3)
    hidden, send_rows, rank, gates = project_and_dispatch(
        attn_parts,
        output_weight,
        own_rows,
        moe_gain,
        router_hosted.reshape(EXPERTS, model_width),
        expert_ids.T,
    )
    send_rows, hosted = barrier((send_rows, hosted))
    planes = lax.all_gather(hosted, "ep", axis_index_groups=Z_GROUPS)
    gate_up_full = (
        planes[:, :, :48].reshape(8, 8, 2, 24, 512).transpose(1, 0, 3, 2, 4).reshape(model_width, 2 * FF)
    )
    down_full = (
        planes[:, :, 48:].reshape(8, 8, 3, 8, 512).transpose(1, 0, 3, 2, 4).reshape(FF, model_width)
    )
    received = in_plane(send_rows.reshape(EXPERTS, CAPACITY, model_width))
    high, low = weighing(rank, gates)
    expert_out = experts(received.reshape(-1, model_width), gate_up_full, down_full)
    returned = in_plane(expert_out.reshape(EXPERTS, CAPACITY, model_width))
    live = lengths - tp_index * row_count
    return combine(live, high, low, returned.reshape(-1, model_width), hidden)


def solution(mesh):
    in_specs = (
        P("ep", None),
        P("ep"),
        P(),
        P("ep", "tp"),
        P("ep", "tp"),
        P("ep", "tp"),
        P("tp", "ep"),
        P("ep", None, "tp"),
        P(None, "ep", None),
        P(),
        P(),
        P(("ep", "tp"), None),
        P("ep", "tp", None),
        P("ep", "tp", None),
    )
    out_specs = P(("ep", "tp"), None)
    return jax.shard_map(
        on_device, mesh=mesh, in_specs=in_specs, out_specs=out_specs, check_vma=False
    )
```

```python
import math

import jax
import jax.numpy as jnp
from jax import lax
from jax.experimental import pallas as pl
from jax.experimental.pallas import tpu as pltpu
from jax.sharding import PartitionSpec as P

HEAD_WIDTH = 64
FF = 512
CAPACITY = 48
EXPERTS = 32


epsilon = 1e-05

Z_GROUPS = [[y * 16 + z * 2 + c for z in range(8)] for y in range(2) for c in range(2)]
CHIP_PAIR_GROUPS = [[y * 16 + z * 2 + c for y in range(2) for c in range(2)] for z in range(8)]
PLANE_GROUPS = [
    [(y * 16 + z * 2 + c) * 8 + t for y in range(2) for c in range(2) for t in range(8)]
    for z in range(8)
]


def rms_scale(values, norm_gain):
    mean_square = jnp.mean(values * values, axis=-1, keepdims=True)
    return values * lax.rsqrt(mean_square + epsilon) * norm_gain


def rotary_tables(positions, first_position):
    lane = jnp.arange(2 * HEAD_WIDTH)
    frequency = jnp.exp(
        (lane % (HEAD_WIDTH // 2)).astype(jnp.float32) * (-2.0 * math.log(10000.0) / HEAD_WIDTH)
    )
    angles = (first_position + jnp.arange(positions)).astype(jnp.float32)[:, None] * frequency
    sign = jnp.where(lane % HEAD_WIDTH < HEAD_WIDTH // 2, -1.0, 1.0)
    return jnp.cos(angles), jnp.sin(angles) * sign


def attention_body(
    length_ref, normalized_ref, weight_ref, pages_ref, cosine_ref, sine_ref,
    out_ref, queries, keys, values,
):
    seq_len = normalized_ref.shape[0]
    prefix = pages_ref.shape[0]
    heads = queries.shape[0]
    chunk = 256
    lane = lax.broadcasted_iota(jnp.int32, (chunk, 256), 1)
    ones = jnp.ones((chunk, HEAD_WIDTH), jnp.bfloat16)
    for c in range(0, prefix, chunk):
        rows = pages_ref[c : c + chunk, :]
        keys[:, c : c + chunk] = rows.astype(jnp.float32).T[:HEAD_WIDTH].astype(jnp.bfloat16)
        values[c : c + chunk, :] = jnp.concatenate([rows[:, HEAD_WIDTH:], ones], axis=1)
    for c in range(0, seq_len, chunk):
        projected = jnp.dot(
            normalized_ref[c : c + chunk, :], weight_ref[...], preferred_element_type=jnp.float32
        )
        plain = projected[:, :256]
        partner = jnp.where(
            lane % HEAD_WIDTH < HEAD_WIDTH // 2,
            pltpu.roll(plain, 256 - HEAD_WIDTH // 2, 1),
            pltpu.roll(plain, HEAD_WIDTH // 2, 1),
        )
        cosine = cosine_ref[c : c + chunk, :]
        sine = sine_ref[c : c + chunk, :]
        rotated = plain * jnp.concatenate([cosine, cosine], axis=1) + partner * jnp.concatenate(
            [sine, sine], axis=1
        )
        rounded = rotated.astype(jnp.bfloat16)
        for h in range(heads):
            queries[h, c : c + chunk, :] = (
                rounded[:, h * HEAD_WIDTH : (h + 1) * HEAD_WIDTH] * HEAD_WIDTH ** (-0.5)
            ).astype(jnp.bfloat16)
        keys[:, prefix + c : prefix + c + chunk] = (
            rotated.T[heads * HEAD_WIDTH :].astype(jnp.bfloat16)
        )
        values[prefix + c : prefix + c + chunk, :] = jnp.concatenate(
            [projected[:, 256 : 256 + HEAD_WIDTH].astype(jnp.bfloat16), ones], axis=1
        )
    length = length_ref[0]
    for start in range(0, seq_len, chunk):
        seen = start + chunk
        column = lax.broadcasted_iota(jnp.int32, (chunk, seen), 1)
        row = lax.broadcasted_iota(jnp.int32, (chunk, seen), 0)
        allowed = (column <= row + start) & (column < length)
        outs = []
        for h in range(heads):
            query = queries[h, start:seen, :]
            cached = jnp.dot(query, keys[:, :prefix], preferred_element_type=jnp.float32)
            own = jnp.dot(query, keys[:, prefix : prefix + seen], preferred_element_type=jnp.float32)
            own = jnp.where(allowed, own, -1e30)
            top = jnp.maximum(
                jnp.max(cached, axis=1, keepdims=True), jnp.max(own, axis=1, keepdims=True)
            )
            total = jnp.dot(
                jnp.exp(cached - top).astype(jnp.bfloat16),
                values[:prefix, :],
                preferred_element_type=jnp.float32,
            ) + jnp.dot(
                jnp.exp(own - top).astype(jnp.bfloat16),
                values[prefix : prefix + seen, :],
                preferred_element_type=jnp.float32,
            )
            outs.append(total[:, :HEAD_WIDTH] / total[:, HEAD_WIDTH : HEAD_WIDTH + 1])
        out_ref[start:seen, :] = jnp.concatenate(outs, axis=1).astype(jnp.bfloat16)


def attention(lengths, normalized, weight, pages, cosine, sine):
    seq_len, model_width = normalized.shape
    heads = 3
    total = seq_len + pages.shape[0]
    vmem = pl.BlockSpec(memory_space=pltpu.VMEM)
    return pl.pallas_call(
        attention_body,
        out_shape=jax.ShapeDtypeStruct((seq_len, heads * HEAD_WIDTH), jnp.bfloat16),
        in_specs=[pl.BlockSpec(memory_space=pltpu.SMEM)] + [vmem] * 5,
        out_specs=vmem,
        scratch_shapes=[
            pltpu.VMEM((heads, seq_len, HEAD_WIDTH), jnp.bfloat16),
            pltpu.VMEM((HEAD_WIDTH, total), jnp.bfloat16),
            pltpu.VMEM((total, 2 * HEAD_WIDTH), jnp.bfloat16),
        ],
        compiler_params=pltpu.CompilerParams(vmem_limit_bytes=48 << 20),
        cost_estimate=pl.CostEstimate(
            flops=12_000_000_000, bytes_accessed=8 << 20, transcendentals=heads * seq_len * total
        ),
        name="attention",
    )(lengths, normalized, weight, pages, cosine, sine)


def project_body(
    parts_ref, weight_hbm, rows_ref, gain_ref, router_ref, ids_ref,
    hidden_ref, send_ref, rank_ref, gates_ref,
    weight, attended, place, staged, sem, out_sem,
):
    copies = []
    for z in range(8):
        for y in range(2):
            copy = pltpu.make_async_copy(
                weight_hbm.at[z, y], weight.at[pl.ds((y * 8 + z) * 96, 96)], sem.at[z * 2 + y]
            )
            copy.start()
            copies.append(copy)
    for t in range(8):
        attended[:, t * 192 : (t + 1) * 192] = parts_ref[t]
    tokens = rows_ref.shape[0]
    host = lax.broadcasted_iota(jnp.int32, (EXPERTS, tokens), 0)
    expert_at = (host // 16) * 16 + (host % 8) * 2 + (host // 8) % 2
    chosen = jnp.zeros((EXPERTS, tokens), jnp.float32)
    for k in range(ids_ref.shape[0]):
        chosen = jnp.where(ids_ref[k : k + 1, :] == expert_at, 1.0, chosen)
    earlier = lax.broadcasted_iota(jnp.int32, (tokens, tokens), 0) < lax.broadcasted_iota(
        jnp.int32, (tokens, tokens), 1
    )
    rank = jnp.dot(
        chosen.astype(jnp.bfloat16),
        jnp.where(earlier, 1.0, 0.0).astype(jnp.bfloat16),
        preferred_element_type=jnp.float32,
    )
    rank = jnp.where(chosen > 0.0, rank, -1.0)
    rank_ref[...] = rank
    slot = lax.broadcasted_iota(jnp.int32, (CAPACITY, tokens), 0).astype(jnp.float32)
    for g in range(EXPERTS):
        place[g * CAPACITY : (g + 1) * CAPACITY, :] = jnp.where(
            rank[g : g + 1, :] == slot, 1.0, 0.0
        ).astype(jnp.bfloat16)
    for copy in copies:
        copy.wait()
    for c in range(0, 1536, 256):
        hidden_ref[:, c : c + 256] = rows_ref[:, c : c + 256].astype(jnp.float32) + lax.dot_general(
            attended[...],
            weight[c : c + 256, :],
            (((1,), (1,)), ((), ())),
            preferred_element_type=jnp.float32,
        )
    hidden = hidden_ref[...]
    moe_in = rms_scale(hidden, gain_ref[...]).astype(jnp.bfloat16)
    for c in range(0, EXPERTS * CAPACITY, 256):
        staged[c : c + 256, :] = jnp.dot(
            place[c : c + 256, :], moe_in, preferred_element_type=jnp.float32
        ).astype(jnp.bfloat16)
        pltpu.make_async_copy(
            staged.at[pl.ds(c, 256)], send_ref.at[pl.ds(c, 256)], out_sem.at[c // 256]
        ).start()
    logits = lax.dot_general(
        router_ref[...], moe_in, (((1,), (1,)), ((), ())), preferred_element_type=jnp.float32
    )
    top_logit = jnp.max(jnp.where(chosen > 0.0, logits, -3e38), axis=0, keepdims=True)
    raised = jnp.where(chosen > 0.0, jnp.exp(jnp.minimum(logits - top_logit, 0.0)), 0.0)
    gates_ref[...] = raised / jnp.sum(raised, axis=0, keepdims=True)
    for c in range(0, EXPERTS * CAPACITY, 256):
        pltpu.make_async_copy(
            staged.at[pl.ds(c, 256)], send_ref.at[pl.ds(c, 256)], out_sem.at[c // 256]
        ).wait()


def project_and_dispatch(parts, output_weight, own_rows, moe_gain, router_hosted, ids_by_choice):
    row_count, model_width = own_rows.shape
    slots = EXPERTS * CAPACITY
    vmem = pl.BlockSpec(memory_space=pltpu.VMEM)
    return pl.pallas_call(
        project_body,
        out_shape=(
            jax.ShapeDtypeStruct((row_count, model_width), jnp.float32),
            pltpu.HBM((slots, model_width), jnp.bfloat16),
            jax.ShapeDtypeStruct((EXPERTS, row_count), jnp.float32),
            jax.ShapeDtypeStruct((EXPERTS, row_count), jnp.float32),
        ),
        in_specs=[vmem, pl.BlockSpec(memory_space=pltpu.HBM), vmem, vmem, vmem, vmem],
        out_specs=(vmem, pl.BlockSpec(memory_space=pltpu.HBM), vmem, vmem),
        scratch_shapes=[
            pltpu.VMEM((model_width, model_width), jnp.bfloat16),
            pltpu.VMEM((row_count, model_width), jnp.bfloat16),
            pltpu.VMEM((slots, row_count), jnp.bfloat16),
            pltpu.VMEM((slots, model_width), jnp.bfloat16),
            pltpu.SemaphoreType.DMA((16,)),
            pltpu.SemaphoreType.DMA((6,)),
        ],
        compiler_params=pltpu.CompilerParams(vmem_limit_bytes=40 << 20),
        cost_estimate=pl.CostEstimate(
            flops=4 * row_count * model_width * model_width,
            bytes_accessed=4 * model_width * model_width,
            transcendentals=0,
        ),
        name="project_and_dispatch",
    )(
        parts,
        pltpu.with_memory_space_constraint(output_weight.reshape(8, 2, 96, model_width), pltpu.HBM),
        own_rows,
        moe_gain.reshape(1, model_width),
        router_hosted,
        ids_by_choice,
    )


def weigh_body(rank_ref, gates_ref, both_ref, weigh):
    tokens = rank_ref.shape[1]
    slot = lax.broadcasted_iota(jnp.int32, (CAPACITY, tokens), 0).astype(jnp.float32)
    for g in range(EXPERTS):
        weigh[g * CAPACITY : (g + 1) * CAPACITY, :] = jnp.where(
            rank_ref[g : g + 1, :] == slot, gates_ref[g : g + 1, :], 0.0
        )
    for c in range(0, EXPERTS * CAPACITY, 128):
        by_token = weigh[c : c + 128, :].T
        high = by_token.astype(jnp.bfloat16)
        both_ref[:tokens, c : c + 128] = high
        both_ref[tokens:, c : c + 128] = (by_token - high.astype(jnp.float32)).astype(jnp.bfloat16)


def weighing(rank, gates):
    row_count = rank.shape[1]
    slots = EXPERTS * CAPACITY
    vmem = pl.BlockSpec(memory_space=pltpu.VMEM)
    return pl.pallas_call(
        weigh_body,
        out_shape=jax.ShapeDtypeStruct((2 * row_count, slots), jnp.bfloat16),
        in_specs=[vmem, vmem],
        out_specs=vmem,
        scratch_shapes=[pltpu.VMEM((slots, row_count), jnp.float32)],
        cost_estimate=pl.CostEstimate(flops=1 << 20, bytes_accessed=1 << 20, transcendentals=0),
        name="weighing",
    )(rank, gates)


def expert_body(rows_ref, gate_up_ref, down_ref, out_ref):
    gate_up = jnp.dot(rows_ref[...], gate_up_ref[...], preferred_element_type=jnp.float32)
    activated = (jax.nn.silu(gate_up[:, :FF]) * gate_up[:, FF:]).astype(jnp.bfloat16)
    out_ref[...] = jnp.dot(activated, down_ref[...], preferred_element_type=jnp.float32).astype(
        jnp.bfloat16
    )


def experts(rows, gate_up, down):
    count, model_width = rows.shape
    tile = 512
    return pl.pallas_call(
        expert_body,
        out_shape=pltpu.HBM((count, model_width), jnp.bfloat16),
        grid=(count // tile,),
        in_specs=[
            pl.BlockSpec((tile, model_width), lambda i: (i, 0)),
            pl.BlockSpec(gate_up.shape, lambda i: (0, 0)),
            pl.BlockSpec(down.shape, lambda i: (0, 0)),
        ],
        out_specs=pl.BlockSpec((tile, model_width), lambda i: (i, 0)),
        compiler_params=pltpu.CompilerParams(vmem_limit_bytes=40 << 20),
        cost_estimate=pl.CostEstimate(
            flops=2 * count * model_width * 3 * FF,
            bytes_accessed=4 * count * model_width + 6 * model_width * FF,
            transcendentals=count * FF,
        ),
        name="experts",
    )(rows, gate_up, down)


def combine_body(live_ref, both_ref, returned_ref, hidden_ref, out_ref, total):
    step = pl.program_id(0)
    tokens = hidden_ref.shape[0]

    @pl.when(step == 0)
    def _():
        total[...] = hidden_ref[...]

    mixed = jnp.dot(both_ref[...], returned_ref[...], preferred_element_type=jnp.float32)
    total[...] += mixed[:tokens] + mixed[tokens:]

    @pl.when(step == pl.num_programs(0) - 1)
    def _():
        row = lax.broadcasted_iota(jnp.int32, total.shape, 0)
        out_ref[...] = jnp.where(row < live_ref[0], total[...], 0.0).astype(jnp.bfloat16)


def combine(live, both, returned, hidden):
    row_count, model_width = hidden.shape
    slots = returned.shape[0]
    tile = slots // 2
    whole = pl.BlockSpec((row_count, model_width), lambda i: (0, 0))
    return pl.pallas_call(
        combine_body,
        out_shape=jax.ShapeDtypeStruct((row_count, model_width), jnp.bfloat16),
        grid=(slots // tile,),
        in_specs=[
            pl.BlockSpec(memory_space=pltpu.SMEM),
            pl.BlockSpec((2 * row_count, tile), lambda i: (0, i)),
            pl.BlockSpec((tile, model_width), lambda i: (i, 0)),
            whole,
        ],
        out_specs=whole,
        scratch_shapes=[pltpu.VMEM((row_count, model_width), jnp.float32)],
        compiler_params=pltpu.CompilerParams(vmem_limit_bytes=24 << 20),
        cost_estimate=pl.CostEstimate(
            flops=4 * row_count * slots * model_width,
            bytes_accessed=2 * slots * model_width + 6 * row_count * model_width,
            transcendentals=0,
        ),
        name="combine",
    )(live, both, returned, hidden)


def on_device(
    tokens_in,
    lengths,
    attn_gain,
    q_proj,
    k_proj,
    value_projection,
    o_proj,
    key_value_pages,
    page_table,
    moe_gain,
    router,
    expert_ids,
    gate_up_proj,
    down_proj,
):
    seq_len, model_width = tokens_in.shape
    barrier = lax.optimization_barrier
    tp_index = lax.axis_index("tp")
    row_count = seq_len // 8

    def in_plane(rows):
        return lax.all_to_all(
            rows, ("ep", "tp"), 0, 0, axis_index_groups=PLANE_GROUPS, tiled=True
        )

    output_shard = o_proj.T.astype(jnp.bfloat16)
    output_plane = in_plane(jnp.broadcast_to(output_shard[None], (EXPERTS, *output_shard.shape)))
    output_plane = (
        output_plane.reshape(4, 8, 48, 192).transpose(0, 2, 1, 3).reshape(192, model_width)
    )

    weight_shard = jnp.concatenate(
        [q_proj, k_proj, value_projection, jnp.zeros_like(k_proj)], axis=1
    ).astype(jnp.bfloat16)
    slabs = weight_shard.reshape(48, 3, 128).transpose(1, 0, 2).reshape(144, 128)
    pages = key_value_pages[page_table[:, 0, :]].reshape(2, 8, 2, 32, 128)
    gate_up_slabs = gate_up_proj.astype(jnp.bfloat16).reshape(8, 24, 8, 128).transpose(0, 2, 1, 3)
    down_slabs = down_proj.astype(jnp.bfloat16).reshape(8, 8, 12, 128).transpose(0, 2, 1, 3)
    payload = jnp.concatenate(
        [
            jnp.broadcast_to(slabs[None], (8, 144, 128)),
            pages.transpose(1, 0, 2, 3, 4).reshape(8, 128, 128),
            gate_up_slabs.reshape(8, 192, 128),
            down_slabs.reshape(8, 96, 128),
        ],
        axis=1,
    )
    payload, output_plane = barrier((payload, output_plane))
    along_z = lax.all_to_all(payload, "ep", 0, 0, axis_index_groups=Z_GROUPS, tiled=True)
    output_plane, along_z = barrier((output_plane, along_z))
    output_weight = lax.all_gather(output_plane, "ep", axis_index_groups=Z_GROUPS)
    payload = jnp.concatenate(
        [
            jnp.broadcast_to(along_z[None, :, :144], (4, 8, 144, 128)),
            along_z[:, 144:272].reshape(8, 4, 32, 128).transpose(1, 0, 2, 3),
        ],
        axis=2,
    )
    across = lax.all_to_all(payload, "ep", 0, 0, axis_index_groups=CHIP_PAIR_GROUPS, tiled=True)
    weight = (
        across[:, :, :144]
        .reshape(2, 2, 8, 3, 48, 128)
        .transpose(0, 2, 1, 4, 3, 5)
        .reshape(model_width, 384)
    )
    prefix = across[:, :, 144:].reshape(2, 2, 8, 32, 128).transpose(0, 2, 1, 3, 4).reshape(-1, 128)
    cosine, sine = rotary_tables(seq_len, prefix.shape[0])
    normalized = rms_scale(tokens_in.astype(jnp.float32), attn_gain).astype(jnp.bfloat16)
    by_expert, weight, prefix = barrier((along_z[:, 272:], weight, prefix))
    hosted = lax.all_to_all(by_expert, "tp", 0, 0, tiled=True)
    attended = attention(lengths, normalized, weight, prefix, cosine, sine)
    attended, hosted = barrier((attended, hosted))
    attn_parts = lax.all_to_all(
        attended.reshape(8, row_count, attended.shape[1]), "tp", 0, 0, tiled=True
    )
    planes = lax.all_gather(hosted, "ep", axis_index_groups=Z_GROUPS)
    own_rows = lax.dynamic_slice_in_dim(tokens_in, tp_index * row_count, row_count, 0)
    router_hosted = router.T.reshape(2, 8, 2, model_width).transpose(0, 2, 1, 3)
    hidden, send_rows, rank, gates = project_and_dispatch(
        attn_parts,
        output_weight,
        own_rows,
        moe_gain,
        router_hosted.reshape(EXPERTS, model_width),
        expert_ids.T,
    )
    gate_up_full = (
        planes[:, :, :192].reshape(8, 8, 8, 24, 128).transpose(1, 0, 3, 2, 4).reshape(model_width, 2 * FF)
    )
    down_full = (
        planes[:, :, 192:].reshape(8, 8, 12, 8, 128).transpose(1, 0, 3, 2, 4).reshape(FF, model_width)
    )
    received = in_plane(send_rows.reshape(EXPERTS, CAPACITY, model_width))
    both = weighing(rank, gates)
    expert_out = experts(received.reshape(-1, model_width), gate_up_full, down_full)
    returned = in_plane(expert_out.reshape(EXPERTS, CAPACITY, model_width))
    live = lengths - tp_index * row_count
    return combine(live, both, returned.reshape(-1, model_width), hidden)


def solution(mesh):
    in_specs = (
        P("ep", None),
        P("ep"),
        P(),
        P("ep", "tp"),
        P("ep", "tp"),
        P("ep", "tp"),
        P("tp", "ep"),
        P("ep", None, "tp"),
        P(None, "ep", None),
        P(),
        P(),
        P(("ep", "tp"), None),
        P("ep", "tp", None),
        P("ep", "tp", None),
    )
    out_specs = P(("ep", "tp"), None)
    return jax.shard_map(
        on_device, mesh=mesh, in_specs=in_specs, out_specs=out_specs, check_vma=False
    )
```

```python
import math

import jax
import jax.numpy as jnp
from jax import lax
from jax.experimental import pallas as pl
from jax.experimental.pallas import tpu as pltpu
from jax.sharding import PartitionSpec as P

HEAD_WIDTH = 64
FF = 512
CAPACITY = 48
EXPERTS = 32


epsilon = 1e-05

Z_GROUPS = [[y * 16 + z * 2 + c for z in range(8)] for y in range(2) for c in range(2)]
CHIP_PAIR_GROUPS = [[y * 16 + z * 2 + c for y in range(2) for c in range(2)] for z in range(8)]
PLANE_GROUPS = [
    [(y * 16 + z * 2 + c) * 8 + t for y in range(2) for c in range(2) for t in range(8)]
    for z in range(8)
]


def rms_scale(values, norm_gain):
    mean_square = jnp.mean(values * values, axis=-1, keepdims=True)
    return values * lax.rsqrt(mean_square + epsilon) * norm_gain


def rotary_table(positions, first_position):
    lane = jnp.arange(2 * HEAD_WIDTH)
    frequency = jnp.exp(
        (lane % (HEAD_WIDTH // 2)).astype(jnp.float32) * (-2.0 * math.log(10000.0) / HEAD_WIDTH)
    )
    angles = (first_position + jnp.arange(positions)).astype(jnp.float32)[:, None] * frequency
    sign = jnp.where(lane % HEAD_WIDTH < HEAD_WIDTH // 2, -1.0, 1.0)
    return jnp.where(lane < HEAD_WIDTH, jnp.cos(angles), jnp.sin(angles) * sign)


def attention_body(
    length_ref, normalized_ref, across_ref, table_ref,
    out_ref, queries, keys, values, weight,
):
    seq_len = normalized_ref.shape[0]
    heads = queries.shape[0]
    prefix = keys.shape[1] - seq_len
    chunk = 256
    lane = lax.broadcasted_iota(jnp.int32, (chunk, 256), 1)
    ones = jnp.ones((chunk, HEAD_WIDTH), jnp.bfloat16)
    for e in range(32):
        pair, z = (e // 16) * 2 + e % 2, (e // 2) % 8
        for j in range(3):
            weight[e * 48 : (e + 1) * 48, j * 128 : (j + 1) * 128] = across_ref[
                pair, z, j * 48 : (j + 1) * 48, :
            ]
    for c in range(0, prefix, chunk):
        rows = jnp.concatenate(
            [
                across_ref[(e // 16) * 2 + e % 2, (e // 2) % 8, 144:176, :]
                for e in range(c // 32, (c + chunk) // 32)
            ],
            axis=0,
        )
        keys[:, c : c + chunk] = rows.astype(jnp.float32).T[:HEAD_WIDTH].astype(jnp.bfloat16)
        values[c : c + chunk, :] = jnp.concatenate([rows[:, HEAD_WIDTH:], ones], axis=1)
    for c in range(0, seq_len, chunk):
        projected = jnp.dot(
            normalized_ref[c : c + chunk, :], weight[...], preferred_element_type=jnp.float32
        )
        plain = projected[:, :256]
        partner = jnp.where(
            lane % HEAD_WIDTH < HEAD_WIDTH // 2,
            pltpu.roll(plain, 256 - HEAD_WIDTH // 2, 1),
            pltpu.roll(plain, HEAD_WIDTH // 2, 1),
        )
        cosine = table_ref[c : c + chunk, :HEAD_WIDTH]
        sine = table_ref[c : c + chunk, HEAD_WIDTH:]
        rotated = plain * jnp.concatenate([cosine] * 4, axis=1) + partner * jnp.concatenate(
            [sine] * 4, axis=1
        )
        rounded = rotated.astype(jnp.bfloat16)
        for h in range(heads):
            queries[h, c : c + chunk, :] = (
                rounded[:, h * HEAD_WIDTH : (h + 1) * HEAD_WIDTH] * HEAD_WIDTH ** (-0.5)
            ).astype(jnp.bfloat16)
        keys[:, prefix + c : prefix + c + chunk] = (
            rotated.T[heads * HEAD_WIDTH :].astype(jnp.bfloat16)
        )
        values[prefix + c : prefix + c + chunk, :] = jnp.concatenate(
            [projected[:, 256 : 256 + HEAD_WIDTH].astype(jnp.bfloat16), ones], axis=1
        )
    length = length_ref[0]
    for start in range(0, seq_len, chunk):
        seen = start + chunk
        column = lax.broadcasted_iota(jnp.int32, (chunk, seen), 1)
        row = lax.broadcasted_iota(jnp.int32, (chunk, seen), 0)
        allowed = (column <= row + start) & (column < length)
        outs = []
        for h in range(heads):
            query = queries[h, start:seen, :]
            cached = jnp.dot(query, keys[:, :prefix], preferred_element_type=jnp.float32)
            own = jnp.dot(query, keys[:, prefix : prefix + seen], preferred_element_type=jnp.float32)
            own = jnp.where(allowed, own, -1e30)
            top = jnp.maximum(
                jnp.max(cached, axis=1, keepdims=True), jnp.max(own, axis=1, keepdims=True)
            )
            total = jnp.dot(
                jnp.exp(cached - top).astype(jnp.bfloat16),
                values[:prefix, :],
                preferred_element_type=jnp.float32,
            ) + jnp.dot(
                jnp.exp(own - top).astype(jnp.bfloat16),
                values[prefix : prefix + seen, :],
                preferred_element_type=jnp.float32,
            )
            outs.append(total[:, :HEAD_WIDTH] / total[:, HEAD_WIDTH : HEAD_WIDTH + 1])
        for t in range(0, chunk, 128):
            block = (start + t) // 128
            low, high = outs[2][t : t + 64], outs[2][t + 64 : t + 128]
            out_ref[block, :128, :] = jnp.concatenate(
                [outs[0][t : t + 128], outs[1][t : t + 128]], axis=1
            ).astype(jnp.bfloat16)
            out_ref[block, 128:, :] = jnp.concatenate([low, high], axis=1).astype(jnp.bfloat16)


def attention(lengths, normalized, across, table):
    seq_len, model_width = normalized.shape
    heads = 3
    total = 2 * seq_len
    vmem = pl.BlockSpec(memory_space=pltpu.VMEM)
    return pl.pallas_call(
        attention_body,
        out_shape=pltpu.HBM((seq_len // 128, 192, 128), jnp.bfloat16),
        in_specs=[pl.BlockSpec(memory_space=pltpu.SMEM)] + [vmem] * 3,
        out_specs=vmem,
        scratch_shapes=[
            pltpu.VMEM((heads, seq_len, HEAD_WIDTH), jnp.bfloat16),
            pltpu.VMEM((HEAD_WIDTH, total), jnp.bfloat16),
            pltpu.VMEM((total, 2 * HEAD_WIDTH), jnp.bfloat16),
            pltpu.VMEM((model_width, 384), jnp.bfloat16),
        ],
        compiler_params=pltpu.CompilerParams(vmem_limit_bytes=48 << 20),
        cost_estimate=pl.CostEstimate(
            flops=12_000_000_000, bytes_accessed=8 << 20, transcendentals=heads * seq_len * total
        ),
        name="attention",
    )(lengths, normalized, across, table)


def relay_body(along_ref, payload_ref, expert_ref, sem):
    copies = [pltpu.make_async_copy(along_ref.at[:, 272:], expert_ref, sem.at[8])]
    for d in range(4):
        copies.append(
            pltpu.make_async_copy(
                along_ref.at[:, :144], payload_ref.at[d, :, pl.ds(0, 144)], sem.at[2 * d]
            )
        )
        copies.append(
            pltpu.make_async_copy(
                along_ref.at[:, pl.ds(144 + 32 * d, 32)],
                payload_ref.at[d, :, pl.ds(144, 32)],
                sem.at[2 * d + 1],
            )
        )
    for copy in copies:
        copy.start()
    for copy in copies:
        copy.wait()


def relay(along_z):
    hbm = pl.BlockSpec(memory_space=pltpu.HBM)
    return pl.pallas_call(
        relay_body,
        out_shape=(
            pltpu.HBM((4, 8, 176, 128), jnp.bfloat16),
            pltpu.HBM((8, 288, 128), jnp.bfloat16),
        ),
        in_specs=[hbm],
        out_specs=(hbm, hbm),
        scratch_shapes=[pltpu.SemaphoreType.DMA((9,))],
        cost_estimate=pl.CostEstimate(flops=0, bytes_accessed=4 << 20, transcendentals=0),
        name="relay",
    )(pltpu.with_memory_space_constraint(along_z, pltpu.HBM))


def project_body(
    parts_ref, weight_hbm, rows_ref, gain_ref, router_ref, ids_ref,
    hidden_out, send_ref, rank_gates_out,
    weight, attended, place, staged, hidden_ref, rank_gates, sem, out_sem,
):
    copies = []
    for z in range(8):
        for y in range(2):
            copy = pltpu.make_async_copy(
                weight_hbm.at[z, y], weight.at[pl.ds((y * 8 + z) * 96, 96)], sem.at[z * 2 + y]
            )
            copy.start()
            copies.append(copy)
    for t in range(8):
        at = t * 192
        attended[:, at : at + 128] = parts_ref[t, :128, :]
        attended[:64, at + 128 : at + 192] = parts_ref[t, 128:, :64]
        attended[64:, at + 128 : at + 192] = parts_ref[t, 128:, 64:]
    tokens = rows_ref.shape[0]
    host = lax.broadcasted_iota(jnp.int32, (EXPERTS, tokens), 0)
    expert_at = (host // 16) * 16 + (host % 8) * 2 + (host // 8) % 2
    chosen = jnp.zeros((EXPERTS, tokens), jnp.float32)
    for k in range(ids_ref.shape[0]):
        chosen = jnp.where(ids_ref[k : k + 1, :] == expert_at, 1.0, chosen)
    earlier = lax.broadcasted_iota(jnp.int32, (tokens, tokens), 0) < lax.broadcasted_iota(
        jnp.int32, (tokens, tokens), 1
    )
    rank = jnp.dot(
        chosen.astype(jnp.bfloat16),
        jnp.where(earlier, 1.0, 0.0).astype(jnp.bfloat16),
        preferred_element_type=jnp.float32,
    )
    rank = jnp.where(chosen > 0.0, rank, -1.0)
    rank_gates[:EXPERTS, :] = rank
    slot = lax.broadcasted_iota(jnp.int32, (CAPACITY, tokens), 0).astype(jnp.float32)
    for g in range(EXPERTS):
        place[g * CAPACITY : (g + 1) * CAPACITY, :] = jnp.where(
            rank[g : g + 1, :] == slot, 1.0, 0.0
        ).astype(jnp.bfloat16)
    for copy in copies:
        copy.wait()
    for c in range(0, 1536, 256):
        hidden_ref[:, c : c + 256] = rows_ref[:, c : c + 256].astype(jnp.float32) + lax.dot_general(
            attended[...],
            weight[c : c + 256, :],
            (((1,), (1,)), ((), ())),
            preferred_element_type=jnp.float32,
        )
    keep = pltpu.make_async_copy(hidden_ref, hidden_out, out_sem.at[6])
    keep.start()
    hidden = hidden_ref[...]
    moe_in = rms_scale(hidden, gain_ref[...]).astype(jnp.bfloat16)
    for c in range(0, EXPERTS * CAPACITY, 256):
        staged[c : c + 256, :] = jnp.dot(
            place[c : c + 256, :], moe_in, preferred_element_type=jnp.float32
        ).astype(jnp.bfloat16)
        pltpu.make_async_copy(
            staged.at[pl.ds(c, 256)], send_ref.at[pl.ds(c, 256)], out_sem.at[c // 256]
        ).start()
    logits = lax.dot_general(
        router_ref[...], moe_in, (((1,), (1,)), ((), ())), preferred_element_type=jnp.float32
    )
    top_logit = jnp.max(jnp.where(chosen > 0.0, logits, -3e38), axis=0, keepdims=True)
    raised = jnp.where(chosen > 0.0, jnp.exp(jnp.minimum(logits - top_logit, 0.0)), 0.0)
    rank_gates[EXPERTS:, :] = raised / jnp.sum(raised, axis=0, keepdims=True)
    last = pltpu.make_async_copy(rank_gates, rank_gates_out, out_sem.at[7])
    last.start()
    for c in range(0, EXPERTS * CAPACITY, 256):
        pltpu.make_async_copy(
            staged.at[pl.ds(c, 256)], send_ref.at[pl.ds(c, 256)], out_sem.at[c // 256]
        ).wait()
    keep.wait()
    last.wait()


def project_and_dispatch(parts, output_weight, own_rows, moe_gain, router_hosted, ids_by_choice):
    row_count, model_width = own_rows.shape
    slots = EXPERTS * CAPACITY
    vmem = pl.BlockSpec(memory_space=pltpu.VMEM)
    return pl.pallas_call(
        project_body,
        out_shape=(
            pltpu.HBM((row_count, model_width), jnp.float32),
            pltpu.HBM((slots, model_width), jnp.bfloat16),
            pltpu.HBM((2 * EXPERTS, row_count), jnp.float32),
        ),
        in_specs=[vmem, pl.BlockSpec(memory_space=pltpu.HBM), vmem, vmem, vmem, vmem],
        out_specs=(pl.BlockSpec(memory_space=pltpu.HBM),) * 3,
        scratch_shapes=[
            pltpu.VMEM((model_width, model_width), jnp.bfloat16),
            pltpu.VMEM((row_count, model_width), jnp.bfloat16),
            pltpu.VMEM((slots, row_count), jnp.bfloat16),
            pltpu.VMEM((slots, model_width), jnp.bfloat16),
            pltpu.VMEM((row_count, model_width), jnp.float32),
            pltpu.VMEM((2 * EXPERTS, row_count), jnp.float32),
            pltpu.SemaphoreType.DMA((16,)),
            pltpu.SemaphoreType.DMA((8,)),
        ],
        compiler_params=pltpu.CompilerParams(vmem_limit_bytes=40 << 20),
        cost_estimate=pl.CostEstimate(
            flops=4 * row_count * model_width * model_width,
            bytes_accessed=4 * model_width * model_width,
            transcendentals=0,
        ),
        name="project_and_dispatch",
    )(
        parts,
        pltpu.with_memory_space_constraint(output_weight.reshape(8, 2, 96, model_width), pltpu.HBM),
        own_rows,
        moe_gain.reshape(1, model_width),
        router_hosted,
        ids_by_choice,
    )


def weigh_body(rank_gates_ref, both_ref, weigh):
    tokens = rank_gates_ref.shape[1]
    slot = lax.broadcasted_iota(jnp.int32, (CAPACITY, tokens), 0).astype(jnp.float32)
    for g in range(EXPERTS):
        weigh[g * CAPACITY : (g + 1) * CAPACITY, :] = jnp.where(
            rank_gates_ref[g : g + 1, :] == slot,
            rank_gates_ref[EXPERTS + g : EXPERTS + g + 1, :],
            0.0,
        )
    for c in range(0, EXPERTS * CAPACITY, 128):
        by_token = weigh[c : c + 128, :].T
        high = by_token.astype(jnp.bfloat16)
        both_ref[:tokens, c : c + 128] = high
        both_ref[tokens:, c : c + 128] = (by_token - high.astype(jnp.float32)).astype(jnp.bfloat16)


def weighing(rank_gates):
    row_count = rank_gates.shape[1]
    slots = EXPERTS * CAPACITY
    vmem = pl.BlockSpec(memory_space=pltpu.VMEM)
    return pl.pallas_call(
        weigh_body,
        out_shape=jax.ShapeDtypeStruct((2 * row_count, slots), jnp.bfloat16),
        in_specs=[vmem],
        out_specs=vmem,
        scratch_shapes=[pltpu.VMEM((slots, row_count), jnp.float32)],
        cost_estimate=pl.CostEstimate(flops=1 << 20, bytes_accessed=1 << 20, transcendentals=0),
        name="weighing",
    )(rank_gates)


def expert_body(rows_ref, gate_up_ref, down_ref, out_ref):
    gate_up = jnp.dot(rows_ref[...], gate_up_ref[...], preferred_element_type=jnp.float32)
    activated = (jax.nn.silu(gate_up[:, :FF]) * gate_up[:, FF:]).astype(jnp.bfloat16)
    out_ref[...] = jnp.dot(activated, down_ref[...], preferred_element_type=jnp.float32).astype(
        jnp.bfloat16
    )


def experts(rows, gate_up, down):
    count, model_width = rows.shape
    tile = 512
    return pl.pallas_call(
        expert_body,
        out_shape=pltpu.HBM((count, model_width), jnp.bfloat16),
        grid=(count // tile,),
        in_specs=[
            pl.BlockSpec((tile, model_width), lambda i: (i, 0)),
            pl.BlockSpec(gate_up.shape, lambda i: (0, 0)),
            pl.BlockSpec(down.shape, lambda i: (0, 0)),
        ],
        out_specs=pl.BlockSpec((tile, model_width), lambda i: (i, 0)),
        compiler_params=pltpu.CompilerParams(vmem_limit_bytes=40 << 20),
        cost_estimate=pl.CostEstimate(
            flops=2 * count * model_width * 3 * FF,
            bytes_accessed=4 * count * model_width + 6 * model_width * FF,
            transcendentals=count * FF,
        ),
        name="experts",
    )(rows, gate_up, down)


def combine_body(live_ref, both_ref, returned_ref, hidden_ref, out_ref, total):
    step = pl.program_id(0)
    tokens = hidden_ref.shape[0]

    @pl.when(step == 0)
    def _():
        total[...] = hidden_ref[...]

    mixed = jnp.dot(both_ref[...], returned_ref[...], preferred_element_type=jnp.float32)
    total[...] += mixed[:tokens] + mixed[tokens:]

    @pl.when(step == pl.num_programs(0) - 1)
    def _():
        row = lax.broadcasted_iota(jnp.int32, total.shape, 0)
        out_ref[...] = jnp.where(row < live_ref[0], total[...], 0.0).astype(jnp.bfloat16)


def combine(live, both, returned, hidden):
    row_count, model_width = hidden.shape
    slots = returned.shape[0]
    tile = slots // 2
    whole = pl.BlockSpec((row_count, model_width), lambda i: (0, 0))
    return pl.pallas_call(
        combine_body,
        out_shape=jax.ShapeDtypeStruct((row_count, model_width), jnp.bfloat16),
        grid=(slots // tile,),
        in_specs=[
            pl.BlockSpec(memory_space=pltpu.SMEM),
            pl.BlockSpec((2 * row_count, tile), lambda i: (0, i)),
            pl.BlockSpec((tile, model_width), lambda i: (i, 0)),
            whole,
        ],
        out_specs=whole,
        scratch_shapes=[pltpu.VMEM((row_count, model_width), jnp.float32)],
        compiler_params=pltpu.CompilerParams(vmem_limit_bytes=24 << 20),
        cost_estimate=pl.CostEstimate(
            flops=4 * row_count * slots * model_width,
            bytes_accessed=2 * slots * model_width + 6 * row_count * model_width,
            transcendentals=0,
        ),
        name="combine",
    )(live, both, returned, hidden)


def on_device(
    tokens_in,
    lengths,
    attn_gain,
    q_proj,
    k_proj,
    value_projection,
    o_proj,
    key_value_pages,
    page_table,
    moe_gain,
    router,
    expert_ids,
    gate_up_proj,
    down_proj,
):
    seq_len, model_width = tokens_in.shape
    barrier = lax.optimization_barrier
    tp_index = lax.axis_index("tp")
    row_count = seq_len // 8

    def in_plane(rows):
        return lax.all_to_all(
            rows, ("ep", "tp"), 0, 0, axis_index_groups=PLANE_GROUPS, tiled=True
        )

    output_shard = o_proj.T.astype(jnp.bfloat16)
    output_plane = in_plane(jnp.broadcast_to(output_shard[None], (EXPERTS, *output_shard.shape)))

    weight_shard = jnp.concatenate(
        [q_proj, k_proj, value_projection, jnp.zeros_like(k_proj)], axis=1
    ).astype(jnp.bfloat16)
    slabs = weight_shard.reshape(48, 3, 128).transpose(1, 0, 2).reshape(144, 128)
    pages = key_value_pages[page_table[:, 0, :]].reshape(2, 8, 2, 32, 128)
    gate_up_slabs = gate_up_proj.astype(jnp.bfloat16).reshape(8, 24, 8, 128).transpose(0, 2, 1, 3)
    down_slabs = down_proj.astype(jnp.bfloat16).reshape(8, 8, 12, 128).transpose(0, 2, 1, 3)
    payload = jnp.concatenate(
        [
            jnp.broadcast_to(slabs[None], (8, 144, 128)),
            pages.transpose(1, 0, 2, 3, 4).reshape(8, 128, 128),
            gate_up_slabs.reshape(8, 192, 128),
            down_slabs.reshape(8, 96, 128),
        ],
        axis=1,
    )
    normalized = rms_scale(tokens_in.astype(jnp.float32), attn_gain).astype(jnp.bfloat16)
    payload, output_plane, normalized = barrier((payload, output_plane, normalized))
    along_z = lax.all_to_all(payload, "ep", 0, 0, axis_index_groups=Z_GROUPS, tiled=True)
    output_plane = (
        output_plane.reshape(4, 8, 48, 192).transpose(0, 2, 1, 3).reshape(192, model_width)
    )
    output_plane, along_z = barrier((output_plane, along_z))
    output_weight = lax.all_gather(output_plane, "ep", axis_index_groups=Z_GROUPS)
    payload, by_expert = relay(along_z)
    across = lax.all_to_all(payload, "ep", 0, 0, axis_index_groups=CHIP_PAIR_GROUPS, tiled=True)
    table = rotary_table(seq_len, 32 * 32)
    by_expert, across = barrier((by_expert, across))
    hosted = lax.all_to_all(by_expert, "tp", 0, 0, tiled=True)
    attended = attention(lengths, normalized, across, table)
    attended, hosted = barrier((attended, hosted))
    attn_parts = lax.all_to_all(attended, "tp", 0, 0, tiled=True)
    planes = lax.all_gather(hosted, "ep", axis_index_groups=Z_GROUPS)
    own_rows = lax.dynamic_slice_in_dim(tokens_in, tp_index * row_count, row_count, 0)
    router_hosted = router.T.reshape(2, 8, 2, model_width).transpose(0, 2, 1, 3)
    hidden, send_rows, rank_gates = project_and_dispatch(
        attn_parts,
        output_weight,
        own_rows,
        moe_gain,
        router_hosted.reshape(EXPERTS, model_width),
        expert_ids.T,
    )
    gate_up_full = (
        planes[:, :, :192].reshape(8, 8, 8, 24, 128).transpose(1, 0, 3, 2, 4).reshape(model_width, 2 * FF)
    )
    down_full = (
        planes[:, :, 192:].reshape(8, 8, 12, 8, 128).transpose(1, 0, 3, 2, 4).reshape(FF, model_width)
    )
    received = in_plane(send_rows.reshape(EXPERTS, CAPACITY, model_width))
    both = weighing(rank_gates)
    expert_out = experts(received.reshape(-1, model_width), gate_up_full, down_full)
    returned = in_plane(expert_out.reshape(EXPERTS, CAPACITY, model_width))
    live = lengths - tp_index * row_count
    return combine(live, both, returned.reshape(-1, model_width), hidden)


def solution(mesh):
    in_specs = (
        P("ep", None),
        P("ep"),
        P(),
        P("ep", "tp"),
        P("ep", "tp"),
        P("ep", "tp"),
        P("tp", "ep"),
        P("ep", None, "tp"),
        P(None, "ep", None),
        P(),
        P(),
        P(("ep", "tp"), None),
        P("ep", "tp", None),
        P("ep", "tp", None),
    )
    out_specs = P(("ep", "tp"), None)
    return jax.shard_map(
        on_device, mesh=mesh, in_specs=in_specs, out_specs=out_specs, check_vma=False
    )
```

```python
import math

import jax
import jax.numpy as jnp
from jax import lax
from jax.experimental import pallas as pl
from jax.experimental.pallas import tpu as pltpu
from jax.sharding import PartitionSpec as P

HEAD_WIDTH = 64
FF = 512
CAPACITY = 48
EXPERTS = 32


epsilon = 1e-05

Z_GROUPS = [[y * 16 + z * 2 + c for z in range(8)] for y in range(2) for c in range(2)]
CHIP_PAIR_GROUPS = [[y * 16 + z * 2 + c for y in range(2) for c in range(2)] for z in range(8)]
PLANE_GROUPS = [
    [(y * 16 + z * 2 + c) * 8 + t for y in range(2) for c in range(2) for t in range(8)]
    for z in range(8)
]


def rms_scale(values, norm_gain):
    mean_square = jnp.mean(values * values, axis=-1, keepdims=True)
    return values * lax.rsqrt(mean_square + epsilon) * norm_gain


def rotary_table(positions, first_position):
    lane = jnp.arange(2 * HEAD_WIDTH)
    frequency = jnp.exp(
        (lane % (HEAD_WIDTH // 2)).astype(jnp.float32) * (-2.0 * math.log(10000.0) / HEAD_WIDTH)
    )
    angles = (first_position + jnp.arange(positions)).astype(jnp.float32)[:, None] * frequency
    sign = jnp.where(lane % HEAD_WIDTH < HEAD_WIDTH // 2, -1.0, 1.0)
    return jnp.where(lane < HEAD_WIDTH, jnp.cos(angles), jnp.sin(angles) * sign)


def attention_body(
    length_ref, normalized_ref, across_ref, table_ref,
    out_ref, queries, keys, values, weight,
):
    seq_len = normalized_ref.shape[0]
    heads = queries.shape[0]
    prefix = keys.shape[1] - seq_len
    chunk = 256
    lane = lax.broadcasted_iota(jnp.int32, (chunk, 256), 1)
    ones = jnp.ones((chunk, HEAD_WIDTH), jnp.bfloat16)
    for e in range(32):
        pair, z = (e // 16) * 2 + e % 2, (e // 2) % 8
        for j in range(3):
            weight[e * 48 : (e + 1) * 48, j * 128 : (j + 1) * 128] = across_ref[
                pair, z, j * 48 : (j + 1) * 48, :
            ]
    for c in range(0, prefix, chunk):
        rows = jnp.concatenate(
            [
                across_ref[(e // 16) * 2 + e % 2, (e // 2) % 8, 144:176, :]
                for e in range(c // 32, (c + chunk) // 32)
            ],
            axis=0,
        )
        keys[:, c : c + chunk] = rows.astype(jnp.float32).T[:HEAD_WIDTH].astype(jnp.bfloat16)
        values[c : c + chunk, :] = jnp.concatenate([rows[:, HEAD_WIDTH:], ones], axis=1)
    for c in range(0, seq_len, chunk):
        projected = jnp.dot(
            normalized_ref[c : c + chunk, :], weight[...], preferred_element_type=jnp.float32
        )
        plain = projected[:, :256]
        partner = jnp.where(
            lane % HEAD_WIDTH < HEAD_WIDTH // 2,
            pltpu.roll(plain, 256 - HEAD_WIDTH // 2, 1),
            pltpu.roll(plain, HEAD_WIDTH // 2, 1),
        )
        cosine = table_ref[c : c + chunk, :HEAD_WIDTH]
        sine = table_ref[c : c + chunk, HEAD_WIDTH:]
        rotated = plain * jnp.concatenate([cosine] * 4, axis=1) + partner * jnp.concatenate(
            [sine] * 4, axis=1
        )
        rounded = rotated.astype(jnp.bfloat16)
        for h in range(heads):
            queries[h, c : c + chunk, :] = (
                rounded[:, h * HEAD_WIDTH : (h + 1) * HEAD_WIDTH] * HEAD_WIDTH ** (-0.5)
            ).astype(jnp.bfloat16)
        keys[:, prefix + c : prefix + c + chunk] = (
            rotated.T[heads * HEAD_WIDTH :].astype(jnp.bfloat16)
        )
        values[prefix + c : prefix + c + chunk, :] = jnp.concatenate(
            [projected[:, 256 : 256 + HEAD_WIDTH].astype(jnp.bfloat16), ones], axis=1
        )
    length = length_ref[0]
    for start in range(0, seq_len, chunk):
        seen = start + chunk
        column = lax.broadcasted_iota(jnp.int32, (chunk, seen), 1)
        row = lax.broadcasted_iota(jnp.int32, (chunk, seen), 0)
        allowed = (column <= row + start) & (column < length)
        outs = []
        for h in range(heads):
            query = queries[h, start:seen, :]
            cached = jnp.dot(query, keys[:, :prefix], preferred_element_type=jnp.float32)
            own = jnp.dot(query, keys[:, prefix : prefix + seen], preferred_element_type=jnp.float32)
            own = jnp.where(allowed, own, -1e30)
            top = jnp.maximum(
                jnp.max(cached, axis=1, keepdims=True), jnp.max(own, axis=1, keepdims=True)
            )
            total = jnp.dot(
                jnp.exp(cached - top).astype(jnp.bfloat16),
                values[:prefix, :],
                preferred_element_type=jnp.float32,
            ) + jnp.dot(
                jnp.exp(own - top).astype(jnp.bfloat16),
                values[prefix : prefix + seen, :],
                preferred_element_type=jnp.float32,
            )
            outs.append(total[:, :HEAD_WIDTH] / total[:, HEAD_WIDTH : HEAD_WIDTH + 1])
        for t in range(0, chunk, 128):
            block = (start + t) // 128
            low, high = outs[2][t : t + 64], outs[2][t + 64 : t + 128]
            out_ref[block, :128, :] = jnp.concatenate(
                [outs[0][t : t + 128], outs[1][t : t + 128]], axis=1
            ).astype(jnp.bfloat16)
            out_ref[block, 128:, :] = jnp.concatenate([low, high], axis=1).astype(jnp.bfloat16)


def attention(lengths, normalized, across, table):
    seq_len, model_width = normalized.shape
    heads = 3
    total = 2 * seq_len
    vmem = pl.BlockSpec(memory_space=pltpu.VMEM)
    return pl.pallas_call(
        attention_body,
        out_shape=pltpu.HBM((seq_len // 128, 192, 128), jnp.bfloat16),
        in_specs=[pl.BlockSpec(memory_space=pltpu.SMEM)] + [vmem] * 3,
        out_specs=vmem,
        scratch_shapes=[
            pltpu.VMEM((heads, seq_len, HEAD_WIDTH), jnp.bfloat16),
            pltpu.VMEM((HEAD_WIDTH, total), jnp.bfloat16),
            pltpu.VMEM((total, 2 * HEAD_WIDTH), jnp.bfloat16),
            pltpu.VMEM((model_width, 384), jnp.bfloat16),
        ],
        compiler_params=pltpu.CompilerParams(vmem_limit_bytes=48 << 20),
        cost_estimate=pl.CostEstimate(
            flops=12_000_000_000, bytes_accessed=8 << 20, transcendentals=heads * seq_len * total
        ),
        name="attention",
    )(lengths, normalized, across, table)


def relay_body(along_ref, payload_ref, expert_ref, held, sem):
    loads = [pltpu.make_async_copy(along_ref.at[z], held.at[z], sem.at[z]) for z in range(8)]
    for load in loads:
        load.start()
    for load in loads:
        load.wait()
    copies = []
    for d in range(4):
        copies.append(
            pltpu.make_async_copy(
                held.at[:, pl.ds(0, 144)], payload_ref.at[d, :, pl.ds(0, 144)], sem.at[2 * d]
            )
        )
        copies.append(
            pltpu.make_async_copy(
                held.at[:, pl.ds(144 + 32 * d, 32)],
                payload_ref.at[d, :, pl.ds(144, 32)],
                sem.at[2 * d + 1],
            )
        )
    copies.append(pltpu.make_async_copy(held.at[:, pl.ds(272, 288)], expert_ref, sem.at[8]))
    for copy in copies:
        copy.start()
    for copy in copies:
        copy.wait()


def relay(along_z):
    hbm = pl.BlockSpec(memory_space=pltpu.HBM)
    return pl.pallas_call(
        relay_body,
        out_shape=(
            pltpu.HBM((4, 8, 176, 128), jnp.bfloat16),
            pltpu.HBM((8, 288, 128), jnp.bfloat16),
        ),
        in_specs=[hbm],
        out_specs=(hbm, hbm),
        scratch_shapes=[pltpu.VMEM(along_z.shape, jnp.bfloat16), pltpu.SemaphoreType.DMA((9,))],
        cost_estimate=pl.CostEstimate(flops=0, bytes_accessed=4 << 20, transcendentals=0),
        name="relay",
    )(pltpu.with_memory_space_constraint(along_z, pltpu.HBM))


def project_body(
    parts_ref, weight_hbm, rows_ref, gain_ref, router_ref, ids_ref,
    hidden_out, send_ref, rank_gates_out,
    weight, attended, place, staged, hidden_ref, rank_gates, sem, out_sem,
):
    copies = []
    for y in range(2):
        for z in range(8):
            copy = pltpu.make_async_copy(
                weight_hbm.at[z, y], weight.at[pl.ds((y * 8 + z) * 96, 96)], sem.at[y * 8 + z]
            )
            copy.start()
            copies.append(copy)
    for t in range(8):
        at = t * 192
        attended[:, at : at + 128] = parts_ref[t, :128, :]
        attended[:64, at + 128 : at + 192] = parts_ref[t, 128:, :64]
        attended[64:, at + 128 : at + 192] = parts_ref[t, 128:, 64:]
    tokens = rows_ref.shape[0]
    host = lax.broadcasted_iota(jnp.int32, (EXPERTS, tokens), 0)
    expert_at = (host // 16) * 16 + (host % 8) * 2 + (host // 8) % 2
    chosen = jnp.zeros((EXPERTS, tokens), jnp.float32)
    for k in range(ids_ref.shape[0]):
        chosen = jnp.where(ids_ref[k : k + 1, :] == expert_at, 1.0, chosen)
    earlier = lax.broadcasted_iota(jnp.int32, (tokens, tokens), 0) < lax.broadcasted_iota(
        jnp.int32, (tokens, tokens), 1
    )
    rank = jnp.dot(
        chosen.astype(jnp.bfloat16),
        jnp.where(earlier, 1.0, 0.0).astype(jnp.bfloat16),
        preferred_element_type=jnp.float32,
    )
    rank = jnp.where(chosen > 0.0, rank, -1.0)
    rank_gates[:EXPERTS, :] = rank
    slot = lax.broadcasted_iota(jnp.int32, (CAPACITY, tokens), 0).astype(jnp.float32)
    for g in range(EXPERTS):
        place[g * CAPACITY : (g + 1) * CAPACITY, :] = jnp.where(
            rank[g : g + 1, :] == slot, 1.0, 0.0
        ).astype(jnp.bfloat16)
    for c in range(0, 1536, 256):
        while copies and len(copies) > 16 - (c + 256 + 95) // 96:
            copies.pop(0).wait()
        hidden_ref[:, c : c + 256] = rows_ref[:, c : c + 256].astype(jnp.float32) + lax.dot_general(
            attended[...],
            weight[c : c + 256, :],
            (((1,), (1,)), ((), ())),
            preferred_element_type=jnp.float32,
        )
    keep = pltpu.make_async_copy(hidden_ref, hidden_out, out_sem.at[6])
    keep.start()
    hidden = hidden_ref[...]
    moe_in = rms_scale(hidden, gain_ref[...]).astype(jnp.bfloat16)
    for c in range(0, EXPERTS * CAPACITY, 256):
        staged[c : c + 256, :] = jnp.dot(
            place[c : c + 256, :], moe_in, preferred_element_type=jnp.float32
        ).astype(jnp.bfloat16)
        pltpu.make_async_copy(
            staged.at[pl.ds(c, 256)], send_ref.at[pl.ds(c, 256)], out_sem.at[c // 256]
        ).start()
    logits = lax.dot_general(
        router_ref[...], moe_in, (((1,), (1,)), ((), ())), preferred_element_type=jnp.float32
    )
    top_logit = jnp.max(jnp.where(chosen > 0.0, logits, -3e38), axis=0, keepdims=True)
    raised = jnp.where(chosen > 0.0, jnp.exp(jnp.minimum(logits - top_logit, 0.0)), 0.0)
    rank_gates[EXPERTS:, :] = raised / jnp.sum(raised, axis=0, keepdims=True)
    last = pltpu.make_async_copy(rank_gates, rank_gates_out, out_sem.at[7])
    last.start()
    for c in range(0, EXPERTS * CAPACITY, 256):
        pltpu.make_async_copy(
            staged.at[pl.ds(c, 256)], send_ref.at[pl.ds(c, 256)], out_sem.at[c // 256]
        ).wait()
    keep.wait()
    last.wait()


def project_and_dispatch(parts, output_weight, own_rows, moe_gain, router_hosted, ids_by_choice):
    row_count, model_width = own_rows.shape
    slots = EXPERTS * CAPACITY
    vmem = pl.BlockSpec(memory_space=pltpu.VMEM)
    return pl.pallas_call(
        project_body,
        out_shape=(
            pltpu.HBM((row_count, model_width), jnp.float32),
            pltpu.HBM((slots, model_width), jnp.bfloat16),
            pltpu.HBM((2 * EXPERTS, row_count), jnp.float32),
        ),
        in_specs=[vmem, pl.BlockSpec(memory_space=pltpu.HBM), vmem, vmem, vmem, vmem],
        out_specs=(pl.BlockSpec(memory_space=pltpu.HBM),) * 3,
        scratch_shapes=[
            pltpu.VMEM((model_width, model_width), jnp.bfloat16),
            pltpu.VMEM((row_count, model_width), jnp.bfloat16),
            pltpu.VMEM((slots, row_count), jnp.bfloat16),
            pltpu.VMEM((slots, model_width), jnp.bfloat16),
            pltpu.VMEM((row_count, model_width), jnp.float32),
            pltpu.VMEM((2 * EXPERTS, row_count), jnp.float32),
            pltpu.SemaphoreType.DMA((16,)),
            pltpu.SemaphoreType.DMA((8,)),
        ],
        compiler_params=pltpu.CompilerParams(vmem_limit_bytes=40 << 20),
        cost_estimate=pl.CostEstimate(
            flops=4 * row_count * model_width * model_width,
            bytes_accessed=4 * model_width * model_width,
            transcendentals=0,
        ),
        name="project_and_dispatch",
    )(
        parts,
        pltpu.with_memory_space_constraint(output_weight.reshape(8, 2, 96, model_width), pltpu.HBM),
        own_rows,
        moe_gain.reshape(1, model_width),
        router_hosted,
        ids_by_choice,
    )


def weigh_body(rank_gates_ref, both_ref, weigh):
    tokens = rank_gates_ref.shape[1]
    slot = lax.broadcasted_iota(jnp.int32, (CAPACITY, tokens), 0).astype(jnp.float32)
    for g in range(EXPERTS):
        weigh[g * CAPACITY : (g + 1) * CAPACITY, :] = jnp.where(
            rank_gates_ref[g : g + 1, :] == slot,
            rank_gates_ref[EXPERTS + g : EXPERTS + g + 1, :],
            0.0,
        )
    for c in range(0, EXPERTS * CAPACITY, 128):
        by_token = weigh[c : c + 128, :].T
        high = by_token.astype(jnp.bfloat16)
        both_ref[:tokens, c : c + 128] = high
        both_ref[tokens:, c : c + 128] = (by_token - high.astype(jnp.float32)).astype(jnp.bfloat16)


def weighing(rank_gates):
    row_count = rank_gates.shape[1]
    slots = EXPERTS * CAPACITY
    vmem = pl.BlockSpec(memory_space=pltpu.VMEM)
    return pl.pallas_call(
        weigh_body,
        out_shape=jax.ShapeDtypeStruct((2 * row_count, slots), jnp.bfloat16),
        in_specs=[vmem],
        out_specs=vmem,
        scratch_shapes=[pltpu.VMEM((slots, row_count), jnp.float32)],
        cost_estimate=pl.CostEstimate(flops=1 << 20, bytes_accessed=1 << 20, transcendentals=0),
        name="weighing",
    )(rank_gates)


def expert_body(rows_ref, gate_up_ref, down_ref, out_ref):
    gate_up = jnp.dot(rows_ref[...], gate_up_ref[...], preferred_element_type=jnp.float32)
    activated = (jax.nn.silu(gate_up[:, :FF]) * gate_up[:, FF:]).astype(jnp.bfloat16)
    out_ref[...] = jnp.dot(activated, down_ref[...], preferred_element_type=jnp.float32).astype(
        jnp.bfloat16
    )


def experts(rows, gate_up, down):
    count, model_width = rows.shape
    tile = 512
    return pl.pallas_call(
        expert_body,
        out_shape=pltpu.HBM((count, model_width), jnp.bfloat16),
        grid=(count // tile,),
        in_specs=[
            pl.BlockSpec((tile, model_width), lambda i: (i, 0)),
            pl.BlockSpec(gate_up.shape, lambda i: (0, 0)),
            pl.BlockSpec(down.shape, lambda i: (0, 0)),
        ],
        out_specs=pl.BlockSpec((tile, model_width), lambda i: (i, 0)),
        compiler_params=pltpu.CompilerParams(vmem_limit_bytes=40 << 20),
        cost_estimate=pl.CostEstimate(
            flops=2 * count * model_width * 3 * FF,
            bytes_accessed=4 * count * model_width + 6 * model_width * FF,
            transcendentals=count * FF,
        ),
        name="experts",
    )(rows, gate_up, down)


def combine_body(live_ref, both_ref, returned_ref, hidden_ref, out_ref):
    tokens = hidden_ref.shape[0]
    mixed = jnp.dot(both_ref[...], returned_ref[...], preferred_element_type=jnp.float32)
    total = hidden_ref[...] + (mixed[:tokens] + mixed[tokens:])
    row = lax.broadcasted_iota(jnp.int32, total.shape, 0)
    out_ref[...] = jnp.where(row < live_ref[0], total, 0.0).astype(jnp.bfloat16)


def combine(live, both, returned, hidden):
    row_count, model_width = hidden.shape
    slots = returned.shape[0]
    tile = model_width // 2
    column = pl.BlockSpec((row_count, tile), lambda i: (0, i))
    return pl.pallas_call(
        combine_body,
        out_shape=jax.ShapeDtypeStruct((row_count, model_width), jnp.bfloat16),
        grid=(model_width // tile,),
        in_specs=[
            pl.BlockSpec(memory_space=pltpu.SMEM),
            pl.BlockSpec(memory_space=pltpu.VMEM),
            pl.BlockSpec((slots, tile), lambda i: (0, i)),
            column,
        ],
        out_specs=column,
        compiler_params=pltpu.CompilerParams(vmem_limit_bytes=24 << 20),
        cost_estimate=pl.CostEstimate(
            flops=4 * row_count * slots * model_width,
            bytes_accessed=2 * slots * model_width + 6 * row_count * model_width,
            transcendentals=0,
        ),
        name="combine",
    )(live, both, returned, hidden)


def on_device(
    tokens_in,
    lengths,
    attn_gain,
    q_proj,
    k_proj,
    value_projection,
    o_proj,
    key_value_pages,
    page_table,
    moe_gain,
    router,
    expert_ids,
    gate_up_proj,
    down_proj,
):
    seq_len, model_width = tokens_in.shape
    barrier = lax.optimization_barrier
    tp_index = lax.axis_index("tp")
    row_count = seq_len // 8

    def in_plane(rows):
        return lax.all_to_all(
            rows, ("ep", "tp"), 0, 0, axis_index_groups=PLANE_GROUPS, tiled=True
        )

    def doubled(block, axis, bit):
        size = lax.axis_size(axis)
        other = lax.ppermute(block, axis, [(i, i ^ bit) for i in range(size)])
        first = (lax.axis_index(axis) & bit) == 0
        return jnp.concatenate(
            [jnp.where(first, block, other), jnp.where(first, other, block)], axis=0
        )

    weight_shard = jnp.concatenate(
        [q_proj, k_proj, value_projection, jnp.zeros_like(k_proj)], axis=1
    ).astype(jnp.bfloat16)
    slabs = weight_shard.reshape(48, 3, 128).transpose(1, 0, 2).reshape(144, 128)
    pages = key_value_pages[page_table[:, 0, :]].reshape(2, 8, 2, 32, 128)
    gate_up_slabs = gate_up_proj.astype(jnp.bfloat16).reshape(8, 24, 8, 128).transpose(0, 2, 1, 3)
    down_slabs = down_proj.astype(jnp.bfloat16).reshape(8, 8, 12, 128).transpose(0, 2, 1, 3)
    payload = jnp.concatenate(
        [
            jnp.broadcast_to(slabs[None], (8, 144, 128)),
            pages.transpose(1, 0, 2, 3, 4).reshape(8, 128, 128),
            gate_up_slabs.reshape(8, 192, 128),
            down_slabs.reshape(8, 96, 128),
        ],
        axis=1,
    )
    normalized = rms_scale(tokens_in.astype(jnp.float32), attn_gain).astype(jnp.bfloat16)
    output_plane = doubled(o_proj.T.astype(jnp.bfloat16)[None], "tp", 1)
    output_plane, unused = barrier((output_plane, payload))
    output_plane = doubled(doubled(output_plane, "tp", 2), "tp", 4)
    output_plane = output_plane.transpose(1, 0, 2).reshape(48, model_width)
    output_plane, normalized = barrier((output_plane, normalized))
    output_plane = doubled(doubled(output_plane, "ep", 1), "ep", 16)
    along_z = lax.all_to_all(payload, "ep", 0, 0, axis_index_groups=Z_GROUPS, tiled=True)
    output_plane, along_z = barrier((output_plane, along_z))
    output_weight = lax.all_gather(output_plane, "ep", axis_index_groups=Z_GROUPS)
    payload, by_expert = relay(along_z)
    across = lax.all_to_all(payload, "ep", 0, 0, axis_index_groups=CHIP_PAIR_GROUPS, tiled=True)
    table = rotary_table(seq_len, 32 * 32)
    by_expert, across = barrier((by_expert, across))
    hosted = lax.all_to_all(by_expert, "tp", 0, 0, tiled=True)
    attended = attention(lengths, normalized, across, table)
    attended, hosted = barrier((attended, hosted))
    attn_parts = lax.all_to_all(attended, "tp", 0, 0, tiled=True)
    planes = lax.all_gather(hosted, "ep", axis_index_groups=Z_GROUPS)
    own_rows = lax.dynamic_slice_in_dim(tokens_in, tp_index * row_count, row_count, 0)
    router_hosted = router.T.reshape(2, 8, 2, model_width).transpose(0, 2, 1, 3)
    hidden, send_rows, rank_gates = project_and_dispatch(
        attn_parts,
        output_weight,
        own_rows,
        moe_gain,
        router_hosted.reshape(EXPERTS, model_width),
        expert_ids.T,
    )
    gate_up_full = (
        planes[:, :, :192].reshape(8, 8, 8, 24, 128).transpose(1, 0, 3, 2, 4).reshape(model_width, 2 * FF)
    )
    down_full = (
        planes[:, :, 192:].reshape(8, 8, 12, 8, 128).transpose(1, 0, 3, 2, 4).reshape(FF, model_width)
    )
    received = in_plane(send_rows.reshape(EXPERTS, CAPACITY, model_width))
    both = weighing(rank_gates)
    expert_out = experts(received.reshape(-1, model_width), gate_up_full, down_full)
    returned = in_plane(expert_out.reshape(EXPERTS, CAPACITY, model_width))
    live = lengths - tp_index * row_count
    return combine(live, both, returned.reshape(-1, model_width), hidden)


def solution(mesh):
    in_specs = (
        P("ep", None),
        P("ep"),
        P(),
        P("ep", "tp"),
        P("ep", "tp"),
        P("ep", "tp"),
        P("tp", "ep"),
        P("ep", None, "tp"),
        P(None, "ep", None),
        P(),
        P(),
        P(("ep", "tp"), None),
        P("ep", "tp", None),
        P("ep", "tp", None),
    )
    out_specs = P(("ep", "tp"), None)
    return jax.shard_map(
        on_device, mesh=mesh, in_specs=in_specs, out_specs=out_specs, check_vma=False
    )
```

```python
import math

import jax
import jax.numpy as jnp
from jax import lax
from jax.experimental import pallas as pl
from jax.experimental.pallas import tpu as pltpu
from jax.sharding import PartitionSpec as P

HEAD_WIDTH = 64
FF = 512
CAPACITY = 48
EXPERTS = 32


epsilon = 1e-05

Z_GROUPS = [[y * 16 + z * 2 + c for z in range(8)] for y in range(2) for c in range(2)]
CHIP_PAIR_GROUPS = [[y * 16 + z * 2 + c for y in range(2) for c in range(2)] for z in range(8)]
PLANE_GROUPS = [
    [(y * 16 + z * 2 + c) * 8 + t for y in range(2) for c in range(2) for t in range(8)]
    for z in range(8)
]


def rms_scale(values, norm_gain):
    mean_square = jnp.mean(values * values, axis=-1, keepdims=True)
    return values * lax.rsqrt(mean_square + epsilon) * norm_gain


def rotary_table(positions, first_position):
    lane = jnp.arange(2 * HEAD_WIDTH)
    frequency = jnp.exp(
        (lane % (HEAD_WIDTH // 2)).astype(jnp.float32) * (-2.0 * math.log(10000.0) / HEAD_WIDTH)
    )
    angles = (first_position + jnp.arange(positions)).astype(jnp.float32)[:, None] * frequency
    sign = jnp.where(lane % HEAD_WIDTH < HEAD_WIDTH // 2, -1.0, 1.0)
    return jnp.where(lane < HEAD_WIDTH, jnp.cos(angles), jnp.sin(angles) * sign)


def attention_body(
    length_ref, source_ref, normalized_ref, first_ref, mine_ref, core_ref, far_ref, both_ref, table_ref,
    out_ref, queries, keys, values, weight, cached_rows,
):
    seq_len = normalized_ref.shape[0]
    heads = queries.shape[0]
    prefix = keys.shape[1] - seq_len
    chunk = 256
    lane = lax.broadcasted_iota(jnp.int32, (chunk, 256), 1)
    ones = jnp.ones((chunk, HEAD_WIDTH), jnp.bfloat16)
    arrived = (
        (first_ref, 32, mine_ref, 0),
        (core_ref, 32, core_ref, 0),
        (far_ref, 0, far_ref, 176),
        (both_ref, 0, both_ref, 144),
    )
    for r, (weights_ref, weights_at, pages_ref, pages_at) in enumerate(arrived):
        for z in range(8):
            e = source_ref[r] + 2 * z
            for j in range(3):
                weight[pl.ds(pl.multiple_of(e * 48, 16), 48), j * 128 : (j + 1) * 128] = weights_ref[
                    z, weights_at + j * 48 : weights_at + (j + 1) * 48, :
                ]
            cached_rows[pl.ds(pl.multiple_of(e * 32, 32), 32), :] = pages_ref[
                z, pages_at : pages_at + 32, :
            ]
    for c in range(0, prefix, chunk):
        rows = cached_rows[c : c + chunk, :]
        keys[:, c : c + chunk] = rows.astype(jnp.float32).T[:HEAD_WIDTH].astype(jnp.bfloat16)
        values[c : c + chunk, :] = jnp.concatenate([rows[:, HEAD_WIDTH:], ones], axis=1)
    for c in range(0, seq_len, chunk):
        projected = jnp.dot(
            normalized_ref[c : c + chunk, :], weight[...], preferred_element_type=jnp.float32
        )
        plain = projected[:, :256]
        partner = jnp.where(
            lane % HEAD_WIDTH < HEAD_WIDTH // 2,
            pltpu.roll(plain, 256 - HEAD_WIDTH // 2, 1),
            pltpu.roll(plain, HEAD_WIDTH // 2, 1),
        )
        cosine = table_ref[c : c + chunk, :HEAD_WIDTH]
        sine = table_ref[c : c + chunk, HEAD_WIDTH:]
        rotated = plain * jnp.concatenate([cosine] * 4, axis=1) + partner * jnp.concatenate(
            [sine] * 4, axis=1
        )
        rounded = rotated.astype(jnp.bfloat16)
        for h in range(heads):
            queries[h, c : c + chunk, :] = (
                rounded[:, h * HEAD_WIDTH : (h + 1) * HEAD_WIDTH] * HEAD_WIDTH ** (-0.5)
            ).astype(jnp.bfloat16)
        keys[:, prefix + c : prefix + c + chunk] = (
            rotated.T[heads * HEAD_WIDTH :].astype(jnp.bfloat16)
        )
        values[prefix + c : prefix + c + chunk, :] = jnp.concatenate(
            [projected[:, 256 : 256 + HEAD_WIDTH].astype(jnp.bfloat16), ones], axis=1
        )
    length = length_ref[0]
    for start in range(0, seq_len, chunk):
        seen = start + chunk
        column = lax.broadcasted_iota(jnp.int32, (chunk, seen), 1)
        row = lax.broadcasted_iota(jnp.int32, (chunk, seen), 0)
        allowed = (column <= row + start) & (column < length)
        outs = []
        for h in range(heads):
            query = queries[h, start:seen, :]
            cached = jnp.dot(query, keys[:, :prefix], preferred_element_type=jnp.float32)
            own = jnp.dot(query, keys[:, prefix : prefix + seen], preferred_element_type=jnp.float32)
            own = jnp.where(allowed, own, -1e30)
            top = jnp.maximum(
                jnp.max(cached, axis=1, keepdims=True), jnp.max(own, axis=1, keepdims=True)
            )
            total = jnp.dot(
                jnp.exp(cached - top).astype(jnp.bfloat16),
                values[:prefix, :],
                preferred_element_type=jnp.float32,
            ) + jnp.dot(
                jnp.exp(own - top).astype(jnp.bfloat16),
                values[prefix : prefix + seen, :],
                preferred_element_type=jnp.float32,
            )
            outs.append(total[:, :HEAD_WIDTH] / total[:, HEAD_WIDTH : HEAD_WIDTH + 1])
        for t in range(0, chunk, 128):
            block = (start + t) // 128
            low, high = outs[2][t : t + 64], outs[2][t + 64 : t + 128]
            out_ref[block, :128, :] = jnp.concatenate(
                [outs[0][t : t + 128], outs[1][t : t + 128]], axis=1
            ).astype(jnp.bfloat16)
            out_ref[block, 128:, :] = jnp.concatenate([low, high], axis=1).astype(jnp.bfloat16)


def attention(lengths, sources, normalized, first, mine, core, far, both, table):
    seq_len, model_width = normalized.shape
    heads = 3
    total = 2 * seq_len
    vmem = pl.BlockSpec(memory_space=pltpu.VMEM)
    return pl.pallas_call(
        attention_body,
        out_shape=pltpu.HBM((seq_len // 128, 192, 128), jnp.bfloat16),
        in_specs=[pl.BlockSpec(memory_space=pltpu.SMEM)] * 2 + [vmem] * 7,
        out_specs=vmem,
        scratch_shapes=[
            pltpu.VMEM((heads, seq_len, HEAD_WIDTH), jnp.bfloat16),
            pltpu.VMEM((HEAD_WIDTH, total), jnp.bfloat16),
            pltpu.VMEM((total, 2 * HEAD_WIDTH), jnp.bfloat16),
            pltpu.VMEM((model_width, 384), jnp.bfloat16),
            pltpu.VMEM((seq_len, 2 * HEAD_WIDTH), jnp.bfloat16),
        ],
        compiler_params=pltpu.CompilerParams(vmem_limit_bytes=48 << 20),
        cost_estimate=pl.CostEstimate(
            flops=12_000_000_000, bytes_accessed=8 << 20, transcendentals=heads * seq_len * total
        ),
        name="attention",
    )(lengths, sources, normalized, first, mine, core, far, both, table)


def relay_body(along_ref, far_ref, first_ref, expert_ref, mine_ref, held, sem):
    loads = [pltpu.make_async_copy(along_ref.at[z], held.at[z], sem.at[z]) for z in range(8)]
    for load in loads:
        load.start()
    for load in loads:
        load.wait()
    copies = [
        pltpu.make_async_copy(held.at[:, pl.ds(32, 208)], far_ref, sem.at[0]),
        pltpu.make_async_copy(held.at[:, pl.ds(0, 176)], first_ref, sem.at[1]),
        pltpu.make_async_copy(held.at[:, pl.ds(240, 32)], mine_ref, sem.at[2]),
        pltpu.make_async_copy(held.at[:, pl.ds(272, 288)], expert_ref, sem.at[3]),
    ]
    for copy in copies:
        copy.start()
    for copy in copies:
        copy.wait()


def relay(along_z):
    hbm = pl.BlockSpec(memory_space=pltpu.HBM)
    return pl.pallas_call(
        relay_body,
        out_shape=tuple(pltpu.HBM((8, rows, 128), jnp.bfloat16) for rows in (208, 176, 288, 32)),
        in_specs=[hbm],
        out_specs=(hbm,) * 4,
        scratch_shapes=[pltpu.VMEM(along_z.shape, jnp.bfloat16), pltpu.SemaphoreType.DMA((8,))],
        cost_estimate=pl.CostEstimate(flops=0, bytes_accessed=4 << 20, transcendentals=0),
        name="relay",
    )(pltpu.with_memory_space_constraint(along_z, pltpu.HBM))


def project_body(
    parts_ref, weight_hbm, rows_ref, gain_ref, router_ref, ids_ref,
    hidden_out, send_ref, rank_gates_out,
    weight, attended, place, staged, hidden_ref, rank_gates, sem, out_sem,
):
    copies = []
    for y in range(2):
        for z in range(8):
            copy = pltpu.make_async_copy(
                weight_hbm.at[z, y], weight.at[pl.ds((y * 8 + z) * 96, 96)], sem.at[y * 8 + z]
            )
            copy.start()
            copies.append(copy)
    for t in range(8):
        at = t * 192
        attended[:, at : at + 128] = parts_ref[t, :128, :]
        attended[:64, at + 128 : at + 192] = parts_ref[t, 128:, :64]
        attended[64:, at + 128 : at + 192] = parts_ref[t, 128:, 64:]
    tokens = rows_ref.shape[0]
    host = lax.broadcasted_iota(jnp.int32, (EXPERTS, tokens), 0)
    expert_at = (host // 16) * 16 + (host % 8) * 2 + (host // 8) % 2
    chosen = jnp.zeros((EXPERTS, tokens), jnp.float32)
    for k in range(ids_ref.shape[0]):
        chosen = jnp.where(ids_ref[k : k + 1, :] == expert_at, 1.0, chosen)
    earlier = lax.broadcasted_iota(jnp.int32, (tokens, tokens), 0) < lax.broadcasted_iota(
        jnp.int32, (tokens, tokens), 1
    )
    rank = jnp.dot(
        chosen.astype(jnp.bfloat16),
        jnp.where(earlier, 1.0, 0.0).astype(jnp.bfloat16),
        preferred_element_type=jnp.float32,
    )
    rank = jnp.where(chosen > 0.0, rank, -1.0)
    rank_gates[:EXPERTS, :] = rank
    slot = lax.broadcasted_iota(jnp.int32, (CAPACITY, tokens), 0).astype(jnp.float32)
    for g in range(EXPERTS):
        place[g * CAPACITY : (g + 1) * CAPACITY, :] = jnp.where(
            rank[g : g + 1, :] == slot, 1.0, 0.0
        ).astype(jnp.bfloat16)
    for c in range(0, 1536, 256):
        while copies and len(copies) > 16 - (c + 256 + 95) // 96:
            copies.pop(0).wait()
        hidden_ref[:, c : c + 256] = rows_ref[:, c : c + 256].astype(jnp.float32) + lax.dot_general(
            attended[...],
            weight[c : c + 256, :],
            (((1,), (1,)), ((), ())),
            preferred_element_type=jnp.float32,
        )
    keep = pltpu.make_async_copy(hidden_ref, hidden_out, out_sem.at[6])
    keep.start()
    hidden = hidden_ref[...]
    moe_in = rms_scale(hidden, gain_ref[...]).astype(jnp.bfloat16)
    for c in range(0, EXPERTS * CAPACITY, 256):
        staged[c : c + 256, :] = jnp.dot(
            place[c : c + 256, :], moe_in, preferred_element_type=jnp.float32
        ).astype(jnp.bfloat16)
        pltpu.make_async_copy(
            staged.at[pl.ds(c, 256)], send_ref.at[pl.ds(c, 256)], out_sem.at[c // 256]
        ).start()
    logits = lax.dot_general(
        router_ref[...], moe_in, (((1,), (1,)), ((), ())), preferred_element_type=jnp.float32
    )
    top_logit = jnp.max(jnp.where(chosen > 0.0, logits, -3e38), axis=0, keepdims=True)
    raised = jnp.where(chosen > 0.0, jnp.exp(jnp.minimum(logits - top_logit, 0.0)), 0.0)
    rank_gates[EXPERTS:, :] = raised / jnp.sum(raised, axis=0, keepdims=True)
    last = pltpu.make_async_copy(rank_gates, rank_gates_out, out_sem.at[7])
    last.start()
    for c in range(0, EXPERTS * CAPACITY, 256):
        pltpu.make_async_copy(
            staged.at[pl.ds(c, 256)], send_ref.at[pl.ds(c, 256)], out_sem.at[c // 256]
        ).wait()
    keep.wait()
    last.wait()


def project_and_dispatch(parts, output_weight, own_rows, moe_gain, router_hosted, ids_by_choice):
    row_count, model_width = own_rows.shape
    slots = EXPERTS * CAPACITY
    vmem = pl.BlockSpec(memory_space=pltpu.VMEM)
    return pl.pallas_call(
        project_body,
        out_shape=(
            pltpu.HBM((row_count, model_width), jnp.float32),
            pltpu.HBM((slots, model_width), jnp.bfloat16),
            pltpu.HBM((2 * EXPERTS, row_count), jnp.float32),
        ),
        in_specs=[vmem, pl.BlockSpec(memory_space=pltpu.HBM), vmem, vmem, vmem, vmem],
        out_specs=(pl.BlockSpec(memory_space=pltpu.HBM),) * 3,
        scratch_shapes=[
            pltpu.VMEM((model_width, model_width), jnp.bfloat16),
            pltpu.VMEM((row_count, model_width), jnp.bfloat16),
            pltpu.VMEM((slots, row_count), jnp.bfloat16),
            pltpu.VMEM((slots, model_width), jnp.bfloat16),
            pltpu.VMEM((row_count, model_width), jnp.float32),
            pltpu.VMEM((2 * EXPERTS, row_count), jnp.float32),
            pltpu.SemaphoreType.DMA((16,)),
            pltpu.SemaphoreType.DMA((8,)),
        ],
        compiler_params=pltpu.CompilerParams(vmem_limit_bytes=40 << 20),
        cost_estimate=pl.CostEstimate(
            flops=4 * row_count * model_width * model_width,
            bytes_accessed=4 * model_width * model_width,
            transcendentals=0,
        ),
        name="project_and_dispatch",
    )(
        parts,
        pltpu.with_memory_space_constraint(output_weight.reshape(8, 2, 96, model_width), pltpu.HBM),
        own_rows,
        moe_gain.reshape(1, model_width),
        router_hosted,
        ids_by_choice,
    )


def weigh_body(rank_gates_ref, both_ref, weigh):
    tokens = rank_gates_ref.shape[1]
    slot = lax.broadcasted_iota(jnp.int32, (CAPACITY, tokens), 0).astype(jnp.float32)
    for g in range(EXPERTS):
        weigh[g * CAPACITY : (g + 1) * CAPACITY, :] = jnp.where(
            rank_gates_ref[g : g + 1, :] == slot,
            rank_gates_ref[EXPERTS + g : EXPERTS + g + 1, :],
            0.0,
        )
    for c in range(0, EXPERTS * CAPACITY, 128):
        by_token = weigh[c : c + 128, :].T
        high = by_token.astype(jnp.bfloat16)
        both_ref[:tokens, c : c + 128] = high
        both_ref[tokens:, c : c + 128] = (by_token - high.astype(jnp.float32)).astype(jnp.bfloat16)


def weighing(rank_gates):
    row_count = rank_gates.shape[1]
    slots = EXPERTS * CAPACITY
    vmem = pl.BlockSpec(memory_space=pltpu.VMEM)
    return pl.pallas_call(
        weigh_body,
        out_shape=jax.ShapeDtypeStruct((2 * row_count, slots), jnp.bfloat16),
        in_specs=[vmem],
        out_specs=vmem,
        scratch_shapes=[pltpu.VMEM((slots, row_count), jnp.float32)],
        cost_estimate=pl.CostEstimate(flops=1 << 20, bytes_accessed=1 << 20, transcendentals=0),
        name="weighing",
    )(rank_gates)


def expert_body(rows_ref, gate_up_ref, down_ref, out_ref):
    gate_up = jnp.dot(rows_ref[...], gate_up_ref[...], preferred_element_type=jnp.float32)
    activated = (jax.nn.silu(gate_up[:, :FF]) * gate_up[:, FF:]).astype(jnp.bfloat16)
    out_ref[...] = jnp.dot(activated, down_ref[...], preferred_element_type=jnp.float32).astype(
        jnp.bfloat16
    )


def experts(rows, gate_up, down):
    count, model_width = rows.shape
    tile = 512
    return pl.pallas_call(
        expert_body,
        out_shape=pltpu.HBM((count, model_width), jnp.bfloat16),
        grid=(count // tile,),
        in_specs=[
            pl.BlockSpec((tile, model_width), lambda i: (i, 0)),
            pl.BlockSpec(gate_up.shape, lambda i: (0, 0)),
            pl.BlockSpec(down.shape, lambda i: (0, 0)),
        ],
        out_specs=pl.BlockSpec((tile, model_width), lambda i: (i, 0)),
        compiler_params=pltpu.CompilerParams(vmem_limit_bytes=40 << 20),
        cost_estimate=pl.CostEstimate(
            flops=2 * count * model_width * 3 * FF,
            bytes_accessed=4 * count * model_width + 6 * model_width * FF,
            transcendentals=count * FF,
        ),
        name="experts",
    )(rows, gate_up, down)


def combine_body(live_ref, both_ref, returned_ref, hidden_ref, out_ref):
    tokens = hidden_ref.shape[0]
    mixed = jnp.dot(both_ref[...], returned_ref[...], preferred_element_type=jnp.float32)
    total = hidden_ref[...] + (mixed[:tokens] + mixed[tokens:])
    row = lax.broadcasted_iota(jnp.int32, total.shape, 0)
    out_ref[...] = jnp.where(row < live_ref[0], total, 0.0).astype(jnp.bfloat16)


def combine(live, both, returned, hidden):
    row_count, model_width = hidden.shape
    slots = returned.shape[0]
    tile = model_width // 2
    column = pl.BlockSpec((row_count, tile), lambda i: (0, i))
    return pl.pallas_call(
        combine_body,
        out_shape=jax.ShapeDtypeStruct((row_count, model_width), jnp.bfloat16),
        grid=(model_width // tile,),
        in_specs=[
            pl.BlockSpec(memory_space=pltpu.SMEM),
            pl.BlockSpec(memory_space=pltpu.VMEM),
            pl.BlockSpec((slots, tile), lambda i: (0, i)),
            column,
        ],
        out_specs=column,
        compiler_params=pltpu.CompilerParams(vmem_limit_bytes=24 << 20),
        cost_estimate=pl.CostEstimate(
            flops=4 * row_count * slots * model_width,
            bytes_accessed=2 * slots * model_width + 6 * row_count * model_width,
            transcendentals=0,
        ),
        name="combine",
    )(live, both, returned, hidden)


def on_device(
    tokens_in,
    lengths,
    attn_gain,
    q_proj,
    k_proj,
    value_projection,
    o_proj,
    key_value_pages,
    page_table,
    moe_gain,
    router,
    expert_ids,
    gate_up_proj,
    down_proj,
):
    seq_len, model_width = tokens_in.shape
    barrier = lax.optimization_barrier
    tp_index = lax.axis_index("tp")
    row_count = seq_len // 8

    def in_plane(rows):
        return lax.all_to_all(
            rows, ("ep", "tp"), 0, 0, axis_index_groups=PLANE_GROUPS, tiled=True
        )

    def doubled(block, axis, bit):
        size = lax.axis_size(axis)
        other = lax.ppermute(block, axis, [(i, i ^ bit) for i in range(size)])
        first = (lax.axis_index(axis) & bit) == 0
        return jnp.concatenate(
            [jnp.where(first, block, other), jnp.where(first, other, block)], axis=0
        )

    weight_shard = jnp.concatenate(
        [q_proj, k_proj, value_projection, jnp.zeros_like(k_proj)], axis=1
    ).astype(jnp.bfloat16)
    slabs = weight_shard.reshape(48, 3, 128).transpose(1, 0, 2).reshape(144, 128)
    ep_index = lax.axis_index("ep")
    pair = (ep_index // 16) * 2 + ep_index % 2
    step_to = jnp.array([1, 3, 2, 0], jnp.int32) ^ pair
    prompts = (step_to // 2 * 16 + step_to % 2)[None, :] + 2 * jnp.arange(8, dtype=jnp.int32)[:, None]
    pages = key_value_pages[page_table[:, 0, :][prompts]].reshape(8, 4, 32, 128)
    gate_up_slabs = gate_up_proj.astype(jnp.bfloat16).reshape(8, 24, 8, 128).transpose(0, 2, 1, 3)
    down_slabs = down_proj.astype(jnp.bfloat16).reshape(8, 8, 12, 128).transpose(0, 2, 1, 3)
    payload = jnp.concatenate(
        [
            pages[:, 0],
            jnp.broadcast_to(slabs[None], (8, 144, 128)),
            pages[:, 1],
            pages[:, 2],
            pages[:, 3],
            gate_up_slabs.reshape(8, 192, 128),
            down_slabs.reshape(8, 96, 128),
        ],
        axis=1,
    )
    normalized = rms_scale(tokens_in.astype(jnp.float32), attn_gain).astype(jnp.bfloat16)
    output_plane = doubled(o_proj.T.astype(jnp.bfloat16)[None], "tp", 1)
    output_plane, unused = barrier((output_plane, payload))
    output_plane = doubled(doubled(output_plane, "tp", 2), "tp", 4)
    output_plane = output_plane.transpose(1, 0, 2).reshape(48, model_width)
    output_plane, normalized = barrier((output_plane, normalized))
    output_plane = doubled(doubled(output_plane, "ep", 1), "ep", 16)
    along_z = lax.all_to_all(payload, "ep", 0, 0, axis_index_groups=Z_GROUPS, tiled=True)
    output_plane, along_z = barrier((output_plane, along_z))
    output_weight = lax.all_gather(output_plane, "ep", axis_index_groups=Z_GROUPS)
    far_out, first, by_expert, mine = relay(along_z)
    far = lax.ppermute(far_out, "ep", [(i, i ^ 16) for i in range(32)])
    core = lax.ppermute(first, "ep", [(i, i ^ 1) for i in range(32)])
    both = lax.ppermute(far, "ep", [(i, i ^ 1) for i in range(32)])
    table = rotary_table(seq_len, 32 * 32)
    hosted = lax.all_to_all(by_expert, "tp", 0, 0, tiled=True)
    source = jnp.array([0, 1, 2, 3], jnp.int32) ^ pair
    sources = source // 2 * 16 + source % 2
    attended = attention(lengths, sources, normalized, first, mine, core, far, both, table)
    attended, hosted = barrier((attended, hosted))
    attn_parts = lax.all_to_all(attended, "tp", 0, 0, tiled=True)
    planes = lax.all_gather(hosted, "ep", axis_index_groups=Z_GROUPS)
    own_rows = lax.dynamic_slice_in_dim(tokens_in, tp_index * row_count, row_count, 0)
    router_hosted = router.T.reshape(2, 8, 2, model_width).transpose(0, 2, 1, 3)
    hidden, send_rows, rank_gates = project_and_dispatch(
        attn_parts,
        output_weight,
        own_rows,
        moe_gain,
        router_hosted.reshape(EXPERTS, model_width),
        expert_ids.T,
    )
    gate_up_full = (
        planes[:, :, :192].reshape(8, 8, 8, 24, 128).transpose(1, 0, 3, 2, 4).reshape(model_width, 2 * FF)
    )
    down_full = (
        planes[:, :, 192:].reshape(8, 8, 12, 8, 128).transpose(1, 0, 3, 2, 4).reshape(FF, model_width)
    )
    received = in_plane(send_rows.reshape(EXPERTS, CAPACITY, model_width))
    weighed = weighing(rank_gates)
    expert_out = experts(received.reshape(-1, model_width), gate_up_full, down_full)
    returned = in_plane(expert_out.reshape(EXPERTS, CAPACITY, model_width))
    live = lengths - tp_index * row_count
    return combine(live, weighed, returned.reshape(-1, model_width), hidden)


def solution(mesh):
    in_specs = (
        P("ep", None),
        P("ep"),
        P(),
        P("ep", "tp"),
        P("ep", "tp"),
        P("ep", "tp"),
        P("tp", "ep"),
        P("ep", None, "tp"),
        P(None, "ep", None),
        P(),
        P(),
        P(("ep", "tp"), None),
        P("ep", "tp", None),
        P("ep", "tp", None),
    )
    out_specs = P(("ep", "tp"), None)
    return jax.shard_map(
        on_device, mesh=mesh, in_specs=in_specs, out_specs=out_specs, check_vma=False
    )
```

```python
import math

import jax
import jax.numpy as jnp
from jax import lax
from jax.experimental import pallas as pl
from jax.experimental.pallas import tpu as pltpu
from jax.sharding import PartitionSpec as P

HEAD_WIDTH = 64
FF = 512
CAPACITY = 48
EXPERTS = 32


epsilon = 1e-05

Z_GROUPS = [[y * 16 + z * 2 + c for z in range(8)] for y in range(2) for c in range(2)]
CHIP_PAIR_GROUPS = [[y * 16 + z * 2 + c for y in range(2) for c in range(2)] for z in range(8)]
PLANE_GROUPS = [
    [(y * 16 + z * 2 + c) * 8 + t for y in range(2) for c in range(2) for t in range(8)]
    for z in range(8)
]


def rms_scale(values, norm_gain):
    mean_square = jnp.mean(values * values, axis=-1, keepdims=True)
    return values * lax.rsqrt(mean_square + epsilon) * norm_gain


def rotary_table(positions, first_position):
    lane = jnp.arange(2 * HEAD_WIDTH)
    frequency = jnp.exp(
        (lane % (HEAD_WIDTH // 2)).astype(jnp.float32) * (-2.0 * math.log(10000.0) / HEAD_WIDTH)
    )
    angles = (first_position + jnp.arange(positions)).astype(jnp.float32)[:, None] * frequency
    sign = jnp.where(lane % HEAD_WIDTH < HEAD_WIDTH // 2, -1.0, 1.0)
    return jnp.where(lane < HEAD_WIDTH, jnp.cos(angles), jnp.sin(angles) * sign)


def attention_body(
    length_ref, normalized_ref, across_ref, table_ref,
    out_ref, queries, keys, values, weight,
):
    seq_len = normalized_ref.shape[0]
    heads = queries.shape[0]
    prefix = keys.shape[1] - seq_len
    chunk = 256
    lane = lax.broadcasted_iota(jnp.int32, (chunk, 256), 1)
    ones = jnp.ones((chunk, HEAD_WIDTH), jnp.bfloat16)
    for e in range(32):
        pair, z = (e // 16) * 2 + e % 2, (e // 2) % 8
        for j in range(3):
            weight[e * 48 : (e + 1) * 48, j * 128 : (j + 1) * 128] = across_ref[
                pair, z, j * 48 : (j + 1) * 48, :
            ]
    for c in range(0, prefix, chunk):
        rows = jnp.concatenate(
            [
                across_ref[(e // 16) * 2 + e % 2, (e // 2) % 8, 144:176, :]
                for e in range(c // 32, (c + chunk) // 32)
            ],
            axis=0,
        )
        keys[:, c : c + chunk] = rows.astype(jnp.float32).T[:HEAD_WIDTH].astype(jnp.bfloat16)
        values[c : c + chunk, :] = jnp.concatenate([rows[:, HEAD_WIDTH:], ones], axis=1)
    for c in range(0, seq_len, chunk):
        projected = jnp.dot(
            normalized_ref[c : c + chunk, :], weight[...], preferred_element_type=jnp.float32
        )
        plain = projected[:, :256]
        partner = jnp.where(
            lane % HEAD_WIDTH < HEAD_WIDTH // 2,
            pltpu.roll(plain, 256 - HEAD_WIDTH // 2, 1),
            pltpu.roll(plain, HEAD_WIDTH // 2, 1),
        )
        cosine = table_ref[c : c + chunk, :HEAD_WIDTH]
        sine = table_ref[c : c + chunk, HEAD_WIDTH:]
        rotated = plain * jnp.concatenate([cosine] * 4, axis=1) + partner * jnp.concatenate(
            [sine] * 4, axis=1
        )
        rounded = rotated.astype(jnp.bfloat16)
        for h in range(heads):
            queries[h, c : c + chunk, :] = (
                rounded[:, h * HEAD_WIDTH : (h + 1) * HEAD_WIDTH] * HEAD_WIDTH ** (-0.5)
            ).astype(jnp.bfloat16)
        keys[:, prefix + c : prefix + c + chunk] = (
            rotated.T[heads * HEAD_WIDTH :].astype(jnp.bfloat16)
        )
        values[prefix + c : prefix + c + chunk, :] = jnp.concatenate(
            [projected[:, 256 : 256 + HEAD_WIDTH].astype(jnp.bfloat16), ones], axis=1
        )
    length = length_ref[0]
    for start in range(0, seq_len, chunk):
        seen = start + chunk
        column = lax.broadcasted_iota(jnp.int32, (chunk, seen), 1)
        row = lax.broadcasted_iota(jnp.int32, (chunk, seen), 0)
        allowed = (column <= row + start) & (column < length)
        outs = []
        for h in range(heads):
            query = queries[h, start:seen, :]
            cached = jnp.dot(query, keys[:, :prefix], preferred_element_type=jnp.float32)
            own = jnp.dot(query, keys[:, prefix : prefix + seen], preferred_element_type=jnp.float32)
            own = jnp.where(allowed, own, -1e30)
            top = jnp.maximum(
                jnp.max(cached, axis=1, keepdims=True), jnp.max(own, axis=1, keepdims=True)
            )
            total = jnp.dot(
                jnp.exp(cached - top).astype(jnp.bfloat16),
                values[:prefix, :],
                preferred_element_type=jnp.float32,
            ) + jnp.dot(
                jnp.exp(own - top).astype(jnp.bfloat16),
                values[prefix : prefix + seen, :],
                preferred_element_type=jnp.float32,
            )
            outs.append(total[:, :HEAD_WIDTH] / total[:, HEAD_WIDTH : HEAD_WIDTH + 1])
        for t in range(0, chunk, 128):
            block = (start + t) // 128
            low, high = outs[2][t : t + 64], outs[2][t + 64 : t + 128]
            out_ref[block, :128, :] = jnp.concatenate(
                [outs[0][t : t + 128], outs[1][t : t + 128]], axis=1
            ).astype(jnp.bfloat16)
            out_ref[block, 128:, :] = jnp.concatenate([low, high], axis=1).astype(jnp.bfloat16)


def attention(lengths, normalized, across, table):
    seq_len, model_width = normalized.shape
    heads = 3
    total = 2 * seq_len
    vmem = pl.BlockSpec(memory_space=pltpu.VMEM)
    return pl.pallas_call(
        attention_body,
        out_shape=pltpu.HBM((seq_len // 128, 192, 128), jnp.bfloat16),
        in_specs=[pl.BlockSpec(memory_space=pltpu.SMEM)] + [vmem] * 3,
        out_specs=vmem,
        scratch_shapes=[
            pltpu.VMEM((heads, seq_len, HEAD_WIDTH), jnp.bfloat16),
            pltpu.VMEM((HEAD_WIDTH, total), jnp.bfloat16),
            pltpu.VMEM((total, 2 * HEAD_WIDTH), jnp.bfloat16),
            pltpu.VMEM((model_width, 384), jnp.bfloat16),
        ],
        compiler_params=pltpu.CompilerParams(vmem_limit_bytes=48 << 20),
        cost_estimate=pl.CostEstimate(
            flops=12_000_000_000, bytes_accessed=8 << 20, transcendentals=heads * seq_len * total
        ),
        name="attention",
    )(lengths, normalized, across, table)


def prepare_body(
    table_ref, query_ref, key_ref, value_ref, gate_up_ref, down_ref, pages_ref, payload_ref, held, sem
):
    weight = jnp.concatenate(
        [query_ref[...], key_ref[...], value_ref[...], jnp.zeros(key_ref.shape, jnp.float32)], axis=1
    ).astype(jnp.bfloat16)
    copies = []
    for z in range(8):
        for j in range(3):
            held[z, j * 48 : (j + 1) * 48, :] = weight[:, j * 128 : (j + 1) * 128]
        for d in range(4):
            prompt = (d // 2) * 16 + z * 2 + d % 2
            for s in range(2):
                at = 144 + 32 * d + 16 * s
                held[z, at : at + 16, :] = pages_ref[table_ref[prompt * 2 + s]]
        for b in range(8):
            held[z, 272 + 24 * b : 296 + 24 * b, :] = gate_up_ref[
                z * 24 : (z + 1) * 24, b * 128 : (b + 1) * 128
            ].astype(jnp.bfloat16)
        for b in range(12):
            held[z, 464 + 8 * b : 472 + 8 * b, :] = down_ref[
                z * 8 : (z + 1) * 8, b * 128 : (b + 1) * 128
            ].astype(jnp.bfloat16)
        copy = pltpu.make_async_copy(held.at[z], payload_ref.at[z], sem.at[z])
        copy.start()
        copies.append(copy)
    for copy in copies:
        copy.wait()


def prepare(page_table, q_proj, k_proj, value_projection, gate_up, down, pages):
    vmem = pl.BlockSpec(memory_space=pltpu.VMEM)
    shape = (8, 560, 128)
    return pl.pallas_call(
        prepare_body,
        out_shape=pltpu.HBM(shape, jnp.bfloat16),
        in_specs=[pl.BlockSpec(memory_space=pltpu.SMEM)] + [vmem] * 6,
        out_specs=pl.BlockSpec(memory_space=pltpu.HBM),
        scratch_shapes=[pltpu.VMEM(shape, jnp.bfloat16), pltpu.SemaphoreType.DMA((8,))],
        cost_estimate=pl.CostEstimate(flops=0, bytes_accessed=3 << 20, transcendentals=0),
        name="prepare",
    )(page_table, q_proj, k_proj, value_projection, gate_up, down, pages)


def relay_body(along_ref, payload_ref, expert_ref, held, sem):
    loads = [pltpu.make_async_copy(along_ref.at[z], held.at[z], sem.at[z]) for z in range(8)]
    for load in loads:
        load.start()
    for load in loads:
        load.wait()
    copies = []
    for d in range(4):
        copies.append(
            pltpu.make_async_copy(
                held.at[:, pl.ds(0, 144)], payload_ref.at[d, :, pl.ds(0, 144)], sem.at[2 * d]
            )
        )
        copies.append(
            pltpu.make_async_copy(
                held.at[:, pl.ds(144 + 32 * d, 32)],
                payload_ref.at[d, :, pl.ds(144, 32)],
                sem.at[2 * d + 1],
            )
        )
    copies.append(pltpu.make_async_copy(held.at[:, pl.ds(272, 288)], expert_ref, sem.at[8]))
    for copy in copies:
        copy.start()
    for copy in copies:
        copy.wait()


def relay(along_z):
    hbm = pl.BlockSpec(memory_space=pltpu.HBM)
    return pl.pallas_call(
        relay_body,
        out_shape=(
            pltpu.HBM((4, 8, 176, 128), jnp.bfloat16),
            pltpu.HBM((8, 288, 128), jnp.bfloat16),
        ),
        in_specs=[hbm],
        out_specs=(hbm, hbm),
        scratch_shapes=[pltpu.VMEM(along_z.shape, jnp.bfloat16), pltpu.SemaphoreType.DMA((9,))],
        cost_estimate=pl.CostEstimate(flops=0, bytes_accessed=4 << 20, transcendentals=0),
        name="relay",
    )(pltpu.with_memory_space_constraint(along_z, pltpu.HBM))


def project_body(
    parts_ref, weight_hbm, rows_ref, gain_ref, router_ref, ids_ref,
    hidden_out, send_ref, rank_gates_out,
    weight, attended, place, staged, hidden_ref, rank_gates, sem, out_sem,
):
    copies = []
    for y in range(2):
        for z in range(8):
            copy = pltpu.make_async_copy(
                weight_hbm.at[z, y], weight.at[pl.ds((y * 8 + z) * 96, 96)], sem.at[y * 8 + z]
            )
            copy.start()
            copies.append(copy)
    for t in range(8):
        at = t * 192
        attended[:, at : at + 128] = parts_ref[t, :128, :]
        attended[:64, at + 128 : at + 192] = parts_ref[t, 128:, :64]
        attended[64:, at + 128 : at + 192] = parts_ref[t, 128:, 64:]
    tokens = rows_ref.shape[0]
    host = lax.broadcasted_iota(jnp.int32, (EXPERTS, tokens), 0)
    expert_at = (host // 16) * 16 + (host % 8) * 2 + (host // 8) % 2
    chosen = jnp.zeros((EXPERTS, tokens), jnp.float32)
    for k in range(ids_ref.shape[0]):
        chosen = jnp.where(ids_ref[k : k + 1, :] == expert_at, 1.0, chosen)
    earlier = lax.broadcasted_iota(jnp.int32, (tokens, tokens), 0) < lax.broadcasted_iota(
        jnp.int32, (tokens, tokens), 1
    )
    rank = jnp.dot(
        chosen.astype(jnp.bfloat16),
        jnp.where(earlier, 1.0, 0.0).astype(jnp.bfloat16),
        preferred_element_type=jnp.float32,
    )
    rank = jnp.where(chosen > 0.0, rank, -1.0)
    rank_gates[:EXPERTS, :] = rank
    slot = lax.broadcasted_iota(jnp.int32, (CAPACITY, tokens), 0).astype(jnp.float32)
    for g in range(EXPERTS):
        place[g * CAPACITY : (g + 1) * CAPACITY, :] = jnp.where(
            rank[g : g + 1, :] == slot, 1.0, 0.0
        ).astype(jnp.bfloat16)
    for c in range(0, 1536, 256):
        while copies and len(copies) > 16 - (c + 256 + 95) // 96:
            copies.pop(0).wait()
        hidden_ref[:, c : c + 256] = rows_ref[:, c : c + 256].astype(jnp.float32) + lax.dot_general(
            attended[...],
            weight[c : c + 256, :],
            (((1,), (1,)), ((), ())),
            preferred_element_type=jnp.float32,
        )
    keep = pltpu.make_async_copy(hidden_ref, hidden_out, out_sem.at[6])
    keep.start()
    hidden = hidden_ref[...]
    moe_in = rms_scale(hidden, gain_ref[...]).astype(jnp.bfloat16)
    for c in range(0, EXPERTS * CAPACITY, 256):
        staged[c : c + 256, :] = jnp.dot(
            place[c : c + 256, :], moe_in, preferred_element_type=jnp.float32
        ).astype(jnp.bfloat16)
        pltpu.make_async_copy(
            staged.at[pl.ds(c, 256)], send_ref.at[pl.ds(c, 256)], out_sem.at[c // 256]
        ).start()
    logits = lax.dot_general(
        router_ref[...], moe_in, (((1,), (1,)), ((), ())), preferred_element_type=jnp.float32
    )
    top_logit = jnp.max(jnp.where(chosen > 0.0, logits, -3e38), axis=0, keepdims=True)
    raised = jnp.where(chosen > 0.0, jnp.exp(jnp.minimum(logits - top_logit, 0.0)), 0.0)
    rank_gates[EXPERTS:, :] = raised / jnp.sum(raised, axis=0, keepdims=True)
    last = pltpu.make_async_copy(rank_gates, rank_gates_out, out_sem.at[7])
    last.start()
    for c in range(0, EXPERTS * CAPACITY, 256):
        pltpu.make_async_copy(
            staged.at[pl.ds(c, 256)], send_ref.at[pl.ds(c, 256)], out_sem.at[c // 256]
        ).wait()
    keep.wait()
    last.wait()


def project_and_dispatch(parts, output_weight, own_rows, moe_gain, router_hosted, ids_by_choice):
    row_count, model_width = own_rows.shape
    slots = EXPERTS * CAPACITY
    vmem = pl.BlockSpec(memory_space=pltpu.VMEM)
    return pl.pallas_call(
        project_body,
        out_shape=(
            pltpu.HBM((row_count, model_width), jnp.float32),
            pltpu.HBM((slots, model_width), jnp.bfloat16),
            pltpu.HBM((2 * EXPERTS, row_count), jnp.float32),
        ),
        in_specs=[vmem, pl.BlockSpec(memory_space=pltpu.HBM), vmem, vmem, vmem, vmem],
        out_specs=(pl.BlockSpec(memory_space=pltpu.HBM),) * 3,
        scratch_shapes=[
            pltpu.VMEM((model_width, model_width), jnp.bfloat16),
            pltpu.VMEM((row_count, model_width), jnp.bfloat16),
            pltpu.VMEM((slots, row_count), jnp.bfloat16),
            pltpu.VMEM((slots, model_width), jnp.bfloat16),
            pltpu.VMEM((row_count, model_width), jnp.float32),
            pltpu.VMEM((2 * EXPERTS, row_count), jnp.float32),
            pltpu.SemaphoreType.DMA((16,)),
            pltpu.SemaphoreType.DMA((8,)),
        ],
        compiler_params=pltpu.CompilerParams(vmem_limit_bytes=40 << 20),
        cost_estimate=pl.CostEstimate(
            flops=4 * row_count * model_width * model_width,
            bytes_accessed=4 * model_width * model_width,
            transcendentals=0,
        ),
        name="project_and_dispatch",
    )(
        parts,
        pltpu.with_memory_space_constraint(output_weight.reshape(8, 2, 96, model_width), pltpu.HBM),
        own_rows,
        moe_gain.reshape(1, model_width),
        router_hosted,
        ids_by_choice,
    )


def weigh_body(rank_gates_ref, both_ref, weigh):
    tokens = rank_gates_ref.shape[1]
    slot = lax.broadcasted_iota(jnp.int32, (CAPACITY, tokens), 0).astype(jnp.float32)
    for g in range(EXPERTS):
        weigh[g * CAPACITY : (g + 1) * CAPACITY, :] = jnp.where(
            rank_gates_ref[g : g + 1, :] == slot,
            rank_gates_ref[EXPERTS + g : EXPERTS + g + 1, :],
            0.0,
        )
    for c in range(0, EXPERTS * CAPACITY, 128):
        by_token = weigh[c : c + 128, :].T
        high = by_token.astype(jnp.bfloat16)
        both_ref[:tokens, c : c + 128] = high
        both_ref[tokens:, c : c + 128] = (by_token - high.astype(jnp.float32)).astype(jnp.bfloat16)


def weighing(rank_gates):
    row_count = rank_gates.shape[1]
    slots = EXPERTS * CAPACITY
    vmem = pl.BlockSpec(memory_space=pltpu.VMEM)
    return pl.pallas_call(
        weigh_body,
        out_shape=jax.ShapeDtypeStruct((2 * row_count, slots), jnp.bfloat16),
        in_specs=[vmem],
        out_specs=vmem,
        scratch_shapes=[pltpu.VMEM((slots, row_count), jnp.float32)],
        cost_estimate=pl.CostEstimate(flops=1 << 20, bytes_accessed=1 << 20, transcendentals=0),
        name="weighing",
    )(rank_gates)


def expert_body(rows_ref, gate_up_ref, down_ref, out_ref):
    gate_up = jnp.dot(rows_ref[...], gate_up_ref[...], preferred_element_type=jnp.float32)
    activated = (jax.nn.silu(gate_up[:, :FF]) * gate_up[:, FF:]).astype(jnp.bfloat16)
    out_ref[...] = jnp.dot(activated, down_ref[...], preferred_element_type=jnp.float32).astype(
        jnp.bfloat16
    )


def experts(rows, gate_up, down):
    count, model_width = rows.shape
    tile = 512
    return pl.pallas_call(
        expert_body,
        out_shape=pltpu.HBM((count, model_width), jnp.bfloat16),
        grid=(count // tile,),
        in_specs=[
            pl.BlockSpec((tile, model_width), lambda i: (i, 0)),
            pl.BlockSpec(gate_up.shape, lambda i: (0, 0)),
            pl.BlockSpec(down.shape, lambda i: (0, 0)),
        ],
        out_specs=pl.BlockSpec((tile, model_width), lambda i: (i, 0)),
        compiler_params=pltpu.CompilerParams(vmem_limit_bytes=40 << 20),
        cost_estimate=pl.CostEstimate(
            flops=2 * count * model_width * 3 * FF,
            bytes_accessed=4 * count * model_width + 6 * model_width * FF,
            transcendentals=count * FF,
        ),
        name="experts",
    )(rows, gate_up, down)


def combine_body(live_ref, both_ref, returned_ref, hidden_ref, out_ref):
    tokens = hidden_ref.shape[0]
    mixed = jnp.dot(both_ref[...], returned_ref[...], preferred_element_type=jnp.float32)
    total = hidden_ref[...] + (mixed[:tokens] + mixed[tokens:])
    row = lax.broadcasted_iota(jnp.int32, total.shape, 0)
    out_ref[...] = jnp.where(row < live_ref[0], total, 0.0).astype(jnp.bfloat16)


def combine(live, both, returned, hidden):
    row_count, model_width = hidden.shape
    slots = returned.shape[0]
    tile = model_width // 2
    column = pl.BlockSpec((row_count, tile), lambda i: (0, i))
    return pl.pallas_call(
        combine_body,
        out_shape=jax.ShapeDtypeStruct((row_count, model_width), jnp.bfloat16),
        grid=(model_width // tile,),
        in_specs=[
            pl.BlockSpec(memory_space=pltpu.SMEM),
            pl.BlockSpec(memory_space=pltpu.VMEM),
            pl.BlockSpec((slots, tile), lambda i: (0, i)),
            column,
        ],
        out_specs=column,
        compiler_params=pltpu.CompilerParams(vmem_limit_bytes=24 << 20),
        cost_estimate=pl.CostEstimate(
            flops=4 * row_count * slots * model_width,
            bytes_accessed=2 * slots * model_width + 6 * row_count * model_width,
            transcendentals=0,
        ),
        name="combine",
    )(live, both, returned, hidden)


def on_device(
    tokens_in,
    lengths,
    attn_gain,
    q_proj,
    k_proj,
    value_projection,
    o_proj,
    key_value_pages,
    page_table,
    moe_gain,
    router,
    expert_ids,
    gate_up_proj,
    down_proj,
):
    seq_len, model_width = tokens_in.shape
    barrier = lax.optimization_barrier
    tp_index = lax.axis_index("tp")
    row_count = seq_len // 8

    def in_plane(rows):
        return lax.all_to_all(
            rows, ("ep", "tp"), 0, 0, axis_index_groups=PLANE_GROUPS, tiled=True
        )

    def doubled(block, axis, bit):
        size = lax.axis_size(axis)
        other = lax.ppermute(block, axis, [(i, i ^ bit) for i in range(size)])
        first = (lax.axis_index(axis) & bit) == 0
        return jnp.concatenate(
            [jnp.where(first, block, other), jnp.where(first, other, block)], axis=0
        )

    payload = prepare(
        page_table.reshape(-1), q_proj, k_proj, value_projection, gate_up_proj[0], down_proj[0], key_value_pages
    )
    normalized = rms_scale(tokens_in.astype(jnp.float32), attn_gain).astype(jnp.bfloat16)
    output_plane = doubled(o_proj.T.astype(jnp.bfloat16)[None], "tp", 1)
    output_plane, unused = barrier((output_plane, payload))
    output_plane = doubled(doubled(output_plane, "tp", 2), "tp", 4)
    output_plane = output_plane.transpose(1, 0, 2).reshape(48, model_width)
    output_plane, normalized = barrier((output_plane, normalized))
    output_plane = doubled(doubled(output_plane, "ep", 1), "ep", 16)
    along_z = lax.all_to_all(payload, "ep", 0, 0, axis_index_groups=Z_GROUPS, tiled=True)
    output_plane, along_z = barrier((output_plane, along_z))
    output_weight = lax.all_gather(output_plane, "ep", axis_index_groups=Z_GROUPS)
    payload, by_expert = relay(along_z)
    across = lax.all_to_all(payload, "ep", 0, 0, axis_index_groups=CHIP_PAIR_GROUPS, tiled=True)
    table = rotary_table(seq_len, 32 * 32)
    by_expert, across = barrier((by_expert, across))
    hosted = lax.all_to_all(by_expert, "tp", 0, 0, tiled=True)
    attended = attention(lengths, normalized, across, table)
    attended, hosted = barrier((attended, hosted))
    attn_parts = lax.all_to_all(attended, "tp", 0, 0, tiled=True)
    planes = lax.all_gather(hosted, "ep", axis_index_groups=Z_GROUPS)
    own_rows = lax.dynamic_slice_in_dim(tokens_in, tp_index * row_count, row_count, 0)
    router_hosted = router.T.reshape(2, 8, 2, model_width).transpose(0, 2, 1, 3)
    hidden, send_rows, rank_gates = project_and_dispatch(
        attn_parts,
        output_weight,
        own_rows,
        moe_gain,
        router_hosted.reshape(EXPERTS, model_width),
        expert_ids.T,
    )
    gate_up_full = (
        planes[:, :, :192].reshape(8, 8, 8, 24, 128).transpose(1, 0, 3, 2, 4).reshape(model_width, 2 * FF)
    )
    down_full = (
        planes[:, :, 192:].reshape(8, 8, 12, 8, 128).transpose(1, 0, 3, 2, 4).reshape(FF, model_width)
    )
    received = in_plane(send_rows.reshape(EXPERTS, CAPACITY, model_width))
    both = weighing(rank_gates)
    expert_out = experts(received.reshape(-1, model_width), gate_up_full, down_full)
    returned = in_plane(expert_out.reshape(EXPERTS, CAPACITY, model_width))
    live = lengths - tp_index * row_count
    return combine(live, both, returned.reshape(-1, model_width), hidden)


def solution(mesh):
    in_specs = (
        P("ep", None),
        P("ep"),
        P(),
        P("ep", "tp"),
        P("ep", "tp"),
        P("ep", "tp"),
        P("tp", "ep"),
        P("ep", None, "tp"),
        P(None, "ep", None),
        P(),
        P(),
        P(("ep", "tp"), None),
        P("ep", "tp", None),
        P("ep", "tp", None),
    )
    out_specs = P(("ep", "tp"), None)
    return jax.shard_map(
        on_device, mesh=mesh, in_specs=in_specs, out_specs=out_specs, check_vma=False
    )
```

```python
import math

import jax
import jax.numpy as jnp
from jax import lax
from jax.experimental import pallas as pl
from jax.experimental.pallas import tpu as pltpu
from jax.sharding import PartitionSpec as P

HEAD_WIDTH = 64
FF = 512
CAPACITY = 48
EXPERTS = 32


epsilon = 1e-05

Z_GROUPS = [[y * 16 + z * 2 + c for z in range(8)] for y in range(2) for c in range(2)]
CHIP_PAIR_GROUPS = [[y * 16 + z * 2 + c for y in range(2) for c in range(2)] for z in range(8)]
PLANE_GROUPS = [
    [(y * 16 + z * 2 + c) * 8 + t for y in range(2) for c in range(2) for t in range(8)]
    for z in range(8)
]


def rms_scale(values, norm_gain):
    mean_square = jnp.mean(values * values, axis=-1, keepdims=True)
    return values * lax.rsqrt(mean_square + epsilon) * norm_gain


def rotary_table(positions, first_position):
    lane = jnp.arange(2 * HEAD_WIDTH)
    frequency = jnp.exp(
        (lane % (HEAD_WIDTH // 2)).astype(jnp.float32) * (-2.0 * math.log(10000.0) / HEAD_WIDTH)
    )
    angles = (first_position + jnp.arange(positions)).astype(jnp.float32)[:, None] * frequency
    sign = jnp.where(lane % HEAD_WIDTH < HEAD_WIDTH // 2, -1.0, 1.0)
    return jnp.where(lane < HEAD_WIDTH, jnp.cos(angles), jnp.sin(angles) * sign)


def attention_body(
    length_ref, normalized_ref, across_ref, table_ref,
    out_ref, queries, keys, values, weight,
):
    seq_len = normalized_ref.shape[0]
    heads = queries.shape[0]
    prefix = keys.shape[1] - seq_len
    chunk = 256
    lane = lax.broadcasted_iota(jnp.int32, (chunk, 256), 1)
    ones = jnp.ones((chunk, HEAD_WIDTH), jnp.bfloat16)
    for e in range(32):
        pair, z = (e // 16) * 2 + e % 2, (e // 2) % 8
        for j in range(3):
            weight[e * 48 : (e + 1) * 48, j * 128 : (j + 1) * 128] = across_ref[
                pair, z, j * 48 : (j + 1) * 48, :
            ]
    for c in range(0, prefix, chunk):
        rows = jnp.concatenate(
            [
                across_ref[(e // 16) * 2 + e % 2, (e // 2) % 8, 144:176, :]
                for e in range(c // 32, (c + chunk) // 32)
            ],
            axis=0,
        )
        keys[:, c : c + chunk] = rows.astype(jnp.float32).T[:HEAD_WIDTH].astype(jnp.bfloat16)
        values[c : c + chunk, :] = jnp.concatenate([rows[:, HEAD_WIDTH:], ones], axis=1)
    for c in range(0, seq_len, chunk):
        projected = jnp.dot(
            normalized_ref[c : c + chunk, :], weight[...], preferred_element_type=jnp.float32
        )
        plain = projected[:, :256]
        partner = jnp.where(
            lane % HEAD_WIDTH < HEAD_WIDTH // 2,
            pltpu.roll(plain, 256 - HEAD_WIDTH // 2, 1),
            pltpu.roll(plain, HEAD_WIDTH // 2, 1),
        )
        cosine = table_ref[c : c + chunk, :HEAD_WIDTH]
        sine = table_ref[c : c + chunk, HEAD_WIDTH:]
        rotated = plain * jnp.concatenate([cosine] * 4, axis=1) + partner * jnp.concatenate(
            [sine] * 4, axis=1
        )
        rounded = rotated.astype(jnp.bfloat16)
        for h in range(heads):
            queries[h, c : c + chunk, :] = (
                rounded[:, h * HEAD_WIDTH : (h + 1) * HEAD_WIDTH] * HEAD_WIDTH ** (-0.5)
            ).astype(jnp.bfloat16)
        keys[:, prefix + c : prefix + c + chunk] = (
            rotated.T[heads * HEAD_WIDTH :].astype(jnp.bfloat16)
        )
        values[prefix + c : prefix + c + chunk, :] = jnp.concatenate(
            [projected[:, 256 : 256 + HEAD_WIDTH].astype(jnp.bfloat16), ones], axis=1
        )
    length = length_ref[0]
    for start in range(0, seq_len, chunk):
        seen = start + chunk
        column = lax.broadcasted_iota(jnp.int32, (chunk, seen), 1)
        row = lax.broadcasted_iota(jnp.int32, (chunk, seen), 0)
        allowed = (column <= row + start) & (column < length)
        outs = []
        for h in range(heads):
            query = queries[h, start:seen, :]
            cached = jnp.dot(query, keys[:, :prefix], preferred_element_type=jnp.float32)
            own = jnp.dot(query, keys[:, prefix : prefix + seen], preferred_element_type=jnp.float32)
            own = jnp.where(allowed, own, -1e30)
            top = jnp.maximum(
                jnp.max(cached, axis=1, keepdims=True), jnp.max(own, axis=1, keepdims=True)
            )
            total = jnp.dot(
                jnp.exp(cached - top).astype(jnp.bfloat16),
                values[:prefix, :],
                preferred_element_type=jnp.float32,
            ) + jnp.dot(
                jnp.exp(own - top).astype(jnp.bfloat16),
                values[prefix : prefix + seen, :],
                preferred_element_type=jnp.float32,
            )
            outs.append(total[:, :HEAD_WIDTH] / total[:, HEAD_WIDTH : HEAD_WIDTH + 1])
        for t in range(0, chunk, 128):
            block = (start + t) // 128
            low, high = outs[2][t : t + 64], outs[2][t + 64 : t + 128]
            out_ref[block, :128, :] = jnp.concatenate(
                [outs[0][t : t + 128], outs[1][t : t + 128]], axis=1
            ).astype(jnp.bfloat16)
            out_ref[block, 128:, :] = jnp.concatenate([low, high], axis=1).astype(jnp.bfloat16)


def attention(lengths, normalized, across, table):
    seq_len, model_width = normalized.shape
    heads = 3
    total = 2 * seq_len
    vmem = pl.BlockSpec(memory_space=pltpu.VMEM)
    return pl.pallas_call(
        attention_body,
        out_shape=pltpu.HBM((seq_len // 128, 192, 128), jnp.bfloat16),
        in_specs=[pl.BlockSpec(memory_space=pltpu.SMEM)] + [vmem] * 3,
        out_specs=vmem,
        scratch_shapes=[
            pltpu.VMEM((heads, seq_len, HEAD_WIDTH), jnp.bfloat16),
            pltpu.VMEM((HEAD_WIDTH, total), jnp.bfloat16),
            pltpu.VMEM((total, 2 * HEAD_WIDTH), jnp.bfloat16),
            pltpu.VMEM((model_width, 384), jnp.bfloat16),
        ],
        compiler_params=pltpu.CompilerParams(vmem_limit_bytes=48 << 20),
        cost_estimate=pl.CostEstimate(
            flops=12_000_000_000, bytes_accessed=8 << 20, transcendentals=heads * seq_len * total
        ),
        name="attention",
    )(lengths, normalized, across, table)


def prepare_body(
    table_ref, query_ref, key_ref, value_ref, gate_up_ref, down_ref, pages_ref, payload_ref, held, sem
):
    weight = jnp.concatenate(
        [query_ref[...], key_ref[...], value_ref[...], jnp.zeros(key_ref.shape, jnp.float32)], axis=1
    ).astype(jnp.bfloat16)
    copies = []
    for z in range(8):
        for j in range(3):
            held[z, j * 48 : (j + 1) * 48, :] = weight[:, j * 128 : (j + 1) * 128]
        for d in range(4):
            prompt = (d // 2) * 16 + z * 2 + d % 2
            for s in range(2):
                at = 144 + 32 * d + 16 * s
                held[z, at : at + 16, :] = pages_ref[table_ref[prompt * 2 + s]]
        for b in range(8):
            held[z, 272 + 24 * b : 296 + 24 * b, :] = gate_up_ref[
                z * 24 : (z + 1) * 24, b * 128 : (b + 1) * 128
            ].astype(jnp.bfloat16)
        for b in range(12):
            held[z, 464 + 8 * b : 472 + 8 * b, :] = down_ref[
                z * 8 : (z + 1) * 8, b * 128 : (b + 1) * 128
            ].astype(jnp.bfloat16)
        copy = pltpu.make_async_copy(held.at[z], payload_ref.at[z], sem.at[z])
        copy.start()
        copies.append(copy)
    for copy in copies:
        copy.wait()


def prepare(page_table, q_proj, k_proj, value_projection, gate_up, down, pages):
    vmem = pl.BlockSpec(memory_space=pltpu.VMEM)
    shape = (8, 560, 128)
    return pl.pallas_call(
        prepare_body,
        out_shape=pltpu.HBM(shape, jnp.bfloat16),
        in_specs=[pl.BlockSpec(memory_space=pltpu.SMEM)] + [vmem] * 6,
        out_specs=pl.BlockSpec(memory_space=pltpu.HBM),
        scratch_shapes=[pltpu.VMEM(shape, jnp.bfloat16), pltpu.SemaphoreType.DMA((8,))],
        cost_estimate=pl.CostEstimate(flops=0, bytes_accessed=3 << 20, transcendentals=0),
        name="prepare",
    )(page_table, q_proj, k_proj, value_projection, gate_up, down, pages)


def relay_body(along_ref, payload_ref, expert_ref, held, sem):
    loads = [pltpu.make_async_copy(along_ref.at[z], held.at[z], sem.at[z]) for z in range(8)]
    for load in loads:
        load.start()
    for load in loads:
        load.wait()
    copies = []
    for d in range(4):
        copies.append(
            pltpu.make_async_copy(
                held.at[:, pl.ds(0, 144)], payload_ref.at[d, :, pl.ds(0, 144)], sem.at[2 * d]
            )
        )
        copies.append(
            pltpu.make_async_copy(
                held.at[:, pl.ds(144 + 32 * d, 32)],
                payload_ref.at[d, :, pl.ds(144, 32)],
                sem.at[2 * d + 1],
            )
        )
    copies.append(pltpu.make_async_copy(held.at[:, pl.ds(272, 288)], expert_ref, sem.at[8]))
    for copy in copies:
        copy.start()
    for copy in copies:
        copy.wait()


def relay(along_z):
    hbm = pl.BlockSpec(memory_space=pltpu.HBM)
    return pl.pallas_call(
        relay_body,
        out_shape=(
            pltpu.HBM((4, 8, 176, 128), jnp.bfloat16),
            pltpu.HBM((8, 288, 128), jnp.bfloat16),
        ),
        in_specs=[hbm],
        out_specs=(hbm, hbm),
        scratch_shapes=[pltpu.VMEM(along_z.shape, jnp.bfloat16), pltpu.SemaphoreType.DMA((9,))],
        cost_estimate=pl.CostEstimate(flops=0, bytes_accessed=4 << 20, transcendentals=0),
        name="relay",
    )(pltpu.with_memory_space_constraint(along_z, pltpu.HBM))


def project_body(
    parts_ref, weight_hbm, rows_ref, gain_ref, router_ref, ids_ref,
    hidden_out, send_ref, rank_gates_out,
    weight, attended, place, staged, hidden_ref, rank_gates, sem, out_sem,
):
    copies = []
    for y in range(2):
        for z in range(8):
            copy = pltpu.make_async_copy(
                weight_hbm.at[z, y], weight.at[pl.ds((y * 8 + z) * 96, 96)], sem.at[y * 8 + z]
            )
            copy.start()
            copies.append(copy)
    for t in range(8):
        at = t * 192
        attended[:, at : at + 128] = parts_ref[t, :128, :]
        attended[:64, at + 128 : at + 192] = parts_ref[t, 128:, :64]
        attended[64:, at + 128 : at + 192] = parts_ref[t, 128:, 64:]
    tokens = rows_ref.shape[0]
    host = lax.broadcasted_iota(jnp.int32, (EXPERTS, tokens), 0)
    expert_at = (host // 16) * 16 + (host % 8) * 2 + (host // 8) % 2
    chosen = jnp.zeros((EXPERTS, tokens), jnp.float32)
    for k in range(ids_ref.shape[0]):
        chosen = jnp.where(ids_ref[k : k + 1, :] == expert_at, 1.0, chosen)
    earlier = lax.broadcasted_iota(jnp.int32, (tokens, tokens), 0) < lax.broadcasted_iota(
        jnp.int32, (tokens, tokens), 1
    )
    rank = jnp.dot(
        chosen.astype(jnp.bfloat16),
        jnp.where(earlier, 1.0, 0.0).astype(jnp.bfloat16),
        preferred_element_type=jnp.float32,
    )
    rank = jnp.where(chosen > 0.0, rank, -1.0)
    rank_gates[:EXPERTS, :] = rank
    slot = lax.broadcasted_iota(jnp.int32, (CAPACITY, tokens), 0).astype(jnp.float32)
    for g in range(EXPERTS):
        place[g * CAPACITY : (g + 1) * CAPACITY, :] = jnp.where(
            rank[g : g + 1, :] == slot, 1.0, 0.0
        ).astype(jnp.bfloat16)
    for c in range(0, 1536, 256):
        while copies and len(copies) > 16 - (c + 256 + 95) // 96:
            copies.pop(0).wait()
        hidden_ref[:, c : c + 256] = rows_ref[:, c : c + 256].astype(jnp.float32) + lax.dot_general(
            attended[...],
            weight[c : c + 256, :],
            (((1,), (1,)), ((), ())),
            preferred_element_type=jnp.float32,
        )
    keep = pltpu.make_async_copy(hidden_ref, hidden_out, out_sem.at[6])
    keep.start()
    hidden = hidden_ref[...]
    moe_in = rms_scale(hidden, gain_ref[...]).astype(jnp.bfloat16)
    for c in range(0, EXPERTS * CAPACITY, 256):
        staged[c : c + 256, :] = jnp.dot(
            place[c : c + 256, :], moe_in, preferred_element_type=jnp.float32
        ).astype(jnp.bfloat16)
        pltpu.make_async_copy(
            staged.at[pl.ds(c, 256)], send_ref.at[pl.ds(c, 256)], out_sem.at[c // 256]
        ).start()
    logits = lax.dot_general(
        router_ref[...], moe_in, (((1,), (1,)), ((), ())), preferred_element_type=jnp.float32
    )
    top_logit = jnp.max(jnp.where(chosen > 0.0, logits, -3e38), axis=0, keepdims=True)
    raised = jnp.where(chosen > 0.0, jnp.exp(jnp.minimum(logits - top_logit, 0.0)), 0.0)
    rank_gates[EXPERTS:, :] = raised / jnp.sum(raised, axis=0, keepdims=True)
    last = pltpu.make_async_copy(rank_gates, rank_gates_out, out_sem.at[7])
    last.start()
    for c in range(0, EXPERTS * CAPACITY, 256):
        pltpu.make_async_copy(
            staged.at[pl.ds(c, 256)], send_ref.at[pl.ds(c, 256)], out_sem.at[c // 256]
        ).wait()
    keep.wait()
    last.wait()


def project_and_dispatch(parts, output_weight, own_rows, moe_gain, router_hosted, ids_by_choice):
    row_count, model_width = own_rows.shape
    slots = EXPERTS * CAPACITY
    vmem = pl.BlockSpec(memory_space=pltpu.VMEM)
    return pl.pallas_call(
        project_body,
        out_shape=(
            pltpu.HBM((row_count, model_width), jnp.float32),
            pltpu.HBM((slots, model_width), jnp.bfloat16),
            pltpu.HBM((2 * EXPERTS, row_count), jnp.float32),
        ),
        in_specs=[vmem, pl.BlockSpec(memory_space=pltpu.HBM), vmem, vmem, vmem, vmem],
        out_specs=(pl.BlockSpec(memory_space=pltpu.HBM),) * 3,
        scratch_shapes=[
            pltpu.VMEM((model_width, model_width), jnp.bfloat16),
            pltpu.VMEM((row_count, model_width), jnp.bfloat16),
            pltpu.VMEM((slots, row_count), jnp.bfloat16),
            pltpu.VMEM((slots, model_width), jnp.bfloat16),
            pltpu.VMEM((row_count, model_width), jnp.float32),
            pltpu.VMEM((2 * EXPERTS, row_count), jnp.float32),
            pltpu.SemaphoreType.DMA((16,)),
            pltpu.SemaphoreType.DMA((8,)),
        ],
        compiler_params=pltpu.CompilerParams(vmem_limit_bytes=40 << 20),
        cost_estimate=pl.CostEstimate(
            flops=4 * row_count * model_width * model_width,
            bytes_accessed=4 * model_width * model_width,
            transcendentals=0,
        ),
        name="project_and_dispatch",
    )(
        parts,
        pltpu.with_memory_space_constraint(output_weight.reshape(8, 2, 96, model_width), pltpu.HBM),
        own_rows,
        moe_gain.reshape(1, model_width),
        router_hosted,
        ids_by_choice,
    )


def weigh_body(rank_gates_ref, both_ref, weigh):
    tokens = rank_gates_ref.shape[1]
    slot = lax.broadcasted_iota(jnp.int32, (CAPACITY, tokens), 0).astype(jnp.float32)
    for g in range(EXPERTS):
        weigh[g * CAPACITY : (g + 1) * CAPACITY, :] = jnp.where(
            rank_gates_ref[g : g + 1, :] == slot,
            rank_gates_ref[EXPERTS + g : EXPERTS + g + 1, :],
            0.0,
        )
    for c in range(0, EXPERTS * CAPACITY, 128):
        by_token = weigh[c : c + 128, :].T
        high = by_token.astype(jnp.bfloat16)
        both_ref[:tokens, c : c + 128] = high
        both_ref[tokens:, c : c + 128] = (by_token - high.astype(jnp.float32)).astype(jnp.bfloat16)


def weighing(rank_gates):
    row_count = rank_gates.shape[1]
    slots = EXPERTS * CAPACITY
    vmem = pl.BlockSpec(memory_space=pltpu.VMEM)
    return pl.pallas_call(
        weigh_body,
        out_shape=jax.ShapeDtypeStruct((2 * row_count, slots), jnp.bfloat16),
        in_specs=[vmem],
        out_specs=vmem,
        scratch_shapes=[pltpu.VMEM((slots, row_count), jnp.float32)],
        cost_estimate=pl.CostEstimate(flops=1 << 20, bytes_accessed=1 << 20, transcendentals=0),
        name="weighing",
    )(rank_gates)


def expert_body(rows_ref, gate_up_ref, down_ref, out_ref):
    gate_up = jnp.dot(rows_ref[...], gate_up_ref[...], preferred_element_type=jnp.float32)
    activated = (jax.nn.silu(gate_up[:, :FF]) * gate_up[:, FF:]).astype(jnp.bfloat16)
    out_ref[...] = jnp.dot(activated, down_ref[...], preferred_element_type=jnp.float32).astype(
        jnp.bfloat16
    )


def experts(rows, gate_up, down):
    count, model_width = rows.shape
    tile = 512
    return pl.pallas_call(
        expert_body,
        out_shape=pltpu.HBM((count, model_width), jnp.bfloat16),
        grid=(count // tile,),
        in_specs=[
            pl.BlockSpec((tile, model_width), lambda i: (i, 0)),
            pl.BlockSpec(gate_up.shape, lambda i: (0, 0)),
            pl.BlockSpec(down.shape, lambda i: (0, 0)),
        ],
        out_specs=pl.BlockSpec((tile, model_width), lambda i: (i, 0)),
        compiler_params=pltpu.CompilerParams(vmem_limit_bytes=40 << 20),
        cost_estimate=pl.CostEstimate(
            flops=2 * count * model_width * 3 * FF,
            bytes_accessed=4 * count * model_width + 6 * model_width * FF,
            transcendentals=count * FF,
        ),
        name="experts",
    )(rows, gate_up, pltpu.with_memory_space_constraint(down, pltpu.HBM))


def combine_body(live_ref, both_ref, returned_ref, hidden_ref, out_ref):
    tokens = hidden_ref.shape[0]
    mixed = jnp.dot(both_ref[...], returned_ref[...], preferred_element_type=jnp.float32)
    total = hidden_ref[...] + (mixed[:tokens] + mixed[tokens:])
    row = lax.broadcasted_iota(jnp.int32, total.shape, 0)
    out_ref[...] = jnp.where(row < live_ref[0], total, 0.0).astype(jnp.bfloat16)


def combine(live, both, returned, hidden):
    row_count, model_width = hidden.shape
    slots = returned.shape[0]
    tile = model_width // 2
    column = pl.BlockSpec((row_count, tile), lambda i: (0, i))
    return pl.pallas_call(
        combine_body,
        out_shape=jax.ShapeDtypeStruct((row_count, model_width), jnp.bfloat16),
        grid=(model_width // tile,),
        in_specs=[
            pl.BlockSpec(memory_space=pltpu.SMEM),
            pl.BlockSpec(both.shape, lambda i: (0, 0)),
            pl.BlockSpec((slots, tile), lambda i: (0, i)),
            column,
        ],
        out_specs=column,
        compiler_params=pltpu.CompilerParams(vmem_limit_bytes=24 << 20),
        cost_estimate=pl.CostEstimate(
            flops=4 * row_count * slots * model_width,
            bytes_accessed=2 * slots * model_width + 6 * row_count * model_width,
            transcendentals=0,
        ),
        name="combine",
    )(
        live,
        pltpu.with_memory_space_constraint(both, pltpu.HBM),
        returned,
        pltpu.with_memory_space_constraint(hidden, pltpu.HBM),
    )


def on_device(
    tokens_in,
    lengths,
    attn_gain,
    q_proj,
    k_proj,
    value_projection,
    o_proj,
    key_value_pages,
    page_table,
    moe_gain,
    router,
    expert_ids,
    gate_up_proj,
    down_proj,
):
    seq_len, model_width = tokens_in.shape
    barrier = lax.optimization_barrier
    tp_index = lax.axis_index("tp")
    row_count = seq_len // 8

    def in_plane(rows):
        return lax.all_to_all(
            rows, ("ep", "tp"), 0, 0, axis_index_groups=PLANE_GROUPS, tiled=True
        )

    def doubled(block, axis, bit):
        size = lax.axis_size(axis)
        other = lax.ppermute(block, axis, [(i, i ^ bit) for i in range(size)])
        first = (lax.axis_index(axis) & bit) == 0
        return jnp.concatenate(
            [jnp.where(first, block, other), jnp.where(first, other, block)], axis=0
        )

    payload = prepare(
        page_table.reshape(-1), q_proj, k_proj, value_projection, gate_up_proj[0], down_proj[0], key_value_pages
    )
    normalized = rms_scale(tokens_in.astype(jnp.float32), attn_gain).astype(jnp.bfloat16)
    output_plane = doubled(o_proj.T.astype(jnp.bfloat16)[None], "tp", 1)
    output_plane, unused = barrier((output_plane, payload))
    output_plane = doubled(doubled(output_plane, "tp", 2), "tp", 4)
    output_plane = output_plane.transpose(1, 0, 2).reshape(48, model_width)
    output_plane, normalized = barrier((output_plane, normalized))
    output_plane = doubled(doubled(output_plane, "ep", 1), "ep", 16)
    along_z = lax.all_to_all(payload, "ep", 0, 0, axis_index_groups=Z_GROUPS, tiled=True)
    output_plane, along_z = barrier((output_plane, along_z))
    output_weight = lax.all_gather(output_plane, "ep", axis_index_groups=Z_GROUPS)
    payload, by_expert = relay(along_z)
    across = lax.all_to_all(payload, "ep", 0, 0, axis_index_groups=CHIP_PAIR_GROUPS, tiled=True)
    table = rotary_table(seq_len, 32 * 32)
    by_expert, across = barrier((by_expert, across))
    hosted = lax.all_to_all(by_expert, "tp", 0, 0, tiled=True)
    attended = attention(lengths, normalized, across, table)
    attended, hosted = barrier((attended, hosted))
    attn_parts = lax.all_to_all(attended, "tp", 0, 0, tiled=True)
    planes = lax.all_gather(hosted, "ep", axis_index_groups=Z_GROUPS)
    own_rows = lax.dynamic_slice_in_dim(tokens_in, tp_index * row_count, row_count, 0)
    router_hosted = router.T.reshape(2, 8, 2, model_width).transpose(0, 2, 1, 3)
    hidden, send_rows, rank_gates = project_and_dispatch(
        attn_parts,
        output_weight,
        own_rows,
        moe_gain,
        router_hosted.reshape(EXPERTS, model_width),
        expert_ids.T,
    )
    gate_up_full = (
        planes[:, :, :192].reshape(8, 8, 8, 24, 128).transpose(1, 0, 3, 2, 4).reshape(model_width, 2 * FF)
    )
    down_full = (
        planes[:, :, 192:].reshape(8, 8, 12, 8, 128).transpose(1, 0, 3, 2, 4).reshape(FF, model_width)
    )
    received = in_plane(send_rows.reshape(EXPERTS, CAPACITY, model_width))
    both = weighing(rank_gates)
    expert_out = experts(received.reshape(-1, model_width), gate_up_full, down_full)
    returned = in_plane(expert_out.reshape(EXPERTS, CAPACITY, model_width))
    live = lengths - tp_index * row_count
    return combine(live, both, returned.reshape(-1, model_width), hidden)


def solution(mesh):
    in_specs = (
        P("ep", None),
        P("ep"),
        P(),
        P("ep", "tp"),
        P("ep", "tp"),
        P("ep", "tp"),
        P("tp", "ep"),
        P("ep", None, "tp"),
        P(None, "ep", None),
        P(),
        P(),
        P(("ep", "tp"), None),
        P("ep", "tp", None),
        P("ep", "tp", None),
    )
    out_specs = P(("ep", "tp"), None)
    return jax.shard_map(
        on_device, mesh=mesh, in_specs=in_specs, out_specs=out_specs, check_vma=False
    )
```
